256 devices in a mesh: sy: 16 (over x, y_hi, core), sx: 16 (over y_lo, z).
Axes of the slice: x: 4, y: 4 (y_hi: 2, y_lo: 2; y = y_hi * 2 + y_lo), z: 8, core: 2. Of those that a mesh axis runs over, the one named last changes fastest.
Arguments:
- object_tile: float32 [2, 2048, 2048], P(None, 'sy', 'sx'), may hold values from -5 to 5
- probe_modes: float32 [2, 2, 128, 128], replicated, may hold values from -4 to 4
- scan_offsets: int32 [16, 16, 4, 2], P('sy', 'sx'), may hold values from 0 to 128
- intensities: float32 [16, 16, 4, 128, 128], P('sy', 'sx'), may hold values from 0 to 2
Outputs:
- object_out: float32 [2, 2048, 2048], P(None, 'sy', 'sx')
- probe_out: float32 [2, 2, 128, 128], replicated
The draws below stay inside these ranges and needn't reach their ends.
Inputs may be any that keep to these rules, and one draw needn't show every extreme that they name: `scan_offsets`: offsets are counted from 64 pixels above and to the left of the device's tile, so a patch stays within 64 pixels of its tile.
All inputs are finite; a program needn't handle non-finite values.
Results may differ from the reference program's by a relative error of at most 0.0003.
Values sent between devices are 32-bit elements; how exact they have to be, the bound alone decides.
A program may use at most 64 MiB of HBM per device.

```python
import jax
import jax.numpy as jnp
from jax import lax

PATCH = 128
MODES = 2
TILE = 128
NPOS = 4
ITERS = 2
HALF = 64
OBJ_Y = 2048
OBJ_X = 2048
N_SY = 16
N_SX = 16


def set_ends(drawn, stream_key, smallest, top_value):
    index_at = [jax.random.randint(jax.random.fold_in(stream_key, axis), (), 0, length) for axis, length in enumerate(drawn.shape)]
    longest = drawn.shape.index(max(drawn.shape))
    next_to = index_at[:longest] + [(index_at[longest] + 1) % drawn.shape[longest]] + index_at[longest + 1:]
    return drawn.at[tuple(index_at)].set(smallest).at[tuple(next_to)].set(top_value)


def level_of(key, dims, cuts, least, top_value):
    def one(axis_at, parts):
        steps = jax.random.uniform(jax.random.fold_in(jax.random.fold_in(key, 6), axis_at), (parts,), jnp.float32, least / len(cuts), top_value / len(cuts))
        return jnp.repeat(jnp.exp(steps), dims[axis_at] // parts).reshape((-1,) + (1,) * (len(dims) - axis_at - 1))

    level = one(*cuts[0])
    for cut in cuts[1:]:
        level = level * one(*cut)
    return level


def centred(own_key, shape, width, most, shards=(), held_as=jnp.bfloat16):
    factor_of = level_of(own_key, shape, shards, -0.22, 0.18) if shards else 1.0
    entries = jax.random.normal(own_key, shape, jnp.float32) * width * factor_of
    return jnp.minimum(jnp.maximum(entries, -most), most).astype(held_as)


def setup_inputs(seed: int = 0) -> dict:
    keys = jax.random.split(jax.random.key(seed), 5)
    object_tile = centred(keys[0], (2, OBJ_Y, OBJ_X), 0.7, 5.0, ((1, 16), (2, 16)), jnp.float32)
    probe_modes = centred(keys[1], (MODES, 2, PATCH, PATCH), 0.5, 4.0, (), jnp.float32)
    scan_offsets = set_ends(jax.random.randint(keys[2], (N_SY, N_SX, NPOS, 2), 0, TILE + 1), jax.random.fold_in(keys[2], 1), 0, TILE).astype(jnp.int32)
    intensities = jnp.clip(2.0 * jax.random.uniform(keys[3], (N_SY, N_SX, NPOS, PATCH, PATCH), jnp.float32) ** level_of(keys[3], (N_SY, N_SX, NPOS, PATCH, PATCH), ((0, 16), (1, 16)), -0.2, 0.2), 0.0, 2.0)
    return dict(object_tile=object_tile, probe_modes=probe_modes, scan_offsets=scan_offsets, intensities=intensities)


OBJECT_STEP = 0.5
PROBE_STEP = 2.0
REGULAR = 1.0


def back_waves(object_real, object_imag, probe_modes, measured):
    probe_cplx = probe_modes[:, 0] + 1j * probe_modes[:, 1]
    patch_cplx = object_real + 1j * object_imag
    exit_wave = probe_cplx[None] * patch_cplx[:, None]
    spectrum = jnp.fft.fft2(exit_wave, norm="ortho")
    power = jnp.real(spectrum) * jnp.real(spectrum) + jnp.imag(spectrum) * jnp.imag(spectrum)
    misfit = jnp.sum(power, axis=1) - measured
    returned = jnp.fft.ifft2(misfit[:, None] * spectrum, norm="ortho")
    return jnp.real(returned), jnp.imag(returned)


def one_pass(canvas, probe_modes, scan_offsets, intensities):
    probe_real = probe_modes[:, 0][None]
    probe_imag = probe_modes[:, 1][None]

    def row_block(carry, inputs):
        gradients, numerator, denominator = carry
        row_number, offsets, measured = inputs
        column_base = (jnp.arange(N_SX, dtype=jnp.int32) * TILE)[:, None]
        corner_rows = (row_number * TILE + offsets[:, :, 0]).reshape(-1).astype(jnp.int32)
        corner_cols = (column_base + offsets[:, :, 1]).reshape(-1).astype(jnp.int32)
        corners = jnp.stack([corner_rows, corner_cols], axis=1)
        patches = jax.vmap(lambda corner: lax.dynamic_slice(canvas, (jnp.int32(0), corner[0], corner[1]), (2, PATCH, PATCH)))(corners)
        object_real = patches[:, 0]
        object_imag = patches[:, 1]
        back_real, back_imag = back_waves(object_real, object_imag, probe_modes, measured.reshape(-1, PATCH, PATCH))
        grad_real = jnp.sum(probe_real * back_real + probe_imag * back_imag, axis=1)
        grad_imag = jnp.sum(probe_real * back_imag - probe_imag * back_real, axis=1)
        lighting = jnp.broadcast_to(jnp.sum(probe_real * probe_real + probe_imag * probe_imag, axis=1), grad_real.shape)
        terms = jnp.stack([grad_real, grad_imag, lighting], axis=1)
        numer_real = jnp.sum(object_real[:, None] * back_real + object_imag[:, None] * back_imag, axis=0)
        numer_imag = jnp.sum(object_real[:, None] * back_imag - object_imag[:, None] * back_real, axis=0)
        numerator = numerator + jnp.stack([numer_real, numer_imag], axis=1)
        denominator = denominator + jnp.sum(object_real * object_real + object_imag * object_imag, axis=0)

        def place_patch(number, running):
            corner = corners[number]
            existing = lax.dynamic_slice(running, (jnp.int32(0), corner[0], corner[1]), (3, PATCH, PATCH))
            return lax.dynamic_update_slice(running, existing + terms[number], (jnp.int32(0), corner[0], corner[1]))

        gradients = lax.fori_loop(0, corners.shape[0], place_patch, gradients)
        return (gradients, numerator, denominator), None

    start = (jnp.zeros((3,) + canvas.shape[1:], canvas.dtype), jnp.zeros(probe_modes.shape, canvas.dtype), jnp.zeros((PATCH, PATCH), canvas.dtype))
    rows_in = jnp.arange(N_SY, dtype=jnp.int32)
    (gradients, numerator, denominator), unused = lax.scan(row_block, start, (rows_in, scan_offsets, intensities))
    inner = gradients[:, HALF:HALF + OBJ_Y, HALF:HALF + OBJ_X]
    fresh = canvas[:, HALF:HALF + OBJ_Y, HALF:HALF + OBJ_X] - OBJECT_STEP * inner[:2] / (inner[2:3] + REGULAR)
    canvas = canvas.at[:, HALF:HALF + OBJ_Y, HALF:HALF + OBJ_X].set(fresh)
    probe_modes = probe_modes - PROBE_STEP * numerator / (denominator + REGULAR)
    return canvas, probe_modes


def reference(object_tile, probe_modes, scan_offsets, intensities):
    canvas = jnp.pad(object_tile, ((0, 0), (HALF, HALF), (HALF, HALF)))
    for iteration in range(ITERS):
        canvas, probe_modes = one_pass(canvas, probe_modes, scan_offsets, intensities)
    return canvas[:, HALF:HALF + OBJ_Y, HALF:HALF + OBJ_X], probe_modes
```

```python
import functools

import numpy as np
import jax
import jax.numpy as jnp
from jax import lax
from jax.experimental import pallas as pl
from jax.experimental.pallas import tpu as pltpu
from jax.sharding import PartitionSpec as P

ITERS = 2
OBJECT_STEP = 0.5
PROBE_STEP = 2.0
REGULAR = 1.0
N = 128
HALF = 64
Y_LO = 2
MESH = pl.DeviceIdType.MESH
F32 = jnp.float32
BF16 = jnp.bfloat16

SIDES = [(-1, 0), (1, 0), (0, -1), (0, 1), (-1, -1), (1, -1), (-1, 1), (1, 1)]


def dft_tables():
    index = np.arange(N)
    angle = (index[:, None] * index[None, :] % N) * (2.0 * np.pi / N)
    scale = 1.0 / np.sqrt(float(N))
    cosine, sine = np.cos(angle) * scale, np.sin(angle) * scale
    forward = np.block([[cosine, -sine], [sine, cosine]])
    parts = []
    for matrix in (forward, forward.T):
        high = matrix.astype(np.float32).astype(BF16)
        low = (matrix - high.astype(np.float64)).astype(np.float32).astype(BF16)
        parts += [high, low]
    return np.stack(parts)


def split(value):
    high = value.astype(BF16)
    low = (value - high.astype(F32)).astype(BF16)
    return high, low


def dot(left, right):
    return jnp.dot(left, right, preferred_element_type=F32)


def swap_blocks(value):
    top = jnp.concatenate([value[:N, :N], value[N:, :N]], axis=1)
    bottom = jnp.concatenate([value[:N, N:], value[N:, N:]], axis=1)
    return jnp.concatenate([top, bottom], axis=0)


def kernel(n_sy, n_sx, positions, modes, offs, tile_in, probe_in, inten, tables,
           obj_out, prb_out,
           tile1, can_t, can_h, pack_l, pack_r, strip_l, strip_r,
           obj, back_g, nacc, pads, g_t, g_h, gp_l, gp_r, g_up, g_dn, f_l, f_r,
           l_t, l_h, l_up, l_dn, lf_l, lf_r, l_sum,
           n_buf, n_rcv, n_part, nz_rcv, m_buf, m_rcv, m_part, mz_rcv, p_buf,
           side_send, side_recv, all_send, all_recv):
    sy = lax.axis_index("sy")
    sx = lax.axis_index("sx")
    depth = n_sx // Y_LO
    group = n_sy * Y_LO
    blocks = group // modes
    rows = N // blocks
    y_lo = lax.div(sx, depth)
    z = lax.rem(sx, depth)
    me = sy * Y_LO + y_lo
    my_mode = lax.div(me, blocks)
    my_block = lax.rem(me, blocks)

    def side_dev(step):
        dy, dx = step
        return (lax.rem(sy + (n_sy + dy), n_sy), lax.rem(sx + (n_sx + dx), n_sx))

    def group_dev(other):
        return (lax.div(other, Y_LO), lax.rem(other, Y_LO) * depth + z)

    def z_dev(other):
        return (sy, y_lo * depth + other)

    lane = lax.broadcasted_iota(jnp.int32, (HALF, N), 1)
    lane_n = lax.broadcasted_iota(jnp.int32, (N, N), 1)
    has_u = jnp.where(sy > 0, 1, 0)
    has_d = jnp.where(sy < n_sy - 1, 1, 0)
    has_l = jnp.where(sx > 0, 1, 0)
    has_r = jnp.where(sx < n_sx - 1, 1, 0)

    def remote(src, dst, send, recv, dev):
        return pltpu.make_async_remote_copy(
            src_ref=src, dst_ref=dst, send_sem=send, recv_sem=recv,
            device_id=dev, device_id_type=MESH)

    def await_bytes(ref, sem):
        pltpu.make_async_copy(ref, ref, sem).wait()

    def fetch_copies(it, tile):
        top, bottom, both = pl.ds(0, HALF), pl.ds(HALF, HALF), pl.ds(0, N)
        c_top, c_mid, c_low = pl.ds(0, HALF), pl.ds(HALF, N), pl.ds(N + HALF, HALF)
        plan = [
            (tile.at[:, top, :], can_t.at[it, :, c_low, :]),
            (tile.at[:, bottom, :], can_t.at[it, :, c_top, :]),
            (pack_l.at[it, both], strip_r.at[it, c_mid]),
            (pack_r.at[it, both], strip_l.at[it, c_mid]),
            (pack_l.at[it, top], strip_r.at[it, c_low]),
            (pack_l.at[it, bottom], strip_r.at[it, c_top]),
            (pack_r.at[it, top], strip_l.at[it, c_low]),
            (pack_r.at[it, bottom], strip_l.at[it, c_top]),
        ]
        return [remote(src, dst, side_send.at[0, it, i], side_recv.at[0, it, i], side_dev(SIDES[i]))
                for i, (src, dst) in enumerate(plan)]

    def strip_copies(kind, it, src_t, src_l, src_r, up, down, left, right):
        top, mid, low = pl.ds(0, HALF), pl.ds(HALF, N), pl.ds(N + HALF, HALF)
        if kind == 1:
            vertical = [(src_t.at[:, top, :], up), (src_t.at[:, low, :], down)]
        else:
            vertical = [(src_t.at[top], up), (src_t.at[low], down)]
        plan = vertical + [
            (src_l.at[mid], right.at[mid]),
            (src_r.at[mid], left.at[mid]),
            (src_l.at[top], right.at[top]),
            (src_l.at[low], right.at[low]),
            (src_r.at[top], left.at[top]),
            (src_r.at[low], left.at[low]),
        ]
        return [remote(src, dst, side_send.at[kind, it, i], side_recv.at[kind, it, i],
                       side_dev(SIDES[i])) for i, (src, dst) in enumerate(plan)]

    def grad_copies(it):
        return strip_copies(1, it, g_t.at[it], gp_l.at[it], gp_r.at[it],
                            g_up.at[it], g_dn.at[it], f_l.at[it], f_r.at[it])

    def light_copies(it):
        return strip_copies(2, it, l_t.at[it], l_h.at[it], l_h.at[it],
                            l_up.at[it], l_dn.at[it], lf_l.at[it], lf_r.at[it])

    def pack(it, tile):
        real, rolled = tile[0], pltpu.roll(tile[1], HALF, 1)
        pack_l[it] = jnp.where(lane_n < HALF, real, rolled)
        pack_r[it] = jnp.where(lane_n >= HALF, real, rolled)

    def column_mask(column):
        return (lane_n >= column - HALF) & (lane_n < column + HALF)

    def assemble(it, tile):
        keep_re = (lane >= HALF * (1 - has_r)) & (lane < HALF + HALF * has_l)
        keep_im = (lane >= HALF * (1 - has_l)) & (lane < HALF + HALF * has_r)
        keep_u = lane < N * has_u
        keep_d = lane < N * has_d
        for c in range(2):
            can_t[it, c, pl.ds(HALF, N), :] = tile[c]
            top = can_t[it, c, pl.ds(0, HALF), :]
            can_t[it, c, pl.ds(0, HALF), :] = jnp.where(keep_u, top, 0.0)
            low = can_t[it, c, pl.ds(N + HALF, HALF), :]
            can_t[it, c, pl.ds(N + HALF, HALF), :] = jnp.where(keep_d, low, 0.0)
        for part in range(4):
            at = pl.ds(part * HALF, HALF)
            left, right = strip_l[it, at], strip_r[it, at]
            real = jnp.where(keep_re, jnp.where(lane < HALF, right, left), 0.0)
            imag = jnp.where(keep_im, jnp.where(lane < HALF, left, right), 0.0)
            if part == 0:
                real, imag = jnp.where(keep_u, real, 0.0), jnp.where(keep_u, imag, 0.0)
            if part == 3:
                real, imag = jnp.where(keep_d, real, 0.0), jnp.where(keep_d, imag, 0.0)
            can_h[it, 0, at, :] = real
            can_h[it, 1, at, :] = pltpu.roll(imag, HALF, 1)

    def extract(it):
        total = None
        for j in range(positions):
            row, column = offs[2 * j], offs[2 * j + 1]
            mask = column_mask(column)
            shift = lax.rem(HALF + N - column, N)
            for c in range(2):
                inner = can_t[it, c, pl.ds(row, N), :]
                outer = can_h[it, c, pl.ds(row, N), :]
                patch = pltpu.roll(jnp.where(mask, inner, outer), shift, 1)
                obj[j, c] = patch
                total = patch * patch if total is None else total + patch * patch
        m_buf[it] = total.reshape(blocks, rows, N)

    def place(channel, term):
        for j in range(positions):
            column = offs[2 * j + 1]
            mask = column_mask(column)
            turned = pltpu.roll(term(j), lax.rem(column + HALF, N), 1)
            pads[channel, 0, j, pl.ds(N, N), :] = jnp.where(mask, turned, 0.0)
            pads[channel, 1, j, pl.ds(N, N), :] = jnp.where(mask, 0.0, turned)

    def placed(channel, half):
        total = None
        for j in range(positions):
            window = pads[channel, half, j, pl.ds(N - offs[2 * j], 2 * N), :]
            total = window if total is None else total + window
        return total

    def probe_part(it, k, c):
        if it == 0:
            return probe_in[k, c]
        return p_buf[it - 1, k * blocks:(k + 1) * blocks, c].reshape(N, N)

    def light(it):
        bright = None
        for k in range(modes):
            for c in range(2):
                part = probe_part(it, k, c)
                bright = part * part if bright is None else bright + part * part
        place(2, lambda j: bright)
        l_t[it] = placed(2, 0)
        l_h[it] = placed(2, 1)

    def spread(what, it, source, target):
        def step(offset, carry):
            other = lax.rem(me + offset, group)
            remote(source(other), target(offset - 1), all_send.at[what, it], all_recv.at[what, it],
                   group_dev(other)).start()
            return carry
        lax.fori_loop(1, group, step, 0)

    def spread_z(what, it, source, target):
        def step(offset, carry):
            remote(source, target(offset - 1), all_send.at[what, it], all_recv.at[what, it],
                   z_dev(lax.rem(z + offset, depth))).start()
            return carry
        lax.fori_loop(1, depth, step, 0)

    def send_m(it):
        spread(0, it, lambda other: m_buf.at[it, lax.rem(other, blocks)], lambda s: m_rcv.at[it, s])

    def send_mz(it):
        await_bytes(m_rcv.at[it], all_recv.at[0, it])
        m_part[it] = m_buf[it, my_block] + jnp.sum(m_rcv[it], axis=0)
        spread_z(1, it, m_part.at[it], lambda s: mz_rcv.at[it, s])

    def send_n(it):
        spread(2, it, lambda other: n_buf.at[it, other], lambda s: n_rcv.at[it, s])

    def send_nz(it):
        await_bytes(n_rcv.at[it], all_recv.at[2, it])
        n_part[it] = n_buf[it, me] + jnp.sum(n_rcv[it], axis=0)
        spread_z(3, it, n_part.at[it], lambda s: nz_rcv.at[it, s])

    def send_p(it):
        await_bytes(mz_rcv.at[it], all_recv.at[1, it])
        denominator = m_part[it] + jnp.sum(mz_rcv[it], axis=0)
        await_bytes(nz_rcv.at[it], all_recv.at[3, it])
        numerator = n_part[it] + jnp.sum(nz_rcv[it], axis=0)
        for c in range(2):
            if it == 0:
                old = probe_in[my_mode, c, pl.ds(pl.multiple_of(my_block * rows, rows), rows), :]
            else:
                old = p_buf[it - 1, me, c]
            p_buf[it, me, c] = old - PROBE_STEP * numerator[c] / (denominator + REGULAR)
        spread(4, it, lambda other: p_buf.at[it, me], lambda s: p_buf.at[it, me])

    def wait_p(it):
        await_bytes(p_buf.at[it, pl.ds(0, group - 1)], all_recv.at[4, it])

    def waves(it):
        nacc[...] = jnp.zeros_like(nacc)

        def position(j, carry):
            o_re, o_im = obj[j, 0], obj[j, 1]
            wave = []
            for k in range(modes):
                p_re, p_im = probe_part(it, k, 0), probe_part(it, k, 1)
                wave.append(jnp.concatenate(
                    [p_re * o_re - p_im * o_im, p_re * o_im + p_im * o_re], axis=1))
            x_h, x_l = split(jnp.concatenate(wave, axis=0))
            half = dot(x_h, tables[0]) + dot(x_l, tables[0]) + dot(x_h, tables[1])
            b_h, b_l = split(swap_blocks(half))
            spec = dot(tables[2], b_h) + dot(tables[2], b_l) + dot(tables[3], b_h)
            power = spec[:N] * spec[:N] + spec[N:] * spec[N:]
            misfit = power[:, :N] + power[:, N:] - inten[j]
            wide = jnp.concatenate([misfit, misfit], axis=1)
            d_h, d_l = split(jnp.concatenate([spec[:N] * wide, spec[N:] * wide], axis=0))
            half = dot(tables[0], d_h) + dot(tables[0], d_l) + dot(tables[1], d_h)
            e_h, e_l = split(swap_blocks(half))
            chi = dot(e_h, tables[2]) + dot(e_l, tables[2]) + dot(e_h, tables[3])
            g_re, g_im = None, None
            for k in range(modes):
                c_re, c_im = chi[k * N:(k + 1) * N, :N], chi[k * N:(k + 1) * N, N:]
                nacc[k, 0] += o_re * c_re + o_im * c_im
                nacc[k, 1] += o_re * c_im - o_im * c_re
                p_re, p_im = probe_part(it, k, 0), probe_part(it, k, 1)
                a_re = p_re * c_re + p_im * c_im
                a_im = p_re * c_im - p_im * c_re
                g_re = a_re if g_re is None else g_re + a_re
                g_im = a_im if g_im is None else g_im + a_im
            back_g[j, 0] = g_re
            back_g[j, 1] = g_im
            return carry

        lax.fori_loop(0, positions, position, 0)
        for k in range(modes):
            for c in range(2):
                n_buf[it, k * blocks:(k + 1) * blocks, c] = nacc[k, c].reshape(blocks, rows, N)

    def gradient(it):
        for c in range(2):
            place(c, lambda j: back_g[j, c])
            g_t[it, c] = placed(c, 0)
            g_h[c] = placed(c, 1)
        wide = lax.broadcasted_iota(jnp.int32, (2 * N, N), 1)
        real, rolled = g_h[0], pltpu.roll(g_h[1], HALF, 1)
        gp_l[it] = jnp.where(wide >= HALF, real, rolled)
        gp_r[it] = jnp.where(wide < HALF, real, rolled)

    def strip_sum(strip):
        top, low = strip[pl.ds(0, HALF)], strip[pl.ds(N + HALF, HALF)]
        upper = strip[pl.ds(HALF, HALF)] + jnp.where(lane < N * has_u, low, 0.0)
        lower = strip[pl.ds(N, HALF)] + jnp.where(lane < N * has_d, top, 0.0)
        return jnp.concatenate([upper, lower], axis=0)

    def own_light(it):
        from_l, from_r = strip_sum(lf_l.at[it]), strip_sum(lf_r.at[it])
        from_up = jnp.where(lane < N * has_u, l_dn[it], 0.0)
        from_down = jnp.where(lane < N * has_d, l_up[it], 0.0)
        total = l_t[it, pl.ds(HALF, N), :] + jnp.concatenate([from_up, from_down], axis=0)
        total += jnp.where(lane_n < HALF * has_l, from_l, 0.0)
        total += jnp.where(lane_n >= N - HALF * has_r, from_r, 0.0)
        l_sum[it] = total

    def update(it, old, new):
        from_l, from_r = strip_sum(f_l.at[it]), strip_sum(f_r.at[it])
        weight = l_sum[it] + REGULAR
        for c in range(2):
            from_up = jnp.where(lane < N * has_u, g_dn[it, c], 0.0)
            from_down = jnp.where(lane < N * has_d, g_up[it, c], 0.0)
            total = g_t[it, c, pl.ds(HALF, N), :] + jnp.concatenate([from_up, from_down], axis=0)
            left = from_l if c == 0 else pltpu.roll(from_l, HALF, 1)
            right = from_r if c == 0 else pltpu.roll(from_r, HALF, 1)
            total += jnp.where(lane_n < HALF * has_l, left, 0.0)
            total += jnp.where(lane_n >= N - HALF * has_r, right, 0.0)
            new[c] = old[c] - OBJECT_STEP * total / weight

    barrier = pltpu.get_barrier_semaphore()
    for step in SIDES:
        pl.semaphore_signal(barrier, inc=1, device_id=side_dev(step), device_id_type=MESH)

    def greet(offset, carry):
        pl.semaphore_signal(barrier, inc=1, device_id=group_dev(lax.rem(me + offset, group)),
                            device_id_type=MESH)
        return carry

    def greet_z(offset, carry):
        pl.semaphore_signal(barrier, inc=1, device_id=z_dev(lax.rem(z + offset, depth)),
                            device_id_type=MESH)
        return carry

    lax.fori_loop(1, group, greet, 0)
    lax.fori_loop(1, depth, greet_z, 0)
    pack(0, tile_in)
    pl.semaphore_wait(barrier, len(SIDES) + group - 1 + depth - 1)

    for copy in fetch_copies(0, tile_in):
        copy.start()
    for channel in range(3):
        for half in range(2):
            for j in range(positions):
                pads[channel, half, j, pl.ds(0, N), :] = jnp.zeros((N, N), F32)
                pads[channel, half, j, pl.ds(2 * N, N), :] = jnp.zeros((N, N), F32)
    light(0)
    for copy in light_copies(0):
        copy.start()

    tiles = [tile_in, tile1, obj_out]
    for it in range(ITERS):
        for copy in fetch_copies(it, tiles[it]):
            copy.wait_recv()
        assemble(it, tiles[it])
        extract(it)
        send_m(it)
        if it > 0:
            wait_p(it - 1)
            light(it)
            for copy in light_copies(it):
                copy.start()
        waves(it)
        send_n(it)
        send_mz(it)
        gradient(it)
        for copy in grad_copies(it):
            copy.start()
        for copy in light_copies(it):
            copy.wait_recv()
        own_light(it)
        send_nz(it)
        for copy in grad_copies(it):
            copy.wait_recv()
        update(it, tiles[it], tiles[it + 1])
        if it + 1 < ITERS:
            pack(it + 1, tiles[it + 1])
            for copy in fetch_copies(it + 1, tiles[it + 1]):
                copy.start()
        send_p(it)
    wait_p(ITERS - 1)
    for k in range(modes):
        for c in range(2):
            prb_out[k, c] = probe_part(ITERS, k, c)

    for it in range(ITERS):
        for copies in (fetch_copies(it, tiles[it]), grad_copies(it), light_copies(it)):
            for copy in copies:
                copy.wait_send()
        await_bytes(m_rcv.at[it], all_send.at[0, it])
        await_bytes(mz_rcv.at[it], all_send.at[1, it])
        await_bytes(n_rcv.at[it], all_send.at[2, it])
        await_bytes(nz_rcv.at[it], all_send.at[3, it])
        await_bytes(p_buf.at[it, pl.ds(0, group - 1)], all_send.at[4, it])


def per_device(n_sy, n_sx, object_tile, probe_modes, scan_offsets, intensities):
    positions = scan_offsets.shape[2]
    modes = probe_modes.shape[0]
    depth = n_sx // Y_LO
    group = n_sy * Y_LO
    blocks = group // modes
    rows = N // blocks
    offsets = scan_offsets.reshape(positions * 2)
    measured = intensities[0, 0]
    tables = jnp.asarray(dft_tables())
    vmem = functools.partial(pltpu.VMEM, dtype=F32)
    it = ITERS
    scratch = [
        vmem((2, N, N)), vmem((it, 2, 2 * N, N)), vmem((it, 2, 2 * N, N)),
        vmem((it, N, N)), vmem((it, N, N)), vmem((it, 2 * N, N)), vmem((it, 2 * N, N)),
        vmem((positions, 2, N, N)), vmem((positions, 2, N, N)), vmem((modes, 2, N, N)),
        vmem((3, 2, positions, 3 * N, N)), vmem((it, 2, 2 * N, N)), vmem((2, 2 * N, N)),
        vmem((it, 2 * N, N)), vmem((it, 2 * N, N)), vmem((it, 2, HALF, N)), vmem((it, 2, HALF, N)),
        vmem((it, 2 * N, N)), vmem((it, 2 * N, N)),
        vmem((it, 2 * N, N)), vmem((it, 2 * N, N)), vmem((it, HALF, N)), vmem((it, HALF, N)),
        vmem((it, 2 * N, N)), vmem((it, 2 * N, N)), vmem((it, N, N)),
        vmem((it, group, 2, rows, N)), vmem((it, group - 1, 2, rows, N)), vmem((it, 2, rows, N)),
        vmem((it, depth - 1, 2, rows, N)),
        vmem((it, blocks, rows, N)), vmem((it, group - 1, rows, N)), vmem((it, rows, N)),
        vmem((it, depth - 1, rows, N)), vmem((it, group, 2, rows, N)),
        pltpu.SemaphoreType.DMA((3, it, len(SIDES))), pltpu.SemaphoreType.DMA((3, it, len(SIDES))),
        pltpu.SemaphoreType.DMA((5, it)), pltpu.SemaphoreType.DMA((5, it)),
    ]
    in_vmem = pl.BlockSpec(memory_space=pltpu.VMEM)
    return pl.pallas_call(
        functools.partial(kernel, n_sy, n_sx, positions, modes),
        out_shape=(jax.ShapeDtypeStruct(object_tile.shape, F32),
                   jax.ShapeDtypeStruct(probe_modes.shape, F32)),
        in_specs=[pl.BlockSpec(memory_space=pltpu.SMEM)] + [in_vmem] * 4,
        out_specs=(in_vmem, in_vmem),
        scratch_shapes=scratch,
        compiler_params=pltpu.CompilerParams(collective_id=0, has_side_effects=True),
    )(offsets, object_tile, probe_modes, measured, tables)


def solution(mesh):
    placed = (P(None, "sy", "sx"), P(), P("sy", "sx", None, None), P("sy", "sx", None, None, None))
    return jax.shard_map(
        functools.partial(per_device, mesh.shape["sy"], mesh.shape["sx"]),
        mesh=mesh,
        in_specs=placed,
        out_specs=(P(None, "sy", "sx"), P()),
        check_vma=False,
    )
```

```python
import functools

import numpy as np
import jax
import jax.numpy as jnp
from jax import lax
from jax.experimental import pallas as pl
from jax.experimental.pallas import tpu as pltpu
from jax.sharding import PartitionSpec as P

ITERS = 2
OBJECT_STEP = 0.5
PROBE_STEP = 2.0
REGULAR = 1.0
N = 128
HALF = 64
Y_LO = 2
MESH = pl.DeviceIdType.MESH
F32 = jnp.float32
BF16 = jnp.bfloat16

SIDES = [(-1, -1), (1, -1), (-1, 1), (1, 1), (-1, 0), (1, 0), (0, -1), (0, 1)]


def dft_tables():
    index = np.arange(N)
    angle = (index[:, None] * index[None, :] % N) * (2.0 * np.pi / N)
    scale = 1.0 / np.sqrt(float(N))
    cosine, sine = np.cos(angle) * scale, np.sin(angle) * scale
    forward = np.block([[cosine, -sine], [sine, cosine]])
    parts = []
    for matrix in (forward, forward.T):
        high = matrix.astype(np.float32).astype(BF16)
        low = (matrix - high.astype(np.float64)).astype(np.float32).astype(BF16)
        parts += [high, low]
    return np.stack(parts)


def split(value):
    high = value.astype(BF16)
    low = (value - high.astype(F32)).astype(BF16)
    return high, low


def dot(left, right):
    return jnp.dot(left, right, preferred_element_type=F32)


def swap_blocks(value):
    top = jnp.concatenate([value[:N, :N], value[N:, :N]], axis=1)
    bottom = jnp.concatenate([value[:N, N:], value[N:, N:]], axis=1)
    return jnp.concatenate([top, bottom], axis=0)


def far_first(count):
    return sorted(range(count), key=lambda d: -min(d, count - d))


def kernel(n_sy, n_sx, positions, modes, offs, tile_hbm, probe_hbm, inten_hbm, tables_hbm,
           obj_out, prb_out,
           tile_in, probe_in, inten, tables, tile1, can_t, can_h, pack_l, pack_r, strip_l, strip_r,
           obj, back_g, nacc, pads, g_t, g_h, gp_l, gp_r, g_up, g_dn, f_l, f_r,
           l_t, l_h, lp_l, lp_r, l_up, l_dn, lf_l, lf_r, l_sum,
           n_buf, n_rcv, n_part, nz_rcv, m_buf, m_rcv, m_part, mz_rcv, p_buf,
           side_send, side_recv, all_send, all_recv, load_sem):
    sy = lax.axis_index("sy")
    sx = lax.axis_index("sx")
    depth = n_sx // Y_LO
    group = n_sy * Y_LO
    blocks = group // modes
    rows = N // blocks
    cores = 2
    n_yh = min(2, n_sy // cores)
    n_x, n_y = n_sy // (cores * n_yh), n_yh * Y_LO
    core = lax.rem(sy, cores)
    x = lax.div(sy, cores * n_yh)
    y_lo = lax.div(sx, depth)
    y = lax.rem(lax.div(sy, cores), n_yh) * Y_LO + y_lo
    z = lax.rem(sx, depth)
    me = sy * Y_LO + y_lo
    my_mode = lax.div(me, blocks)
    my_block = lax.rem(me, blocks)
    x_part = [lax.rem(x + d, n_x) * (cores * n_yh * Y_LO) for d in range(n_x)]
    y_at = [lax.rem(y + d, n_y) for d in range(n_y)]
    y_part = [lax.div(v, Y_LO) * (cores * Y_LO) + lax.rem(v, Y_LO) for v in y_at]
    c_part = [lax.rem(core + d, cores) * Y_LO for d in range(cores)]
    y_col = [lax.rem(v, Y_LO) * depth + z for v in y_at]
    peers = [(dx, dy, dc) for dx in far_first(n_x) for dy in far_first(n_y) for dc in range(cores)
             if dx or dy or dc]
    peers.sort(key=lambda p: -(min(p[0], n_x - p[0]) + min(p[1], n_y - p[1])))
    peer_index = [x_part[dx] + y_part[dy] + c_part[dc] for dx, dy, dc in peers]
    peer_dev = [(lax.div(at, Y_LO), y_col[p[1]]) for at, p in zip(peer_index, peers)]
    z_devs = [(sy, y_lo * depth + lax.rem(z + d, depth)) for d in far_first(depth) if d]

    def side_dev(step):
        dy, dx = step
        return (lax.rem(sy + (n_sy + dy), n_sy), lax.rem(sx + (n_sx + dx), n_sx))

    lane = lax.broadcasted_iota(jnp.int32, (HALF, N), 1)
    lane_n = lax.broadcasted_iota(jnp.int32, (N, N), 1)
    has_u = jnp.where(sy > 0, 1, 0)
    has_d = jnp.where(sy < n_sy - 1, 1, 0)
    has_l = jnp.where(sx > 0, 1, 0)
    has_r = jnp.where(sx < n_sx - 1, 1, 0)

    def remote(src, dst, send, recv, dev):
        return pltpu.make_async_remote_copy(
            src_ref=src, dst_ref=dst, send_sem=send, recv_sem=recv,
            device_id=dev, device_id_type=MESH)

    def await_bytes(ref, sem):
        pltpu.make_async_copy(ref, ref, sem).wait()

    def fetch_copies(it, tile):
        top, bottom, both = pl.ds(0, HALF), pl.ds(HALF, HALF), pl.ds(0, N)
        c_top, c_mid, c_low = pl.ds(0, HALF), pl.ds(HALF, N), pl.ds(N + HALF, HALF)
        plan = [
            (pack_l.at[it, top], strip_r.at[it, c_low]),
            (pack_l.at[it, bottom], strip_r.at[it, c_top]),
            (pack_r.at[it, top], strip_l.at[it, c_low]),
            (pack_r.at[it, bottom], strip_l.at[it, c_top]),
            (tile.at[:, top, :], can_t.at[it, :, c_low, :]),
            (tile.at[:, bottom, :], can_t.at[it, :, c_top, :]),
            (pack_l.at[it, both], strip_r.at[it, c_mid]),
            (pack_r.at[it, both], strip_l.at[it, c_mid]),
        ]
        return [remote(src, dst, side_send.at[0, it, i], side_recv.at[0, it, i], side_dev(SIDES[i]))
                for i, (src, dst) in enumerate(plan)]

    def strip_copies(kind, it, unit, vertical, src_l, src_r, left, right):
        top, mid, low = pl.ds(0, unit), pl.ds(unit, 2 * unit), pl.ds(3 * unit, unit)
        plan = [
            (src_l.at[top], right.at[top]),
            (src_l.at[low], right.at[low]),
            (src_r.at[top], left.at[top]),
            (src_r.at[low], left.at[low]),
        ] + vertical + [
            (src_l.at[mid], right.at[mid]),
            (src_r.at[mid], left.at[mid]),
        ]
        return [remote(src, dst, side_send.at[kind, it, i], side_recv.at[kind, it, i],
                       side_dev(SIDES[i])) for i, (src, dst) in enumerate(plan)]

    def grad_copies(it):
        vertical = [(g_t.at[it, :, pl.ds(0, HALF), :], g_up.at[it]),
                    (g_t.at[it, :, pl.ds(N + HALF, HALF), :], g_dn.at[it])]
        return strip_copies(1, it, HALF, vertical, gp_l.at[it], gp_r.at[it], f_l.at[it], f_r.at[it])

    def light_copies(it):
        vertical = [(l_t.at[it, pl.ds(0, HALF)], l_up.at[it]),
                    (l_t.at[it, pl.ds(N + HALF, HALF)], l_dn.at[it])]
        return strip_copies(2, it, HALF // 2, vertical, lp_l.at[it], lp_r.at[it],
                            lf_l.at[it], lf_r.at[it])

    def pack(it, tile):
        real, rolled = tile[0], pltpu.roll(tile[1], HALF, 1)
        pack_l[it] = jnp.where(lane_n < HALF, real, rolled)
        pack_r[it] = jnp.where(lane_n >= HALF, real, rolled)

    def column_mask(column):
        return (lane_n >= column - HALF) & (lane_n < column + HALF)

    def assemble(it, tile):
        keep_re = (lane >= HALF * (1 - has_r)) & (lane < HALF + HALF * has_l)
        keep_im = (lane >= HALF * (1 - has_l)) & (lane < HALF + HALF * has_r)
        keep_u = lane < N * has_u
        keep_d = lane < N * has_d
        for c in range(2):
            can_t[it, c, pl.ds(HALF, N), :] = tile[c]
            top = can_t[it, c, pl.ds(0, HALF), :]
            can_t[it, c, pl.ds(0, HALF), :] = jnp.where(keep_u, top, 0.0)
            low = can_t[it, c, pl.ds(N + HALF, HALF), :]
            can_t[it, c, pl.ds(N + HALF, HALF), :] = jnp.where(keep_d, low, 0.0)
        for part in range(4):
            at = pl.ds(part * HALF, HALF)
            left, right = strip_l[it, at], strip_r[it, at]
            real = jnp.where(keep_re, jnp.where(lane < HALF, right, left), 0.0)
            imag = jnp.where(keep_im, jnp.where(lane < HALF, left, right), 0.0)
            if part == 0:
                real, imag = jnp.where(keep_u, real, 0.0), jnp.where(keep_u, imag, 0.0)
            if part == 3:
                real, imag = jnp.where(keep_d, real, 0.0), jnp.where(keep_d, imag, 0.0)
            can_h[it, 0, at, :] = real
            can_h[it, 1, at, :] = pltpu.roll(imag, HALF, 1)

    def extract(it):
        total = None
        for j in range(positions):
            row, column = offs[0, 0, 0, j], offs[0, 0, 1, j]
            mask = column_mask(column)
            shift = lax.rem(HALF + N - column, N)
            for c in range(2):
                inner = can_t[it, c, pl.ds(row, N), :]
                outer = can_h[it, c, pl.ds(row, N), :]
                patch = pltpu.roll(jnp.where(mask, inner, outer), shift, 1)
                obj[j, c] = patch
                total = patch * patch if total is None else total + patch * patch
        m_buf[it] = total.reshape(blocks, rows, N)

    def place(channel, term):
        for j in range(positions):
            column = offs[0, 0, 1, j]
            mask = column_mask(column)
            turned = pltpu.roll(term(j), lax.rem(column + HALF, N), 1)
            pads[channel, 0, j, pl.ds(N, N), :] = jnp.where(mask, turned, 0.0)
            pads[channel, 1, j, pl.ds(N, N), :] = jnp.where(mask, 0.0, turned)

    def placed(channel, half):
        total = None
        for j in range(positions):
            window = pads[channel, half, j, pl.ds(N - offs[0, 0, 0, j], 2 * N), :]
            total = window if total is None else total + window
        return total

    def probe_part(it, k, c):
        if it == 0:
            return probe_in[k, c]
        return p_buf[it - 1, k * blocks:(k + 1) * blocks, c].reshape(N, N)

    def light(it):
        bright = None
        for k in range(modes):
            for c in range(2):
                part = probe_part(it, k, c)
                bright = part * part if bright is None else bright + part * part
        place(2, lambda j: bright)
        l_t[it] = placed(2, 0)
        l_h[...] = placed(2, 1)
        half = HALF // 2
        low_lanes = lax.broadcasted_iota(jnp.int32, (half, N), 1) < HALF
        for part in range(4):
            first = l_h[pl.ds(part * HALF, half), :]
            second = l_h[pl.ds(part * HALF + half, half), :]
            at = pl.ds(part * half, half)
            lp_l[it, at, :] = jnp.where(low_lanes, pltpu.roll(first, HALF, 1), second)
            lp_r[it, at, :] = jnp.where(low_lanes, first, pltpu.roll(second, HALF, 1))

    def spread(what, it, source, target):
        for slot, (other, dev) in enumerate(zip(peer_index, peer_dev)):
            remote(source(other), target(slot), all_send.at[what, it], all_recv.at[what, it],
                   dev).start()

    def spread_z(what, it, source, target):
        for slot, dev in enumerate(z_devs):
            remote(source, target(slot), all_send.at[what, it], all_recv.at[what, it], dev).start()

    def send_m(it):
        spread(0, it, lambda other: m_buf.at[it, lax.rem(other, blocks)], lambda s: m_rcv.at[it, s])

    def send_mz(it):
        await_bytes(m_rcv.at[it], all_recv.at[0, it])
        m_part[it] = m_buf[it, my_block] + jnp.sum(m_rcv[it], axis=0)
        spread_z(1, it, m_part.at[it], lambda s: mz_rcv.at[it, s])

    def send_n(it):
        spread(2, it, lambda other: n_buf.at[it, other], lambda s: n_rcv.at[it, s])

    def send_nz(it):
        await_bytes(n_rcv.at[it], all_recv.at[2, it])
        n_part[it] = n_buf[it, me] + jnp.sum(n_rcv[it], axis=0)
        spread_z(3, it, n_part.at[it], lambda s: nz_rcv.at[it, s])

    def send_p(it):
        await_bytes(mz_rcv.at[it], all_recv.at[1, it])
        denominator = m_part[it] + jnp.sum(mz_rcv[it], axis=0)
        await_bytes(nz_rcv.at[it], all_recv.at[3, it])
        numerator = n_part[it] + jnp.sum(nz_rcv[it], axis=0)
        for c in range(2):
            if it == 0:
                old = probe_in[my_mode, c, pl.ds(pl.multiple_of(my_block * rows, rows), rows), :]
            else:
                old = p_buf[it - 1, me, c]
            p_buf[it, me, c] = old - PROBE_STEP * numerator[c] / (denominator + REGULAR)
        spread(4, it, lambda other: p_buf.at[it, me], lambda s: p_buf.at[it, me])

    def wait_p(it):
        await_bytes(p_buf.at[it, pl.ds(0, group - 1)], all_recv.at[4, it])

    def waves(it):
        nacc[...] = jnp.zeros_like(nacc)

        def position(j, carry):
            o_re, o_im = obj[j, 0], obj[j, 1]
            wave = []
            for k in range(modes):
                p_re, p_im = probe_part(it, k, 0), probe_part(it, k, 1)
                wave.append(jnp.concatenate(
                    [p_re * o_re - p_im * o_im, p_re * o_im + p_im * o_re], axis=1))
            x_h, x_l = split(jnp.concatenate(wave, axis=0))
            half = dot(x_h, tables[0]) + dot(x_l, tables[0]) + dot(x_h, tables[1])
            b_h, b_l = split(swap_blocks(half))
            spec = dot(tables[2], b_h) + dot(tables[2], b_l) + dot(tables[3], b_h)
            power = spec[:N] * spec[:N] + spec[N:] * spec[N:]
            misfit = power[:, :N] + power[:, N:] - inten[j]
            wide = jnp.concatenate([misfit, misfit], axis=1)
            d_h, d_l = split(jnp.concatenate([spec[:N] * wide, spec[N:] * wide], axis=0))
            half = dot(tables[0], d_h) + dot(tables[0], d_l) + dot(tables[1], d_h)
            e_h, e_l = split(swap_blocks(half))
            chi = dot(e_h, tables[2]) + dot(e_l, tables[2]) + dot(e_h, tables[3])
            g_re, g_im = None, None
            for k in range(modes):
                c_re, c_im = chi[k * N:(k + 1) * N, :N], chi[k * N:(k + 1) * N, N:]
                nacc[k, 0] += o_re * c_re + o_im * c_im
                nacc[k, 1] += o_re * c_im - o_im * c_re
                p_re, p_im = probe_part(it, k, 0), probe_part(it, k, 1)
                a_re = p_re * c_re + p_im * c_im
                a_im = p_re * c_im - p_im * c_re
                g_re = a_re if g_re is None else g_re + a_re
                g_im = a_im if g_im is None else g_im + a_im
            back_g[j, 0] = g_re
            back_g[j, 1] = g_im
            return carry

        lax.fori_loop(0, positions, position, 0)
        for k in range(modes):
            for c in range(2):
                n_buf[it, k * blocks:(k + 1) * blocks, c] = nacc[k, c].reshape(blocks, rows, N)

    def gradient(it):
        for c in range(2):
            place(c, lambda j: back_g[j, c])
            g_t[it, c] = placed(c, 0)
            g_h[c] = placed(c, 1)
        wide = lax.broadcasted_iota(jnp.int32, (2 * N, N), 1)
        real, rolled = g_h[0], pltpu.roll(g_h[1], HALF, 1)
        gp_l[it] = jnp.where(wide >= HALF, real, rolled)
        gp_r[it] = jnp.where(wide < HALF, real, rolled)

    def strip_sum(strip):
        top, low = strip[pl.ds(0, HALF)], strip[pl.ds(N + HALF, HALF)]
        upper = strip[pl.ds(HALF, HALF)] + jnp.where(lane < N * has_u, low, 0.0)
        lower = strip[pl.ds(N, HALF)] + jnp.where(lane < N * has_d, top, 0.0)
        return jnp.concatenate([upper, lower], axis=0)

    def own_light(it):
        half = HALF // 2

        def unpacked(strip, here):
            parts = []
            for part in range(4):
                block = strip[pl.ds(part * half, half), :]
                turned = pltpu.roll(block, HALF, 1)
                parts += [turned, block] if here else [block, turned]
            low = jnp.where(lane < N * has_u, jnp.concatenate(parts[6:], axis=0), 0.0)
            top = jnp.where(lane < N * has_d, jnp.concatenate(parts[:2], axis=0), 0.0)
            upper = jnp.concatenate(parts[2:4], axis=0) + low
            lower = jnp.concatenate(parts[4:6], axis=0) + top
            return jnp.concatenate([upper, lower], axis=0)

        from_r, from_l = unpacked(lf_r.at[it], True), unpacked(lf_l.at[it], False)
        from_up = jnp.where(lane < N * has_u, l_dn[it], 0.0)
        from_down = jnp.where(lane < N * has_d, l_up[it], 0.0)
        total = l_t[it, pl.ds(HALF, N), :] + jnp.concatenate([from_up, from_down], axis=0)
        total += jnp.where(lane_n < HALF * has_l, from_l, 0.0)
        total += jnp.where(lane_n >= N - HALF * has_r, from_r, 0.0)
        l_sum[it] = total

    def update(it, old, new):
        from_l, from_r = strip_sum(f_l.at[it]), strip_sum(f_r.at[it])
        weight = l_sum[it] + REGULAR
        for c in range(2):
            from_up = jnp.where(lane < N * has_u, g_dn[it, c], 0.0)
            from_down = jnp.where(lane < N * has_d, g_up[it, c], 0.0)
            total = g_t[it, c, pl.ds(HALF, N), :] + jnp.concatenate([from_up, from_down], axis=0)
            left = from_l if c == 0 else pltpu.roll(from_l, HALF, 1)
            right = from_r if c == 0 else pltpu.roll(from_r, HALF, 1)
            total += jnp.where(lane_n < HALF * has_l, left, 0.0)
            total += jnp.where(lane_n >= N - HALF * has_r, right, 0.0)
            new[c] = old[c] - OBJECT_STEP * total / weight

    barrier = pltpu.get_barrier_semaphore()
    greeted = [side_dev(step) for step in SIDES] + peer_dev + z_devs
    for dev in greeted:
        pl.semaphore_signal(barrier, inc=1, device_id=dev, device_id_type=MESH)
    loads = [pltpu.make_async_copy(src, dst, load_sem.at[i]) for i, (src, dst) in enumerate(
        [(tile_hbm, tile_in), (probe_hbm, probe_in), (tables_hbm, tables), (inten_hbm, inten)])]
    for load in loads:
        load.start()
    loads[0].wait()
    pack(0, tile_in)
    pl.semaphore_wait(barrier, len(greeted))

    for copy in fetch_copies(0, tile_in):
        copy.start()
    for channel in range(3):
        for half in range(2):
            for j in range(positions):
                pads[channel, half, j, pl.ds(0, N), :] = jnp.zeros((N, N), F32)
                pads[channel, half, j, pl.ds(2 * N, N), :] = jnp.zeros((N, N), F32)
    loads[1].wait()
    light(0)
    for copy in light_copies(0):
        copy.start()

    loads[2].wait()
    loads[3].wait()
    tiles = [tile_in, tile1, obj_out]
    for it in range(ITERS):
        for copy in fetch_copies(it, tiles[it]):
            copy.wait_recv()
        assemble(it, tiles[it])
        extract(it)
        send_m(it)
        if it > 0:
            wait_p(it - 1)
        waves(it)
        send_n(it)
        send_mz(it)
        gradient(it)
        for copy in grad_copies(it):
            copy.start()
        if it > 0:
            light(it)
            for copy in light_copies(it):
                copy.start()
        for copy in light_copies(it):
            copy.wait_recv()
        own_light(it)
        send_nz(it)
        for copy in grad_copies(it):
            copy.wait_recv()
        update(it, tiles[it], tiles[it + 1])
        if it + 1 < ITERS:
            pack(it + 1, tiles[it + 1])
            for copy in fetch_copies(it + 1, tiles[it + 1]):
                copy.start()
        send_p(it)
    wait_p(ITERS - 1)
    for k in range(modes):
        for c in range(2):
            prb_out[k, c] = probe_part(ITERS, k, c)

    for it in range(ITERS):
        for copies in (fetch_copies(it, tiles[it]), grad_copies(it), light_copies(it)):
            for copy in copies:
                copy.wait_send()
        await_bytes(m_rcv.at[it], all_send.at[0, it])
        await_bytes(mz_rcv.at[it], all_send.at[1, it])
        await_bytes(n_rcv.at[it], all_send.at[2, it])
        await_bytes(nz_rcv.at[it], all_send.at[3, it])
        await_bytes(p_buf.at[it, pl.ds(0, group - 1)], all_send.at[4, it])


def per_device(n_sy, n_sx, object_tile, probe_modes, scan_offsets, intensities):
    positions = scan_offsets.shape[2]
    modes = probe_modes.shape[0]
    depth = n_sx // Y_LO
    group = n_sy * Y_LO
    blocks = group // modes
    rows = N // blocks
    offsets = scan_offsets.transpose(0, 1, 3, 2)
    measured = intensities[0, 0]
    tables = jnp.asarray(dft_tables())
    vmem = functools.partial(pltpu.VMEM, dtype=F32)
    it = ITERS
    scratch = [
        vmem(object_tile.shape), vmem(probe_modes.shape), vmem(measured.shape),
        pltpu.VMEM(tables.shape, BF16),
        vmem((2, N, N)), vmem((it, 2, 2 * N, N)), vmem((it, 2, 2 * N, N)),
        vmem((it, N, N)), vmem((it, N, N)), vmem((it, 2 * N, N)), vmem((it, 2 * N, N)),
        vmem((positions, 2, N, N)), vmem((positions, 2, N, N)), vmem((modes, 2, N, N)),
        vmem((3, 2, positions, 3 * N, N)), vmem((it, 2, 2 * N, N)), vmem((2, 2 * N, N)),
        vmem((it, 2 * N, N)), vmem((it, 2 * N, N)), vmem((it, 2, HALF, N)), vmem((it, 2, HALF, N)),
        vmem((it, 2 * N, N)), vmem((it, 2 * N, N)),
        vmem((it, 2 * N, N)), vmem((2 * N, N)), vmem((it, N, N)), vmem((it, N, N)),
        vmem((it, HALF, N)), vmem((it, HALF, N)),
        vmem((it, N, N)), vmem((it, N, N)), vmem((it, N, N)),
        vmem((it, group, 2, rows, N)), vmem((it, group - 1, 2, rows, N)), vmem((it, 2, rows, N)),
        vmem((it, depth - 1, 2, rows, N)),
        vmem((it, blocks, rows, N)), vmem((it, group - 1, rows, N)), vmem((it, rows, N)),
        vmem((it, depth - 1, rows, N)), vmem((it, group, 2, rows, N)),
        pltpu.SemaphoreType.DMA((3, it, len(SIDES))), pltpu.SemaphoreType.DMA((3, it, len(SIDES))),
        pltpu.SemaphoreType.DMA((5, it)), pltpu.SemaphoreType.DMA((5, it)),
        pltpu.SemaphoreType.DMA((4,)),
    ]
    in_vmem = pl.BlockSpec(memory_space=pltpu.VMEM)
    return pl.pallas_call(
        functools.partial(kernel, n_sy, n_sx, positions, modes),
        out_shape=(jax.ShapeDtypeStruct(object_tile.shape, F32),
                   jax.ShapeDtypeStruct(probe_modes.shape, F32)),
        in_specs=[pl.BlockSpec(memory_space=pltpu.SMEM)] + [pl.BlockSpec(memory_space=pl.ANY)] * 4,
        out_specs=(in_vmem, in_vmem),
        scratch_shapes=scratch,
        compiler_params=pltpu.CompilerParams(collective_id=0, has_side_effects=True),
    )(offsets, object_tile, probe_modes, measured, tables)


def solution(mesh):
    placed = (P(None, "sy", "sx"), P(), P("sy", "sx", None, None), P("sy", "sx", None, None, None))
    return jax.shard_map(
        functools.partial(per_device, mesh.shape["sy"], mesh.shape["sx"]),
        mesh=mesh,
        in_specs=placed,
        out_specs=(P(None, "sy", "sx"), P()),
        check_vma=False,
    )
```

```python
import functools

import numpy as np
import jax
import jax.numpy as jnp
from jax import lax
from jax.experimental import pallas as pl
from jax.experimental.pallas import tpu as pltpu
from jax.sharding import PartitionSpec as P

ITERS = 2
OBJECT_STEP = 0.5
PROBE_STEP = 2.0
REGULAR = 1.0
N = 128
HALF = 64
Y_LO = 2
MESH = pl.DeviceIdType.MESH
F32 = jnp.float32
BF16 = jnp.bfloat16

SIDES = [(-1, -1), (1, -1), (-1, 1), (1, 1), (-1, 0), (1, 0), (0, -1), (0, 1)]


def dft_tables():
    index = np.arange(N)
    angle = (index[:, None] * index[None, :] % N) * (2.0 * np.pi / N)
    scale = 1.0 / np.sqrt(float(N))
    cosine, sine = np.cos(angle) * scale, np.sin(angle) * scale
    forward = np.block([[cosine, -sine], [sine, cosine]])
    parts = []
    for matrix in (forward, forward.T):
        high = matrix.astype(np.float32).astype(BF16)
        low = (matrix - high.astype(np.float64)).astype(np.float32).astype(BF16)
        parts += [high, low]
    return np.stack(parts)


def split(value):
    high = value.astype(BF16)
    low = (value - high.astype(F32)).astype(BF16)
    return high, low


def dot(left, right):
    return jnp.dot(left, right, preferred_element_type=F32)


def swap_blocks(value):
    top = jnp.concatenate([value[:N, :N], value[N:, :N]], axis=1)
    bottom = jnp.concatenate([value[:N, N:], value[N:, N:]], axis=1)
    return jnp.concatenate([top, bottom], axis=0)


def far_first(count):
    return sorted(range(count), key=lambda d: -min(d, count - d))


def kernel(n_sy, n_sx, positions, modes, offs, tile_hbm, probe_hbm, inten_hbm, tables_hbm,
           obj_out, prb_out,
           tile_in, probe_in, inten, tables, near_offs,
           tile1, can_t, can_h, pack_l, pack_r, strip_l, strip_r,
           obj, nacc, pads, bright_pad, g_t, g_h, gp_l, gp_r, g_up, g_dn, f_l, f_r, l_sum,
           n_buf, n_pre, n_chip, n_rcv, n_part, nz_rcv,
           m_buf, m_pre, m_chip, m_rcv, m_part, mz_rcv, p_buf,
           side_send, side_recv, pair_send, pair_recv, all_send, all_recv, load_sem):
    sy = lax.axis_index("sy")
    sx = lax.axis_index("sx")
    depth = n_sx // Y_LO
    cores = 2
    n_yh = min(2, n_sy // cores)
    n_x, n_y = n_sy // (cores * n_yh), n_yh * Y_LO
    core = lax.rem(sy, cores)
    x = lax.div(sy, cores * n_yh)
    y_lo = lax.div(sx, depth)
    y = lax.rem(lax.div(sy, cores), n_yh) * Y_LO + y_lo
    z = lax.rem(sx, depth)
    x_at = [lax.rem(x + d, n_x) for d in range(n_x)]
    y_at = [lax.rem(y + d, n_y) for d in range(n_y)]
    y_row = [lax.div(v, Y_LO) * cores + core for v in y_at]
    y_col = [lax.rem(v, Y_LO) * depth + z for v in y_at]
    blocks = n_x * n_y
    rows = N // blocks
    me = x * n_y + y
    peers = [(dx, dy) for dx in far_first(n_x) for dy in far_first(n_y) if dx or dy]
    peers.sort(key=lambda p: -(min(p[0], n_x - p[0]) + min(p[1], n_y - p[1])))
    peer_index = [x_at[dx] * n_y + y_at[dy] for dx, dy in peers]
    peer_dev = [(x_at[dx] * (cores * n_yh) + y_row[dy], y_col[dy]) for dx, dy in peers]
    z_devs = [(sy, y_lo * depth + lax.rem(z + d, depth)) for d in far_first(depth) if d]
    partner = (sy + 1 - 2 * core, sx)

    def side_dev(step):
        dy, dx = step
        return (lax.rem(sy + (n_sy + dy), n_sy), lax.rem(sx + (n_sx + dx), n_sx))

    lane = lax.broadcasted_iota(jnp.int32, (HALF, N), 1)
    lane_n = lax.broadcasted_iota(jnp.int32, (N, N), 1)
    has_u = jnp.where(sy > 0, 1, 0)
    has_d = jnp.where(sy < n_sy - 1, 1, 0)
    has_l = jnp.where(sx > 0, 1, 0)
    has_r = jnp.where(sx < n_sx - 1, 1, 0)

    def remote(src, dst, send, recv, dev):
        return pltpu.make_async_remote_copy(
            src_ref=src, dst_ref=dst, send_sem=send, recv_sem=recv,
            device_id=dev, device_id_type=MESH)

    def await_bytes(ref, sem):
        pltpu.make_async_copy(ref, ref, sem).wait()

    def fetch_copies(it, tile):
        top, bottom, both = pl.ds(0, HALF), pl.ds(HALF, HALF), pl.ds(0, N)
        c_top, c_mid, c_low = pl.ds(0, HALF), pl.ds(HALF, N), pl.ds(N + HALF, HALF)
        plan = [
            (pack_l.at[it, top], strip_r.at[it, c_low]),
            (pack_l.at[it, bottom], strip_r.at[it, c_top]),
            (pack_r.at[it, top], strip_l.at[it, c_low]),
            (pack_r.at[it, bottom], strip_l.at[it, c_top]),
            (tile.at[:, top, :], can_t.at[it, :, c_low, :]),
            (tile.at[:, bottom, :], can_t.at[it, :, c_top, :]),
            (pack_l.at[it, both], strip_r.at[it, c_mid]),
            (pack_r.at[it, both], strip_l.at[it, c_mid]),
        ]
        return [remote(src, dst, side_send.at[0, it, i], side_recv.at[0, it, i], side_dev(SIDES[i]))
                for i, (src, dst) in enumerate(plan)]

    def strip_copies(kind, it, unit, vertical, src_l, src_r, left, right):
        top, mid, low = pl.ds(0, unit), pl.ds(unit, 2 * unit), pl.ds(3 * unit, unit)
        plan = [
            (src_l.at[top], right.at[top]),
            (src_l.at[low], right.at[low]),
            (src_r.at[top], left.at[top]),
            (src_r.at[low], left.at[low]),
        ] + vertical + [
            (src_l.at[mid], right.at[mid]),
            (src_r.at[mid], left.at[mid]),
        ]
        return [remote(src, dst, side_send.at[kind, it, i], side_recv.at[kind, it, i],
                       side_dev(SIDES[i])) for i, (src, dst) in enumerate(plan)]

    def grad_copies(it):
        vertical = [(g_t.at[it, :, pl.ds(0, HALF), :], g_up.at[it]),
                    (g_t.at[it, :, pl.ds(N + HALF, HALF), :], g_dn.at[it])]
        return strip_copies(1, it, HALF, vertical, gp_l.at[it], gp_r.at[it], f_l.at[it], f_r.at[it])

    def offset_copies():
        return [remote(offs, near_offs.at[i], side_send.at[2, 0, i], side_recv.at[2, 0, i],
                       side_dev(step)) for i, step in enumerate(SIDES)]

    def pack(it, tile):
        real, rolled = tile[0], pltpu.roll(tile[1], HALF, 1)
        pack_l[it] = jnp.where(lane_n < HALF, real, rolled)
        pack_r[it] = jnp.where(lane_n >= HALF, real, rolled)

    def column_mask(column):
        return (lane_n >= column - HALF) & (lane_n < column + HALF)

    def assemble(it, tile):
        keep_re = (lane >= HALF * (1 - has_r)) & (lane < HALF + HALF * has_l)
        keep_im = (lane >= HALF * (1 - has_l)) & (lane < HALF + HALF * has_r)
        keep_u = lane < N * has_u
        keep_d = lane < N * has_d
        for c in range(2):
            can_t[it, c, pl.ds(HALF, N), :] = tile[c]
            top = can_t[it, c, pl.ds(0, HALF), :]
            can_t[it, c, pl.ds(0, HALF), :] = jnp.where(keep_u, top, 0.0)
            low = can_t[it, c, pl.ds(N + HALF, HALF), :]
            can_t[it, c, pl.ds(N + HALF, HALF), :] = jnp.where(keep_d, low, 0.0)
        for part in range(4):
            at = pl.ds(part * HALF, HALF)
            left, right = strip_l[it, at], strip_r[it, at]
            real = jnp.where(keep_re, jnp.where(lane < HALF, right, left), 0.0)
            imag = jnp.where(keep_im, jnp.where(lane < HALF, left, right), 0.0)
            if part == 0:
                real, imag = jnp.where(keep_u, real, 0.0), jnp.where(keep_u, imag, 0.0)
            if part == 3:
                real, imag = jnp.where(keep_d, real, 0.0), jnp.where(keep_d, imag, 0.0)
            can_h[it, 0, at, :] = real
            can_h[it, 1, at, :] = pltpu.roll(imag, HALF, 1)

    def extract(it):
        total = None
        for j in range(positions):
            row, column = offs[0, 0, 0, j], offs[0, 0, 1, j]
            mask = column_mask(column)
            shift = lax.rem(HALF + N - column, N)
            for c in range(2):
                inner = can_t[it, c, pl.ds(row, N), :]
                outer = can_h[it, c, pl.ds(row, N), :]
                patch = pltpu.roll(jnp.where(mask, inner, outer), shift, 1)
                obj[j, c] = patch
                total = patch * patch if total is None else total + patch * patch
        m_buf[it] = total.reshape(blocks, rows, N)
        pair(0, it, m_buf.at[it], m_pre.at[it]).start()

    def place(channel, j, term):
        column = offs[0, 0, 1, j]
        mask = column_mask(column)
        turned = pltpu.roll(term, lax.rem(column + HALF, N), 1)
        pads[channel, 0, j, pl.ds(N, N), :] = jnp.where(mask, turned, 0.0)
        pads[channel, 1, j, pl.ds(N, N), :] = jnp.where(mask, 0.0, turned)

    def placed(channel, half):
        total = None
        for j in range(positions):
            window = pads[channel, half, j, pl.ds(N - offs[0, 0, 0, j], 2 * N), :]
            total = window if total is None else total + window
        return total

    def probe_part(it, k, c):
        if it == 0:
            return probe_in[k, c]
        return p_buf[it - 1, c, :, k].reshape(N, N)

    def light(it):
        bright = None
        for k in range(modes):
            for c in range(2):
                part = probe_part(it, k, c)
                bright = part * part if bright is None else bright + part * part
        bright_pad[pl.ds(N + HALF, N), :] = bright
        total = jnp.zeros((N, N), F32)
        for dy in (-1, 0, 1):
            for dx in (-1, 0, 1):
                inside = jnp.where((sy + dy >= 0) & (sy + dy < n_sy)
                                   & (sx + dx >= 0) & (sx + dx < n_sx), 0, 4 * N)
                table = near_offs.at[SIDES.index((-dy, -dx))] if dx or dy else offs

                def position(j, running, dy=dy, dx=dx, inside=inside, table=table):
                    column = table[0, 0, 1, j]
                    window = bright_pad[pl.ds(2 * N - N * dy - table[0, 0, 0, j], N), :]
                    turned = pltpu.roll(window, lax.rem(column + HALF, N), 1)
                    first = column + (N * dx - HALF) + inside
                    mask = (lane_n >= first) & (lane_n < first + N)
                    return running + jnp.where(mask, turned, 0.0)

                total = lax.fori_loop(0, positions, position, total)
        l_sum[it] = total

    def pair(what, it, src, dst):
        return remote(src, dst, pair_send.at[what, it], pair_recv.at[what, it], partner)

    def n_pair(it):
        return pair(1, it, n_buf.at[it, 1 - core], n_pre.at[it])

    def p_pair(it):
        return pair(2, it, p_buf.at[it, core], p_buf.at[it, core])

    def spread(what, it, source, target):
        for slot, (other, dev) in enumerate(zip(peer_index, peer_dev)):
            remote(source(other), target(slot), all_send.at[what, it], all_recv.at[what, it],
                   dev).start()

    def spread_z(what, it, source, target):
        for slot, dev in enumerate(z_devs):
            remote(source, target(slot), all_send.at[what, it], all_recv.at[what, it], dev).start()

    def send_m(it):
        pair(0, it, m_buf.at[it], m_pre.at[it]).wait_recv()
        m_chip[it] = m_buf[it] + m_pre[it]
        spread(0, it, lambda other: m_chip.at[it, other], lambda s: m_rcv.at[it, s])

    def send_mz(it):
        await_bytes(m_rcv.at[it], all_recv.at[0, it])
        m_part[it] = m_chip[it, me] + jnp.sum(m_rcv[it], axis=0)
        spread_z(1, it, m_part.at[it], lambda s: mz_rcv.at[it, s])

    def send_n(it):
        n_pair(it).wait_recv()
        n_chip[it] = n_buf[it, core] + n_pre[it]
        spread(2, it, lambda other: n_chip.at[it, other], lambda s: n_rcv.at[it, s])

    def send_nz(it):
        await_bytes(n_rcv.at[it], all_recv.at[2, it])
        n_part[it] = n_chip[it, me] + jnp.sum(n_rcv[it], axis=0)
        spread_z(3, it, n_part.at[it], lambda s: nz_rcv.at[it, s])

    def send_p(it):
        await_bytes(mz_rcv.at[it], all_recv.at[1, it])
        weight = m_part[it] + jnp.sum(mz_rcv[it], axis=0) + REGULAR
        await_bytes(nz_rcv.at[it], all_recv.at[3, it])
        numerator = n_part[it] + jnp.sum(nz_rcv[it], axis=0)
        for k in range(modes):
            if it == 0:
                old = probe_in[k, core, pl.ds(pl.multiple_of(me * rows, rows), rows), :]
            else:
                old = p_buf[it - 1, core, me, k]
            p_buf[it, core, me, k] = old - PROBE_STEP * numerator[k] / weight
        spread(4, it, lambda other: p_buf.at[it, core, me], lambda s: p_buf.at[it, core, me])

    def forward_p(it):
        await_bytes(p_buf.at[it, 0, pl.ds(0, blocks - 1)], all_recv.at[4, it])
        p_pair(it).start()

    def waves(it):
        nacc[...] = jnp.zeros_like(nacc)

        def position(j):
            o_re, o_im = obj[j, 0], obj[j, 1]
            wave = []
            for k in range(modes):
                p_re, p_im = probe_part(it, k, 0), probe_part(it, k, 1)
                wave.append(jnp.concatenate(
                    [p_re * o_re - p_im * o_im, p_re * o_im + p_im * o_re], axis=1))
            x_h, x_l = split(jnp.concatenate(wave, axis=0))
            half = dot(x_h, tables[0]) + dot(x_l, tables[0]) + dot(x_h, tables[1])
            b_h, b_l = split(swap_blocks(half))
            spec = dot(tables[2], b_h) + dot(tables[2], b_l) + dot(tables[3], b_h)
            power = spec[:N] * spec[:N] + spec[N:] * spec[N:]
            misfit = power[:, :N] + power[:, N:] - inten[j]
            wide = jnp.concatenate([misfit, misfit], axis=1)
            d_h, d_l = split(jnp.concatenate([spec[:N] * wide, spec[N:] * wide], axis=0))
            half = dot(tables[0], d_h) + dot(tables[0], d_l) + dot(tables[1], d_h)
            e_h, e_l = split(swap_blocks(half))
            chi = dot(e_h, tables[2]) + dot(e_l, tables[2]) + dot(e_h, tables[3])
            g_re, g_im = None, None
            for k in range(modes):
                c_re, c_im = chi[k * N:(k + 1) * N, :N], chi[k * N:(k + 1) * N, N:]
                nacc[k, 0] += o_re * c_re + o_im * c_im
                nacc[k, 1] += o_re * c_im - o_im * c_re
                p_re, p_im = probe_part(it, k, 0), probe_part(it, k, 1)
                a_re = p_re * c_re + p_im * c_im
                a_im = p_re * c_im - p_im * c_re
                g_re = a_re if g_re is None else g_re + a_re
                g_im = a_im if g_im is None else g_im + a_im
            place(0, j, g_re)
            place(1, j, g_im)

        for j in range(positions):
            position(j)
            if j == 0:
                send_m(it)
        for k in range(modes):
            for c in range(2):
                n_buf[it, c, :, k] = nacc[k, c].reshape(blocks, rows, N)
        n_pair(it).start()

    def gradient(it):
        for c in range(2):
            g_t[it, c] = placed(c, 0)
            g_h[c] = placed(c, 1)
        wide = lax.broadcasted_iota(jnp.int32, (2 * N, N), 1)
        real, rolled = g_h[0], pltpu.roll(g_h[1], HALF, 1)
        gp_l[it] = jnp.where(wide >= HALF, real, rolled)
        gp_r[it] = jnp.where(wide < HALF, real, rolled)

    def strip_sum(strip):
        top, low = strip[pl.ds(0, HALF)], strip[pl.ds(N + HALF, HALF)]
        upper = strip[pl.ds(HALF, HALF)] + jnp.where(lane < N * has_u, low, 0.0)
        lower = strip[pl.ds(N, HALF)] + jnp.where(lane < N * has_d, top, 0.0)
        return jnp.concatenate([upper, lower], axis=0)

    def update(it, old, new):
        from_l, from_r = strip_sum(f_l.at[it]), strip_sum(f_r.at[it])
        weight = l_sum[it] + REGULAR
        for c in range(2):
            from_up = jnp.where(lane < N * has_u, g_dn[it, c], 0.0)
            from_down = jnp.where(lane < N * has_d, g_up[it, c], 0.0)
            total = g_t[it, c, pl.ds(HALF, N), :] + jnp.concatenate([from_up, from_down], axis=0)
            left = from_l if c == 0 else pltpu.roll(from_l, HALF, 1)
            right = from_r if c == 0 else pltpu.roll(from_r, HALF, 1)
            total += jnp.where(lane_n < HALF * has_l, left, 0.0)
            total += jnp.where(lane_n >= N - HALF * has_r, right, 0.0)
            new[c] = old[c] - OBJECT_STEP * total / weight

    barrier = pltpu.get_barrier_semaphore()
    greeted = [side_dev(step) for step in SIDES] + peer_dev + z_devs + [partner]
    for dev in greeted:
        pl.semaphore_signal(barrier, inc=1, device_id=dev, device_id_type=MESH)
    loads = [pltpu.make_async_copy(src, dst, load_sem.at[i]) for i, (src, dst) in enumerate(
        [(tile_hbm, tile_in), (probe_hbm, probe_in), (tables_hbm, tables), (inten_hbm, inten)])]
    for load in loads:
        load.start()
    loads[0].wait()
    pack(0, tile_in)
    pl.semaphore_wait(barrier, len(greeted))

    for copy in fetch_copies(0, tile_in) + offset_copies():
        copy.start()
    for channel in range(2):
        for half in range(2):
            for j in range(positions):
                pads[channel, half, j, pl.ds(0, N), :] = jnp.zeros((N, N), F32)
                pads[channel, half, j, pl.ds(2 * N, N), :] = jnp.zeros((N, N), F32)
    bright_pad[...] = jnp.zeros_like(bright_pad)
    for load in loads[1:]:
        load.wait()

    tiles = [tile_in, tile1, obj_out]
    for it in range(ITERS):
        for copy in fetch_copies(it, tiles[it]):
            copy.wait_recv()
        assemble(it, tiles[it])
        extract(it)
        if it > 0:
            p_pair(it - 1).wait_recv()
        waves(it)
        gradient(it)
        send_n(it)
        for copy in grad_copies(it):
            copy.start()
        send_mz(it)
        if it == 0:
            for copy in offset_copies():
                copy.wait_recv()
        light(it)
        send_nz(it)
        for copy in grad_copies(it):
            copy.wait_recv()
        update(it, tiles[it], tiles[it + 1])
        if it + 1 < ITERS:
            pack(it + 1, tiles[it + 1])
            for copy in fetch_copies(it + 1, tiles[it + 1]):
                copy.start()
        send_p(it)
        forward_p(it)
    p_pair(ITERS - 1).wait_recv()
    for k in range(modes):
        for c in range(2):
            prb_out[k, c] = probe_part(ITERS, k, c)

    for copy in offset_copies():
        copy.wait_send()
    for it in range(ITERS):
        for copy in fetch_copies(it, tiles[it]) + grad_copies(it):
            copy.wait_send()
        pair(0, it, m_buf.at[it], m_pre.at[it]).wait_send()
        n_pair(it).wait_send()
        p_pair(it).wait_send()
        await_bytes(m_rcv.at[it], all_send.at[0, it])
        await_bytes(mz_rcv.at[it], all_send.at[1, it])
        await_bytes(n_rcv.at[it], all_send.at[2, it])
        await_bytes(nz_rcv.at[it], all_send.at[3, it])
        await_bytes(p_buf.at[it, 0, pl.ds(0, blocks - 1)], all_send.at[4, it])


def per_device(n_sy, n_sx, object_tile, probe_modes, scan_offsets, intensities):
    positions = scan_offsets.shape[2]
    modes = probe_modes.shape[0]
    depth = n_sx // Y_LO
    blocks = n_sy // 2 * Y_LO
    rows = N // blocks
    offsets = scan_offsets.transpose(0, 1, 3, 2)
    measured = intensities[0, 0]
    tables = jnp.asarray(dft_tables())
    vmem = functools.partial(pltpu.VMEM, dtype=F32)
    it = ITERS
    scratch = [
        vmem(object_tile.shape), vmem(probe_modes.shape), vmem(measured.shape),
        pltpu.VMEM(tables.shape, BF16), pltpu.SMEM((len(SIDES),) + offsets.shape, jnp.int32),
        vmem((2, N, N)), vmem((it, 2, 2 * N, N)), vmem((it, 2, 2 * N, N)),
        vmem((it, N, N)), vmem((it, N, N)), vmem((it, 2 * N, N)), vmem((it, 2 * N, N)),
        vmem((positions, 2, N, N)), vmem((modes, 2, N, N)),
        vmem((2, 2, positions, 3 * N, N)), vmem((4 * N, N)),
        vmem((it, 2, 2 * N, N)), vmem((2, 2 * N, N)),
        vmem((it, 2 * N, N)), vmem((it, 2 * N, N)), vmem((it, 2, HALF, N)), vmem((it, 2, HALF, N)),
        vmem((it, 2 * N, N)), vmem((it, 2 * N, N)), vmem((it, N, N)),
        vmem((it, 2, blocks, modes, rows, N)), vmem((it, blocks, modes, rows, N)),
        vmem((it, blocks, modes, rows, N)), vmem((it, blocks - 1, modes, rows, N)),
        vmem((it, modes, rows, N)), vmem((it, depth - 1, modes, rows, N)),
        vmem((it, blocks, rows, N)), vmem((it, blocks, rows, N)), vmem((it, blocks, rows, N)),
        vmem((it, blocks - 1, rows, N)), vmem((it, rows, N)), vmem((it, depth - 1, rows, N)),
        vmem((it, 2, blocks, modes, rows, N)),
        pltpu.SemaphoreType.DMA((3, it, len(SIDES))), pltpu.SemaphoreType.DMA((3, it, len(SIDES))),
        pltpu.SemaphoreType.DMA((3, it)), pltpu.SemaphoreType.DMA((3, it)),
        pltpu.SemaphoreType.DMA((5, it)), pltpu.SemaphoreType.DMA((5, it)),
        pltpu.SemaphoreType.DMA((4,)),
    ]
    in_vmem = pl.BlockSpec(memory_space=pltpu.VMEM)
    return pl.pallas_call(
        functools.partial(kernel, n_sy, n_sx, positions, modes),
        out_shape=(jax.ShapeDtypeStruct(object_tile.shape, F32),
                   jax.ShapeDtypeStruct(probe_modes.shape, F32)),
        in_specs=[pl.BlockSpec(memory_space=pltpu.SMEM)] + [pl.BlockSpec(memory_space=pl.ANY)] * 4,
        out_specs=(in_vmem, in_vmem),
        scratch_shapes=scratch,
        compiler_params=pltpu.CompilerParams(collective_id=0, has_side_effects=True),
    )(offsets, object_tile, probe_modes, measured, tables)


def solution(mesh):
    placed = (P(None, "sy", "sx"), P(), P("sy", "sx", None, None), P("sy", "sx", None, None, None))
    return jax.shard_map(
        functools.partial(per_device, mesh.shape["sy"], mesh.shape["sx"]),
        mesh=mesh,
        in_specs=placed,
        out_specs=(P(None, "sy", "sx"), P()),
        check_vma=False,
    )
```

```python
import functools

import numpy as np
import jax
import jax.numpy as jnp
from jax import lax
from jax.experimental import pallas as pl
from jax.experimental.pallas import tpu as pltpu
from jax.sharding import PartitionSpec as P

ITERS = 2
OBJECT_STEP = 0.5
PROBE_STEP = 2.0
REGULAR = 1.0
N = 128
HALF = 64
Y_LO = 2
MESH = pl.DeviceIdType.MESH
F32 = jnp.float32
BF16 = jnp.bfloat16

SIDES = [(-1, -1), (1, -1), (-1, 1), (1, 1), (-1, 0), (1, 0), (0, -1), (0, 1)]


def dft_tables():
    index = np.arange(N)
    angle = (index[:, None] * index[None, :] % N) * (2.0 * np.pi / N)
    scale = 1.0 / np.sqrt(float(N))
    cosine, sine = np.cos(angle) * scale, np.sin(angle) * scale
    forward = np.block([[cosine, -sine], [sine, cosine]])
    parts = []
    for matrix in (forward, forward.T):
        high = matrix.astype(np.float32).astype(BF16)
        low = (matrix - high.astype(np.float64)).astype(np.float32).astype(BF16)
        parts += [high, low]
    return np.stack(parts)


def split(value):
    high = value.astype(BF16)
    low = (value - high.astype(F32)).astype(BF16)
    return high, low


def dot(left, right):
    return jnp.dot(left, right, preferred_element_type=F32)


def swap_blocks(value):
    top = jnp.concatenate([value[:N, :N], value[N:, :N]], axis=1)
    bottom = jnp.concatenate([value[:N, N:], value[N:, N:]], axis=1)
    return jnp.concatenate([top, bottom], axis=0)


def far_first(count):
    return sorted(range(count), key=lambda d: -min(d, count - d))


def kernel(n_sy, n_sx, positions, modes, offs, tile_hbm, probe_hbm, inten_hbm, tables_hbm,
           obj_out, prb_out,
           tile_in, probe_in, inten, tables, near_offs,
           tile1, can_t, can_h, pack_l, pack_r, strip_l, strip_r,
           obj, nacc, pads, bright_pad, g_t, g_h, gp_l, gp_r, g_up, g_dn, f_l, f_r, l_sum,
           n_buf, n_pre, n_chip, n_rcv, n_part, nz_rcv,
           m_buf, m_pre, m_chip, m_rcv, m_part, mz_rcv, p_buf,
           side_send, side_recv, pair_send, pair_recv, all_send, all_recv, load_sem):
    sy = lax.axis_index("sy")
    sx = lax.axis_index("sx")
    depth = n_sx // Y_LO
    cores = 2
    n_yh = min(2, n_sy // cores)
    n_x, n_y = n_sy // (cores * n_yh), n_yh * Y_LO
    core = lax.rem(sy, cores)
    x = lax.div(sy, cores * n_yh)
    y_lo = lax.div(sx, depth)
    y = lax.rem(lax.div(sy, cores), n_yh) * Y_LO + y_lo
    z = lax.rem(sx, depth)
    x_at = [lax.rem(x + d, n_x) for d in range(n_x)]
    y_at = [lax.rem(y + d, n_y) for d in range(n_y)]
    y_row = [lax.div(v, Y_LO) * cores + core for v in y_at]
    y_col = [lax.rem(v, Y_LO) * depth + z for v in y_at]
    blocks = n_x * n_y
    rows = N // blocks
    me = x * n_y + y
    peers = [(dx, dy) for dx in far_first(n_x) for dy in far_first(n_y) if dx or dy]
    peers.sort(key=lambda p: -(min(p[0], n_x - p[0]) + min(p[1], n_y - p[1])))
    peer_index = [x_at[dx] * n_y + y_at[dy] for dx, dy in peers]
    peer_dev = [(x_at[dx] * (cores * n_yh) + y_row[dy], y_col[dy]) for dx, dy in peers]
    z_devs = [(sy, y_lo * depth + lax.rem(z + d, depth)) for d in far_first(depth) if d]
    partner = (sy + 1 - 2 * core, sx)

    def side_dev(step):
        dy, dx = step
        return (lax.rem(sy + (n_sy + dy), n_sy), lax.rem(sx + (n_sx + dx), n_sx))

    lane = lax.broadcasted_iota(jnp.int32, (HALF, N), 1)
    lane_n = lax.broadcasted_iota(jnp.int32, (N, N), 1)
    has_u = jnp.where(sy > 0, 1, 0)
    has_d = jnp.where(sy < n_sy - 1, 1, 0)
    has_l = jnp.where(sx > 0, 1, 0)
    has_r = jnp.where(sx < n_sx - 1, 1, 0)

    def remote(src, dst, send, recv, dev):
        return pltpu.make_async_remote_copy(
            src_ref=src, dst_ref=dst, send_sem=send, recv_sem=recv,
            device_id=dev, device_id_type=MESH)

    def await_bytes(ref, sem):
        pltpu.make_async_copy(ref, ref, sem).wait()

    def fetch_copies(it, tile):
        top, bottom, both = pl.ds(0, HALF), pl.ds(HALF, HALF), pl.ds(0, N)
        c_top, c_mid, c_low = pl.ds(0, HALF), pl.ds(HALF, N), pl.ds(N + HALF, HALF)
        plan = [
            (pack_l.at[it, top], strip_r.at[it, c_low]),
            (pack_l.at[it, bottom], strip_r.at[it, c_top]),
            (pack_r.at[it, top], strip_l.at[it, c_low]),
            (pack_r.at[it, bottom], strip_l.at[it, c_top]),
            (tile.at[:, top, :], can_t.at[it, :, c_low, :]),
            (tile.at[:, bottom, :], can_t.at[it, :, c_top, :]),
            (pack_l.at[it, both], strip_r.at[it, c_mid]),
            (pack_r.at[it, both], strip_l.at[it, c_mid]),
        ]
        return [remote(src, dst, side_send.at[0, it, i], side_recv.at[0, it, i], side_dev(SIDES[i]))
                for i, (src, dst) in enumerate(plan)]

    def strip_copies(kind, it, unit, vertical, src_l, src_r, left, right):
        top, mid, low = pl.ds(0, unit), pl.ds(unit, 2 * unit), pl.ds(3 * unit, unit)
        plan = [
            (src_l.at[top], right.at[top]),
            (src_l.at[low], right.at[low]),
            (src_r.at[top], left.at[top]),
            (src_r.at[low], left.at[low]),
        ] + vertical + [
            (src_l.at[mid], right.at[mid]),
            (src_r.at[mid], left.at[mid]),
        ]
        return [remote(src, dst, side_send.at[kind, it, i], side_recv.at[kind, it, i],
                       side_dev(SIDES[i])) for i, (src, dst) in enumerate(plan)]

    def grad_copies(it):
        vertical = [(g_t.at[it, :, pl.ds(0, HALF), :], g_up.at[it]),
                    (g_t.at[it, :, pl.ds(N + HALF, HALF), :], g_dn.at[it])]
        return strip_copies(1, it, HALF, vertical, gp_l.at[it], gp_r.at[it], f_l.at[it], f_r.at[it])

    def offset_copies():
        return [remote(offs, near_offs.at[i], side_send.at[2, 0, i], side_recv.at[2, 0, i],
                       side_dev(step)) for i, step in enumerate(SIDES)]

    def pack(it, tile):
        real, rolled = tile[0], pltpu.roll(tile[1], HALF, 1)
        pack_l[it] = jnp.where(lane_n < HALF, real, rolled)
        pack_r[it] = jnp.where(lane_n >= HALF, real, rolled)

    def column_mask(column):
        return (lane_n >= column - HALF) & (lane_n < column + HALF)

    def assemble(it, tile):
        keep_re = (lane >= HALF * (1 - has_r)) & (lane < HALF + HALF * has_l)
        keep_im = (lane >= HALF * (1 - has_l)) & (lane < HALF + HALF * has_r)
        keep_u = lane < N * has_u
        keep_d = lane < N * has_d
        for c in range(2):
            can_t[it, c, pl.ds(HALF, N), :] = tile[c]
            top = can_t[it, c, pl.ds(0, HALF), :]
            can_t[it, c, pl.ds(0, HALF), :] = jnp.where(keep_u, top, 0.0)
            low = can_t[it, c, pl.ds(N + HALF, HALF), :]
            can_t[it, c, pl.ds(N + HALF, HALF), :] = jnp.where(keep_d, low, 0.0)
        for part in range(4):
            at = pl.ds(part * HALF, HALF)
            left, right = strip_l[it, at], strip_r[it, at]
            real = jnp.where(keep_re, jnp.where(lane < HALF, right, left), 0.0)
            imag = jnp.where(keep_im, jnp.where(lane < HALF, left, right), 0.0)
            if part == 0:
                real, imag = jnp.where(keep_u, real, 0.0), jnp.where(keep_u, imag, 0.0)
            if part == 3:
                real, imag = jnp.where(keep_d, real, 0.0), jnp.where(keep_d, imag, 0.0)
            can_h[it, 0, at, :] = real
            can_h[it, 1, at, :] = pltpu.roll(imag, HALF, 1)

    def extract(it):
        total = None
        for j in range(positions):
            row, column = offs[0, 0, 0, j], offs[0, 0, 1, j]
            mask = column_mask(column)
            shift = lax.rem(HALF + N - column, N)
            for c in range(2):
                inner = can_t[it, c, pl.ds(row, N), :]
                outer = can_h[it, c, pl.ds(row, N), :]
                patch = pltpu.roll(jnp.where(mask, inner, outer), shift, 1)
                obj[j, c] = patch
                total = patch * patch if total is None else total + patch * patch
        m_buf[it] = total.reshape(blocks, rows, N)
        pair(0, it, m_buf.at[it], m_pre.at[it]).start()

    def place(channel, j, term):
        column = offs[0, 0, 1, j]
        mask = column_mask(column)
        turned = pltpu.roll(term, lax.rem(column + HALF, N), 1)
        pads[channel, 0, j, pl.ds(N, N), :] = jnp.where(mask, turned, 0.0)
        pads[channel, 1, j, pl.ds(N, N), :] = jnp.where(mask, 0.0, turned)

    def placed(channel, half):
        total = None
        for j in range(positions):
            window = pads[channel, half, j, pl.ds(N - offs[0, 0, 0, j], 2 * N), :]
            total = window if total is None else total + window
        return total

    def probe_part(it, k, c):
        if it == 0:
            return probe_in[k, c]
        return p_buf[it - 1, c, :, k].reshape(N, N)

    def light(it):
        bright = None
        for k in range(modes):
            for c in range(2):
                part = probe_part(it, k, c)
                bright = part * part if bright is None else bright + part * part
        bright_pad[pl.ds(N + HALF, N), :] = bright
        total = jnp.zeros((N, N), F32)
        for dy in (-1, 0, 1):
            for dx in (-1, 0, 1):
                inside = jnp.where((sy + dy >= 0) & (sy + dy < n_sy)
                                   & (sx + dx >= 0) & (sx + dx < n_sx), 0, 4 * N)
                table = near_offs.at[SIDES.index((-dy, -dx))] if dx or dy else offs

                def position(j, running, dy=dy, dx=dx, inside=inside, table=table):
                    column = table[0, 0, 1, j]
                    window = bright_pad[pl.ds(2 * N - N * dy - table[0, 0, 0, j], N), :]
                    turned = pltpu.roll(window, lax.rem(column + HALF, N), 1)
                    first = column + (N * dx - HALF) + inside
                    mask = (lane_n >= first) & (lane_n < first + N)
                    return running + jnp.where(mask, turned, 0.0)

                total = lax.fori_loop(0, positions, position, total)
        l_sum[it] = total

    def pair(what, it, src, dst):
        return remote(src, dst, pair_send.at[what, it], pair_recv.at[what, it], partner)

    def n_pair(it):
        return pair(1, it, n_buf.at[it, 1 - core], n_pre.at[it])

    def p_pair(it):
        return pair(2, it, p_buf.at[it, core], p_buf.at[it, core])

    def spread(what, it, source, target):
        for slot, (other, dev) in enumerate(zip(peer_index, peer_dev)):
            remote(source(other), target(slot), all_send.at[what, it], all_recv.at[what, it],
                   dev).start()

    def spread_z(what, it, source, target):
        for slot, dev in enumerate(z_devs):
            remote(source, target(slot), all_send.at[what, it], all_recv.at[what, it], dev).start()

    def send_m(it):
        pair(0, it, m_buf.at[it], m_pre.at[it]).wait_recv()
        m_chip[it] = m_buf[it] + m_pre[it]
        spread(0, it, lambda other: m_chip.at[it, other], lambda s: m_rcv.at[it, s])

    def send_mz(it):
        await_bytes(m_rcv.at[it], all_recv.at[0, it])
        m_part[it] = m_chip[it, me] + jnp.sum(m_rcv[it], axis=0)
        spread_z(1, it, m_part.at[it], lambda s: mz_rcv.at[it, s])

    def send_n(it):
        n_pair(it).wait_recv()
        n_chip[it] = n_buf[it, core] + n_pre[it]
        spread(2, it, lambda other: n_chip.at[it, other], lambda s: n_rcv.at[it, s])

    def send_nz(it):
        await_bytes(n_rcv.at[it], all_recv.at[2, it])
        n_part[it] = n_chip[it, me] + jnp.sum(n_rcv[it], axis=0)
        spread_z(3, it, n_part.at[it], lambda s: nz_rcv.at[it, s])

    def send_p(it):
        await_bytes(mz_rcv.at[it], all_recv.at[1, it])
        weight = m_part[it] + jnp.sum(mz_rcv[it], axis=0) + REGULAR
        await_bytes(nz_rcv.at[it], all_recv.at[3, it])
        numerator = n_part[it] + jnp.sum(nz_rcv[it], axis=0)
        for k in range(modes):
            if it == 0:
                old = probe_in[k, core, pl.ds(pl.multiple_of(me * rows, rows), rows), :]
            else:
                old = p_buf[it - 1, core, me, k]
            p_buf[it, core, me, k] = old - PROBE_STEP * numerator[k] / weight
        spread(4, it, lambda other: p_buf.at[it, core, me], lambda s: p_buf.at[it, core, me])

    def forward_p(it):
        await_bytes(p_buf.at[it, 0, pl.ds(0, blocks - 1)], all_recv.at[4, it])
        p_pair(it).start()

    def waves(it):
        def right(v, t):
            h, l = split(v)
            return dot(h, tables[t]) + dot(l, tables[t]) + dot(h, tables[t + 1])

        def right_all(vs, t):
            if True:
                return [right(v, t) for v in vs]
            out = right(jnp.concatenate(vs, axis=0), t)
            return [out[i * 2 * N:(i + 1) * 2 * N] for i in range(len(vs))]

        def left(t, v):
            h, l = split(v)
            return dot(tables[t], h) + dot(tables[t], l) + dot(tables[t + 1], h)

        def exits(j):
            o_re, o_im = obj[j, 0], obj[j, 1]
            wave = []
            for k in range(modes):
                p_re, p_im = probe_part(it, k, 0), probe_part(it, k, 1)
                wave.append(jnp.concatenate(
                    [p_re * o_re - p_im * o_im, p_re * o_im + p_im * o_re], axis=1))
            return jnp.concatenate(wave, axis=0)

        def misfits(j, spec):
            power = spec[:N] * spec[:N] + spec[N:] * spec[N:]
            misfit = power[:, :N] + power[:, N:] - inten[j]
            wide = jnp.concatenate([misfit, misfit], axis=1)
            return jnp.concatenate([spec[:N] * wide, spec[N:] * wide], axis=0)

        def gather(j, chi, first):
            o_re, o_im = obj[j, 0], obj[j, 1]
            g_re, g_im = None, None
            for k in range(modes):
                c_re, c_im = chi[k * N:(k + 1) * N, :N], chi[k * N:(k + 1) * N, N:]
                n_re = o_re * c_re + o_im * c_im
                n_im = o_re * c_im - o_im * c_re
                nacc[k, 0] = n_re if first else nacc[k, 0] + n_re
                nacc[k, 1] = n_im if first else nacc[k, 1] + n_im
                p_re, p_im = probe_part(it, k, 0), probe_part(it, k, 1)
                a_re = p_re * c_re + p_im * c_im
                a_im = p_re * c_im - p_im * c_re
                g_re = a_re if g_re is None else g_re + a_re
                g_im = a_im if g_im is None else g_im + a_im
            place(0, j, g_re)
            place(1, j, g_im)

        for start in range(0, positions, 4):
            members = range(start, start + 4)
            waves_in = [exits(j) for j in members]
            half = [swap_blocks(v) for v in right_all(waves_in, 0)]
            spec = [left(2, v) for v in half]
            dev = [misfits(j, v) for j, v in zip(members, spec)]
            if start == 0:
                send_m(it)
            half = [swap_blocks(left(0, v)) for v in dev]
            chis = right_all(half, 2)
            for j, chi in zip(members, chis):
                gather(j, chi, j == 0)
        for k in range(modes):
            for c in range(2):
                n_buf[it, c, :, k] = nacc[k, c].reshape(blocks, rows, N)
        n_pair(it).start()

    def gradient(it):
        for c in range(2):
            g_t[it, c] = placed(c, 0)
            g_h[c] = placed(c, 1)
        wide = lax.broadcasted_iota(jnp.int32, (2 * N, N), 1)
        real, rolled = g_h[0], pltpu.roll(g_h[1], HALF, 1)
        gp_l[it] = jnp.where(wide >= HALF, real, rolled)
        gp_r[it] = jnp.where(wide < HALF, real, rolled)

    def strip_sum(strip):
        top, low = strip[pl.ds(0, HALF)], strip[pl.ds(N + HALF, HALF)]
        upper = strip[pl.ds(HALF, HALF)] + jnp.where(lane < N * has_u, low, 0.0)
        lower = strip[pl.ds(N, HALF)] + jnp.where(lane < N * has_d, top, 0.0)
        return jnp.concatenate([upper, lower], axis=0)

    def update(it, old, new):
        from_l, from_r = strip_sum(f_l.at[it]), strip_sum(f_r.at[it])
        weight = l_sum[it] + REGULAR
        for c in range(2):
            from_up = jnp.where(lane < N * has_u, g_dn[it, c], 0.0)
            from_down = jnp.where(lane < N * has_d, g_up[it, c], 0.0)
            total = g_t[it, c, pl.ds(HALF, N), :] + jnp.concatenate([from_up, from_down], axis=0)
            left = from_l if c == 0 else pltpu.roll(from_l, HALF, 1)
            right = from_r if c == 0 else pltpu.roll(from_r, HALF, 1)
            total += jnp.where(lane_n < HALF * has_l, left, 0.0)
            total += jnp.where(lane_n >= N - HALF * has_r, right, 0.0)
            new[c] = old[c] - OBJECT_STEP * total / weight

    loads = [pltpu.make_async_copy(src, dst, load_sem.at[i]) for i, (src, dst) in enumerate(
        [(tile_hbm, tile_in), (probe_hbm, probe_in), (tables_hbm, tables), (inten_hbm, inten)])]
    for load in loads:
        load.start()
    barrier = pltpu.get_barrier_semaphore()
    greeted = [side_dev(step) for step in SIDES] + peer_dev + z_devs + [partner]
    for dev in greeted:
        pl.semaphore_signal(barrier, inc=1, device_id=dev, device_id_type=MESH)
    loads[0].wait()
    pack(0, tile_in)
    pl.semaphore_wait(barrier, len(greeted))

    for copy in fetch_copies(0, tile_in) + offset_copies():
        copy.start()
    for channel in range(2):
        for half in range(2):
            for j in range(positions):
                pads[channel, half, j, pl.ds(0, N), :] = jnp.zeros((N, N), F32)
                pads[channel, half, j, pl.ds(2 * N, N), :] = jnp.zeros((N, N), F32)
    bright_pad[...] = jnp.zeros_like(bright_pad)
    for load in loads[1:]:
        load.wait()

    tiles = [tile_in, tile1, obj_out]
    for it in range(ITERS):
        for copy in fetch_copies(it, tiles[it]):
            copy.wait_recv()
        assemble(it, tiles[it])
        extract(it)
        if it > 0:
            p_pair(it - 1).wait_recv()
        waves(it)
        gradient(it)
        send_n(it)
        if it + 1 < ITERS:
            for copy in grad_copies(it):
                copy.start()
        send_mz(it)
        if it == 0:
            for copy in offset_copies():
                copy.wait_recv()
        light(it)
        send_nz(it)
        if it + 1 == ITERS:
            for copy in grad_copies(it):
                copy.start()
        if it + 1 == ITERS:
            send_p(it)
        for copy in grad_copies(it):
            copy.wait_recv()
        update(it, tiles[it], tiles[it + 1])
        if it + 1 < ITERS:
            pack(it + 1, tiles[it + 1])
            for copy in fetch_copies(it + 1, tiles[it + 1]):
                copy.start()
            send_p(it)
        forward_p(it)
    p_pair(ITERS - 1).wait_recv()
    for k in range(modes):
        for c in range(2):
            prb_out[k, c] = probe_part(ITERS, k, c)

    for copy in offset_copies():
        copy.wait_send()
    for it in range(ITERS):
        for copy in fetch_copies(it, tiles[it]) + grad_copies(it):
            copy.wait_send()
        pair(0, it, m_buf.at[it], m_pre.at[it]).wait_send()
        n_pair(it).wait_send()
        p_pair(it).wait_send()
        await_bytes(m_rcv.at[it], all_send.at[0, it])
        await_bytes(mz_rcv.at[it], all_send.at[1, it])
        await_bytes(n_rcv.at[it], all_send.at[2, it])
        await_bytes(nz_rcv.at[it], all_send.at[3, it])
        await_bytes(p_buf.at[it, 0, pl.ds(0, blocks - 1)], all_send.at[4, it])


def per_device(n_sy, n_sx, object_tile, probe_modes, scan_offsets, intensities):
    positions = scan_offsets.shape[2]
    modes = probe_modes.shape[0]
    depth = n_sx // Y_LO
    blocks = n_sy // 2 * Y_LO
    rows = N // blocks
    offsets = scan_offsets.transpose(0, 1, 3, 2)
    measured = intensities[0, 0]
    tables = jnp.asarray(dft_tables())
    vmem = functools.partial(pltpu.VMEM, dtype=F32)
    it = ITERS
    scratch = [
        vmem(object_tile.shape), vmem(probe_modes.shape), vmem(measured.shape),
        pltpu.VMEM(tables.shape, BF16), pltpu.SMEM((len(SIDES),) + offsets.shape, jnp.int32),
        vmem((2, N, N)), vmem((it, 2, 2 * N, N)), vmem((it, 2, 2 * N, N)),
        vmem((it, N, N)), vmem((it, N, N)), vmem((it, 2 * N, N)), vmem((it, 2 * N, N)),
        vmem((positions, 2, N, N)), vmem((modes, 2, N, N)),
        vmem((2, 2, positions, 3 * N, N)), vmem((4 * N, N)),
        vmem((it, 2, 2 * N, N)), vmem((2, 2 * N, N)),
        vmem((it, 2 * N, N)), vmem((it, 2 * N, N)), vmem((it, 2, HALF, N)), vmem((it, 2, HALF, N)),
        vmem((it, 2 * N, N)), vmem((it, 2 * N, N)), vmem((it, N, N)),
        vmem((it, 2, blocks, modes, rows, N)), vmem((it, blocks, modes, rows, N)),
        vmem((it, blocks, modes, rows, N)), vmem((it, blocks - 1, modes, rows, N)),
        vmem((it, modes, rows, N)), vmem((it, depth - 1, modes, rows, N)),
        vmem((it, blocks, rows, N)), vmem((it, blocks, rows, N)), vmem((it, blocks, rows, N)),
        vmem((it, blocks - 1, rows, N)), vmem((it, rows, N)), vmem((it, depth - 1, rows, N)),
        vmem((it, 2, blocks, modes, rows, N)),
        pltpu.SemaphoreType.DMA((3, it, len(SIDES))), pltpu.SemaphoreType.DMA((3, it, len(SIDES))),
        pltpu.SemaphoreType.DMA((3, it)), pltpu.SemaphoreType.DMA((3, it)),
        pltpu.SemaphoreType.DMA((5, it)), pltpu.SemaphoreType.DMA((5, it)),
        pltpu.SemaphoreType.DMA((4,)),
    ]
    in_vmem = pl.BlockSpec(memory_space=pltpu.VMEM)
    return pl.pallas_call(
        functools.partial(kernel, n_sy, n_sx, positions, modes),
        out_shape=(pltpu.VMEM(object_tile.shape, F32), pltpu.VMEM(probe_modes.shape, F32)),
        in_specs=[pl.BlockSpec(memory_space=pltpu.SMEM)] + [pl.BlockSpec(memory_space=pl.ANY)] * 4,
        out_specs=(in_vmem, in_vmem),
        scratch_shapes=scratch,
        compiler_params=pltpu.CompilerParams(collective_id=0, has_side_effects=True),
    )(offsets, object_tile, probe_modes, measured, tables)


def solution(mesh):
    placed = (P(None, "sy", "sx"), P(), P("sy", "sx", None, None), P("sy", "sx", None, None, None))
    return jax.shard_map(
        functools.partial(per_device, mesh.shape["sy"], mesh.shape["sx"]),
        mesh=mesh,
        in_specs=placed,
        out_specs=(P(None, "sy", "sx"), P()),
        check_vma=False,
    )
```

```python
import functools

import numpy as np
import jax
import jax.numpy as jnp
from jax import lax
from jax.experimental import pallas as pl
from jax.experimental.pallas import tpu as pltpu
from jax.sharding import PartitionSpec as P

ITERS = 2
OBJECT_STEP = 0.5
PROBE_STEP = 2.0
REGULAR = 1.0
N = 128
HALF = 64
Y_LO = 2
MESH = pl.DeviceIdType.MESH
F32 = jnp.float32
BF16 = jnp.bfloat16

SIDES = [(-1, -1), (1, -1), (-1, 1), (1, 1), (-1, 0), (1, 0), (0, -1), (0, 1)]


def dft_tables():
    index = np.arange(N)
    angle = (index[:, None] * index[None, :] % N) * (2.0 * np.pi / N)
    scale = 1.0 / np.sqrt(float(N))
    cosine, sine = np.cos(angle) * scale, np.sin(angle) * scale
    forward = np.block([[cosine, -sine], [sine, cosine]])
    parts = []
    for matrix in (forward, forward.T):
        high = matrix.astype(np.float32).astype(BF16)
        low = (matrix - high.astype(np.float64)).astype(np.float32).astype(BF16)
        parts += [high, low]
    return np.stack(parts)


def split(value):
    high = value.astype(BF16)
    low = (value - high.astype(F32)).astype(BF16)
    return high, low


def dot(left, right):
    return jnp.dot(left, right, preferred_element_type=F32)


def swap_blocks(value):
    top = jnp.concatenate([value[:N, :N], value[N:, :N]], axis=1)
    bottom = jnp.concatenate([value[:N, N:], value[N:, N:]], axis=1)
    return jnp.concatenate([top, bottom], axis=0)


def far_first(count):
    return sorted(range(count), key=lambda d: -min(d, count - d))


def kernel(n_sy, n_sx, positions, modes, offs_hbm, tile_hbm, probe_hbm, inten_hbm, tables_hbm,
           obj_out, prb_out,
           tile_in, probe_in, inten, tables, offs, near_offs,
           tile1, can_t, can_h, pack_l, pack_r, strip_l, strip_r,
           obj, back, pads, bright_pad, g_t, g_h, gp_l, gp_r, g_up, g_dn, f_l, f_r, l_sum,
           n_buf, n_pre, n_chip, n_rcv, n_part, nz_rcv,
           m_buf, m_pre, m_chip, m_rcv, m_part, mz_rcv, p_buf,
           side_send, side_recv, pair_send, pair_recv, all_send, all_recv, load_sem):
    sy = lax.axis_index("sy")
    sx = lax.axis_index("sx")
    depth = n_sx // Y_LO
    cores = 2
    n_yh = min(2, n_sy // cores)
    n_x, n_y = n_sy // (cores * n_yh), n_yh * Y_LO
    core = lax.rem(sy, cores)
    x = lax.div(sy, cores * n_yh)
    y_lo = lax.div(sx, depth)
    y = lax.rem(lax.div(sy, cores), n_yh) * Y_LO + y_lo
    z = lax.rem(sx, depth)
    x_at = [lax.rem(x + d, n_x) for d in range(n_x)]
    y_at = [lax.rem(y + d, n_y) for d in range(n_y)]
    y_row = [lax.div(v, Y_LO) * cores + core for v in y_at]
    y_col = [lax.rem(v, Y_LO) * depth + z for v in y_at]
    blocks = n_x * n_y
    rows = N // blocks
    me = x * n_y + y
    peers = [(dx, dy) for dx in far_first(n_x) for dy in far_first(n_y) if dx or dy]
    peers.sort(key=lambda p: -(min(p[0], n_x - p[0]) + min(p[1], n_y - p[1])))
    peer_index = [x_at[dx] * n_y + y_at[dy] for dx, dy in peers]
    peer_dev = [(x_at[dx] * (cores * n_yh) + y_row[dy], y_col[dy]) for dx, dy in peers]
    z_devs = [(sy, y_lo * depth + lax.rem(z + d, depth)) for d in far_first(depth) if d]
    partner = (sy + 1 - 2 * core, sx)

    def side_dev(step):
        dy, dx = step
        return (lax.rem(sy + (n_sy + dy), n_sy), lax.rem(sx + (n_sx + dx), n_sx))

    lane = lax.broadcasted_iota(jnp.int32, (HALF, N), 1)
    lane_n = lax.broadcasted_iota(jnp.int32, (N, N), 1)
    has_u = jnp.where(sy > 0, 1, 0)
    has_d = jnp.where(sy < n_sy - 1, 1, 0)
    has_l = jnp.where(sx > 0, 1, 0)
    has_r = jnp.where(sx < n_sx - 1, 1, 0)

    def remote(src, dst, send, recv, dev):
        return pltpu.make_async_remote_copy(
            src_ref=src, dst_ref=dst, send_sem=send, recv_sem=recv,
            device_id=dev, device_id_type=MESH)

    def await_bytes(ref, sem):
        pltpu.make_async_copy(ref, ref, sem).wait()

    def fetch_copies(it, tile):
        top, bottom, both = pl.ds(0, HALF), pl.ds(HALF, HALF), pl.ds(0, N)
        c_top, c_mid, c_low = pl.ds(0, HALF), pl.ds(HALF, N), pl.ds(N + HALF, HALF)
        plan = [
            (pack_l.at[it, top], strip_r.at[it, c_low]),
            (pack_l.at[it, bottom], strip_r.at[it, c_top]),
            (pack_r.at[it, top], strip_l.at[it, c_low]),
            (pack_r.at[it, bottom], strip_l.at[it, c_top]),
            (tile.at[:, top, :], can_t.at[it, :, c_low, :]),
            (tile.at[:, bottom, :], can_t.at[it, :, c_top, :]),
            (pack_l.at[it, both], strip_r.at[it, c_mid]),
            (pack_r.at[it, both], strip_l.at[it, c_mid]),
        ]
        return [remote(src, dst, side_send.at[0, it, i], side_recv.at[0, it, i], side_dev(SIDES[i]))
                for i, (src, dst) in enumerate(plan)]

    def strip_copies(kind, it, unit, vertical, src_l, src_r, left, right):
        top, mid, low = pl.ds(0, unit), pl.ds(unit, 2 * unit), pl.ds(3 * unit, unit)
        plan = [
            (src_l.at[top], right.at[top]),
            (src_l.at[low], right.at[low]),
            (src_r.at[top], left.at[top]),
            (src_r.at[low], left.at[low]),
        ] + vertical + [
            (src_l.at[mid], right.at[mid]),
            (src_r.at[mid], left.at[mid]),
        ]
        return [remote(src, dst, side_send.at[kind, it, i], side_recv.at[kind, it, i],
                       side_dev(SIDES[i])) for i, (src, dst) in enumerate(plan)]

    def grad_copies(it):
        vertical = [(g_t.at[it, :, pl.ds(0, HALF), :], g_up.at[it]),
                    (g_t.at[it, :, pl.ds(N + HALF, HALF), :], g_dn.at[it])]
        return strip_copies(1, it, HALF, vertical, gp_l.at[it], gp_r.at[it], f_l.at[it], f_r.at[it])

    def offset_copies():
        return [remote(offs, near_offs.at[i], side_send.at[2, 0, i], side_recv.at[2, 0, i],
                       side_dev(step)) for i, step in enumerate(SIDES)]

    def pack(it, tile):
        real, rolled = tile[0], pltpu.roll(tile[1], HALF, 1)
        pack_l[it] = jnp.where(lane_n < HALF, real, rolled)
        pack_r[it] = jnp.where(lane_n >= HALF, real, rolled)

    def column_mask(column):
        return (lane_n >= column - HALF) & (lane_n < column + HALF)

    def assemble(it, tile):
        keep_re = (lane >= HALF * (1 - has_r)) & (lane < HALF + HALF * has_l)
        keep_im = (lane >= HALF * (1 - has_l)) & (lane < HALF + HALF * has_r)
        keep_u = lane < N * has_u
        keep_d = lane < N * has_d
        for c in range(2):
            can_t[it, c, pl.ds(HALF, N), :] = tile[c]
            top = can_t[it, c, pl.ds(0, HALF), :]
            can_t[it, c, pl.ds(0, HALF), :] = jnp.where(keep_u, top, 0.0)
            low = can_t[it, c, pl.ds(N + HALF, HALF), :]
            can_t[it, c, pl.ds(N + HALF, HALF), :] = jnp.where(keep_d, low, 0.0)
        for part in range(4):
            at = pl.ds(part * HALF, HALF)
            left, right = strip_l[it, at], strip_r[it, at]
            real = jnp.where(keep_re, jnp.where(lane < HALF, right, left), 0.0)
            imag = jnp.where(keep_im, jnp.where(lane < HALF, left, right), 0.0)
            if part == 0:
                real, imag = jnp.where(keep_u, real, 0.0), jnp.where(keep_u, imag, 0.0)
            if part == 3:
                real, imag = jnp.where(keep_d, real, 0.0), jnp.where(keep_d, imag, 0.0)
            can_h[it, 0, at, :] = real
            can_h[it, 1, at, :] = pltpu.roll(imag, HALF, 1)

    def extract(it):
        total = None
        for j in range(positions):
            row, column = offs[0, 0, 0, j], offs[0, 0, 1, j]
            mask = column_mask(column)
            shift = lax.rem(HALF + N - column, N)
            for c in range(2):
                inner = can_t[it, c, pl.ds(row, N), :]
                outer = can_h[it, c, pl.ds(row, N), :]
                patch = pltpu.roll(jnp.where(mask, inner, outer), shift, 1)
                obj[j, c] = patch
                total = patch * patch if total is None else total + patch * patch
        m_buf[it] = total.reshape(blocks, rows, N)
        pair(0, it, m_buf.at[it], m_pre.at[it]).start()

    def place(channel, j, term):
        column = offs[0, 0, 1, j]
        mask = column_mask(column)
        turned = pltpu.roll(term, lax.rem(column + HALF, N), 1)
        pads[channel, 0, j, pl.ds(N, N), :] = jnp.where(mask, turned, 0.0)
        pads[channel, 1, j, pl.ds(N, N), :] = jnp.where(mask, 0.0, turned)

    def placed(channel, half):
        total = None
        for j in range(positions):
            window = pads[channel, half, j, pl.ds(N - offs[0, 0, 0, j], 2 * N), :]
            total = window if total is None else total + window
        return total

    def probe_part(it, k, c):
        if it == 0:
            return probe_in[k, c]
        return p_buf[it - 1, c, :, k].reshape(N, N)

    def light(it):
        bright = None
        for k in range(modes):
            for c in range(2):
                part = probe_part(it, k, c)
                bright = part * part if bright is None else bright + part * part
        bright_pad[pl.ds(N + HALF, N), :] = bright
        total = jnp.zeros((N, N), F32)
        for dy in (-1, 0, 1):
            for dx in (-1, 0, 1):
                inside = jnp.where((sy + dy >= 0) & (sy + dy < n_sy)
                                   & (sx + dx >= 0) & (sx + dx < n_sx), 0, 4 * N)
                table = near_offs.at[SIDES.index((-dy, -dx))] if dx or dy else offs

                def position(j, running, dy=dy, dx=dx, inside=inside, table=table):
                    column = table[0, 0, 1, j]
                    window = bright_pad[pl.ds(2 * N - N * dy - table[0, 0, 0, j], N), :]
                    turned = pltpu.roll(window, lax.rem(column + HALF, N), 1)
                    first = column + (N * dx - HALF) + inside
                    mask = (lane_n >= first) & (lane_n < first + N)
                    return running + jnp.where(mask, turned, 0.0)

                total = lax.fori_loop(0, positions, position, total)
        l_sum[it] = total

    def pair(what, it, src, dst):
        return remote(src, dst, pair_send.at[what, it], pair_recv.at[what, it], partner)

    def n_pair(it):
        return pair(1, it, n_buf.at[it, 1 - core], n_pre.at[it])

    def p_pair(it):
        return pair(2, it, p_buf.at[it, core], p_buf.at[it, core])

    def spread(what, it, source, target):
        for slot, (other, dev) in enumerate(zip(peer_index, peer_dev)):
            remote(source(other), target(slot), all_send.at[what, it], all_recv.at[what, it],
                   dev).start()

    def spread_z(what, it, source, target):
        for slot, dev in enumerate(z_devs):
            remote(source, target(slot), all_send.at[what, it], all_recv.at[what, it], dev).start()

    def send_m(it):
        pair(0, it, m_buf.at[it], m_pre.at[it]).wait_recv()
        m_chip[it] = m_buf[it] + m_pre[it]
        spread(0, it, lambda other: m_chip.at[it, other], lambda s: m_rcv.at[it, s])

    def send_mz(it):
        await_bytes(m_rcv.at[it], all_recv.at[0, it])
        m_part[it] = m_chip[it, me] + jnp.sum(m_rcv[it], axis=0)
        spread_z(1, it, m_part.at[it], lambda s: mz_rcv.at[it, s])

    def send_n(it):
        n_pair(it).wait_recv()
        n_chip[it] = n_buf[it, core] + n_pre[it]
        spread(2, it, lambda other: n_chip.at[it, other], lambda s: n_rcv.at[it, s])

    def send_nz(it):
        await_bytes(n_rcv.at[it], all_recv.at[2, it])
        n_part[it] = n_chip[it, me] + jnp.sum(n_rcv[it], axis=0)
        spread_z(3, it, n_part.at[it], lambda s: nz_rcv.at[it, s])

    def send_p(it):
        await_bytes(mz_rcv.at[it], all_recv.at[1, it])
        weight = m_part[it] + jnp.sum(mz_rcv[it], axis=0) + REGULAR
        await_bytes(nz_rcv.at[it], all_recv.at[3, it])
        numerator = n_part[it] + jnp.sum(nz_rcv[it], axis=0)
        for k in range(modes):
            if it == 0:
                old = probe_in[k, core, pl.ds(pl.multiple_of(me * rows, rows), rows), :]
            else:
                old = p_buf[it - 1, core, me, k]
            p_buf[it, core, me, k] = old - PROBE_STEP * numerator[k] / weight
        spread(4, it, lambda other: p_buf.at[it, core, me], lambda s: p_buf.at[it, core, me])

    def forward_p(it):
        await_bytes(p_buf.at[it, 0, pl.ds(0, blocks - 1)], all_recv.at[4, it])
        p_pair(it).start()

    def waves(it):
        def right(v, t):
            h, l = split(v)
            count = v.shape[0]
            both = dot(jnp.concatenate([h, l], axis=0), tables[t])
            return both[:count] + both[count:] + dot(h, tables[t + 1])

        def right_all(vs, t):
            outs = []
            for i in range(0, len(vs), 2):
                out = right(jnp.concatenate(vs[i:i + 2], axis=0), t)
                outs += [out[:2 * N], out[2 * N:]]
            return outs

        def left(t, v):
            h, l = split(v)
            both = dot(tables[t:t + 2].reshape(4 * N, 2 * N), h)
            return both[:2 * N] + both[2 * N:] + dot(tables[t], l)

        def exits(j):
            o_re, o_im = obj[j, 0], obj[j, 1]
            wave = []
            for k in range(modes):
                p_re, p_im = probe_part(it, k, 0), probe_part(it, k, 1)
                wave.append(jnp.concatenate(
                    [p_re * o_re - p_im * o_im, p_re * o_im + p_im * o_re], axis=1))
            return jnp.concatenate(wave, axis=0)

        def misfits(j, spec):
            power = spec[:N] * spec[:N] + spec[N:] * spec[N:]
            misfit = power[:, :N] + power[:, N:] - inten[j]
            wide = jnp.concatenate([misfit, misfit], axis=1)
            return jnp.concatenate([spec[:N] * wide, spec[N:] * wide], axis=0)

        members = range(positions)
        waves_in = [exits(j) for j in members]
        half = [swap_blocks(v) for v in right_all(waves_in, 0)]
        spec = [left(2, v) for v in half]
        dev = [misfits(j, v) for j, v in zip(members, spec)]
        half = [swap_blocks(left(0, v)) for v in dev]
        chis = right_all(half, 2)
        for k in range(modes):
            n_re, n_im = None, None
            for j, chi in zip(members, chis):
                o_re, o_im = obj[j, 0], obj[j, 1]
                c_re, c_im = chi[k * N:(k + 1) * N, :N], chi[k * N:(k + 1) * N, N:]
                back[j, k, 0] = c_re
                back[j, k, 1] = c_im
                a_re = o_re * c_re + o_im * c_im
                a_im = o_re * c_im - o_im * c_re
                n_re = a_re if n_re is None else n_re + a_re
                n_im = a_im if n_im is None else n_im + a_im
            n_buf[it, 0, :, k] = n_re.reshape(blocks, rows, N)
            n_buf[it, 1, :, k] = n_im.reshape(blocks, rows, N)
        n_pair(it).start()

    def gradient(it):
        for j in range(positions):
            g_re, g_im = None, None
            for k in range(modes):
                c_re, c_im = back[j, k, 0], back[j, k, 1]
                p_re, p_im = probe_part(it, k, 0), probe_part(it, k, 1)
                a_re = p_re * c_re + p_im * c_im
                a_im = p_re * c_im - p_im * c_re
                g_re = a_re if g_re is None else g_re + a_re
                g_im = a_im if g_im is None else g_im + a_im
            place(0, j, g_re)
            place(1, j, g_im)
        for c in range(2):
            g_t[it, c] = placed(c, 0)
            g_h[c] = placed(c, 1)
        wide = lax.broadcasted_iota(jnp.int32, (2 * N, N), 1)
        real, rolled = g_h[0], pltpu.roll(g_h[1], HALF, 1)
        gp_l[it] = jnp.where(wide >= HALF, real, rolled)
        gp_r[it] = jnp.where(wide < HALF, real, rolled)

    def strip_sum(strip):
        top, low = strip[pl.ds(0, HALF)], strip[pl.ds(N + HALF, HALF)]
        upper = strip[pl.ds(HALF, HALF)] + jnp.where(lane < N * has_u, low, 0.0)
        lower = strip[pl.ds(N, HALF)] + jnp.where(lane < N * has_d, top, 0.0)
        return jnp.concatenate([upper, lower], axis=0)

    def update(it, old, new):
        from_l, from_r = strip_sum(f_l.at[it]), strip_sum(f_r.at[it])
        weight = l_sum[it] + REGULAR
        for c in range(2):
            from_up = jnp.where(lane < N * has_u, g_dn[it, c], 0.0)
            from_down = jnp.where(lane < N * has_d, g_up[it, c], 0.0)
            total = g_t[it, c, pl.ds(HALF, N), :] + jnp.concatenate([from_up, from_down], axis=0)
            left = from_l if c == 0 else pltpu.roll(from_l, HALF, 1)
            right = from_r if c == 0 else pltpu.roll(from_r, HALF, 1)
            total += jnp.where(lane_n < HALF * has_l, left, 0.0)
            total += jnp.where(lane_n >= N - HALF * has_r, right, 0.0)
            new[c] = old[c] - OBJECT_STEP * total / weight

    def drain():
        for copy in offset_copies():
            copy.wait_send()
        for it in range(ITERS):
            for copy in fetch_copies(it, tiles[it]) + grad_copies(it):
                copy.wait_send()
            pair(0, it, m_buf.at[it], m_pre.at[it]).wait_send()
            n_pair(it).wait_send()
            await_bytes(m_rcv.at[it], all_send.at[0, it])
            await_bytes(mz_rcv.at[it], all_send.at[1, it])
            await_bytes(n_rcv.at[it], all_send.at[2, it])
            await_bytes(nz_rcv.at[it], all_send.at[3, it])
            if it + 1 < ITERS:
                p_pair(it).wait_send()
                await_bytes(p_buf.at[it, 0, pl.ds(0, blocks - 1)], all_send.at[4, it])

    barrier = pltpu.get_barrier_semaphore()
    greeted = peer_dev + z_devs + [side_dev(step) for step in SIDES] + [partner]
    for dev in greeted:
        pl.semaphore_signal(barrier, inc=1, device_id=dev, device_id_type=MESH)
    loads = [pltpu.make_async_copy(src, dst, load_sem.at[i]) for i, (src, dst) in enumerate(
        [(tile_hbm, tile_in), (offs_hbm, offs), (probe_hbm, probe_in), (tables_hbm, tables),
         (inten_hbm, inten)])]
    for load in loads:
        load.start()
    loads[0].wait()
    pack(0, tile_in)
    loads[1].wait()
    pl.semaphore_wait(barrier, len(greeted))

    for copy in fetch_copies(0, tile_in) + offset_copies():
        copy.start()
    for channel in range(2):
        for half in range(2):
            for j in range(positions):
                pads[channel, half, j, pl.ds(0, N), :] = jnp.zeros((N, N), F32)
                pads[channel, half, j, pl.ds(2 * N, N), :] = jnp.zeros((N, N), F32)
    bright_pad[...] = jnp.zeros_like(bright_pad)
    for load in loads[2:]:
        load.wait()

    tiles = [tile_in, tile1, obj_out]
    for it in range(ITERS):
        for copy in fetch_copies(it, tiles[it]):
            copy.wait_recv()
        assemble(it, tiles[it])
        extract(it)
        if it > 0:
            p_pair(it - 1).wait_recv()
        waves(it)
        send_m(it)
        gradient(it)
        if it + 1 < ITERS:
            for copy in grad_copies(it):
                copy.start()
        send_n(it)
        if it == 0:
            for copy in offset_copies():
                copy.wait_recv()
        light(it)
        send_mz(it)
        send_nz(it)
        if it + 1 == ITERS:
            for copy in grad_copies(it):
                copy.start()
        if it + 1 == ITERS:
            send_p(it)
        for copy in grad_copies(it):
            copy.wait_recv()
        update(it, tiles[it], tiles[it + 1])
        if it + 1 < ITERS:
            pack(it + 1, tiles[it + 1])
            for copy in fetch_copies(it + 1, tiles[it + 1]):
                copy.start()
            send_p(it)
        if it + 1 == ITERS:
            drain()
        forward_p(it)
    p_pair(ITERS - 1).wait_recv()
    for k in range(modes):
        for c in range(2):
            prb_out[k, c] = probe_part(ITERS, k, c)

    p_pair(ITERS - 1).wait_send()
    await_bytes(p_buf.at[ITERS - 1, 0, pl.ds(0, blocks - 1)], all_send.at[4, ITERS - 1])


def deliver(obj_in, prb_in, obj_out, prb_out, sem):
    copies = [pltpu.make_async_copy(obj_in, obj_out, sem.at[0]),
              pltpu.make_async_copy(prb_in, prb_out, sem.at[1])]
    for copy in copies:
        copy.start()
    for copy in copies:
        copy.wait()


def per_device(n_sy, n_sx, object_tile, probe_modes, scan_offsets, intensities):
    positions = scan_offsets.shape[2]
    modes = probe_modes.shape[0]
    depth = n_sx // Y_LO
    blocks = n_sy // 2 * Y_LO
    rows = N // blocks
    offsets = scan_offsets.transpose(0, 1, 3, 2)
    measured = intensities[0, 0]
    tables = jnp.asarray(dft_tables())
    vmem = functools.partial(pltpu.VMEM, dtype=F32)
    it = ITERS
    scratch = [
        vmem(object_tile.shape), vmem(probe_modes.shape), vmem(measured.shape),
        pltpu.VMEM(tables.shape, BF16), pltpu.SMEM(offsets.shape, jnp.int32),
        pltpu.SMEM((len(SIDES),) + offsets.shape, jnp.int32),
        vmem((2, N, N)), vmem((it, 2, 2 * N, N)), vmem((it, 2, 2 * N, N)),
        vmem((it, N, N)), vmem((it, N, N)), vmem((it, 2 * N, N)), vmem((it, 2 * N, N)),
        vmem((positions, 2, N, N)), vmem((positions, modes, 2, N, N)),
        vmem((2, 2, positions, 3 * N, N)), vmem((4 * N, N)),
        vmem((it, 2, 2 * N, N)), vmem((2, 2 * N, N)),
        vmem((it, 2 * N, N)), vmem((it, 2 * N, N)), vmem((it, 2, HALF, N)), vmem((it, 2, HALF, N)),
        vmem((it, 2 * N, N)), vmem((it, 2 * N, N)), vmem((it, N, N)),
        vmem((it, 2, blocks, modes, rows, N)), vmem((it, blocks, modes, rows, N)),
        vmem((it, blocks, modes, rows, N)), vmem((it, blocks - 1, modes, rows, N)),
        vmem((it, modes, rows, N)), vmem((it, depth - 1, modes, rows, N)),
        vmem((it, blocks, rows, N)), vmem((it, blocks, rows, N)), vmem((it, blocks, rows, N)),
        vmem((it, blocks - 1, rows, N)), vmem((it, rows, N)), vmem((it, depth - 1, rows, N)),
        vmem((it, 2, blocks, modes, rows, N)),
        pltpu.SemaphoreType.DMA((3, it, len(SIDES))), pltpu.SemaphoreType.DMA((3, it, len(SIDES))),
        pltpu.SemaphoreType.DMA((3, it)), pltpu.SemaphoreType.DMA((3, it)),
        pltpu.SemaphoreType.DMA((5, it)), pltpu.SemaphoreType.DMA((5, it)),
        pltpu.SemaphoreType.DMA((5,)),
    ]
    in_vmem = pl.BlockSpec(memory_space=pltpu.VMEM)
    results = pl.pallas_call(
        functools.partial(kernel, n_sy, n_sx, positions, modes),
        out_shape=(pltpu.VMEM(object_tile.shape, F32), pltpu.VMEM(probe_modes.shape, F32)),
        in_specs=[pl.BlockSpec(memory_space=pl.ANY)] * 5,
        out_specs=(in_vmem, in_vmem),
        scratch_shapes=scratch,
        compiler_params=pltpu.CompilerParams(collective_id=0, has_side_effects=True),
    )(offsets, object_tile, probe_modes, measured, tables)
    results = [pltpu.with_memory_space_constraint(r, pltpu.VMEM) for r in results]
    return pl.pallas_call(
        deliver,
        out_shape=(jax.ShapeDtypeStruct(object_tile.shape, F32),
                   jax.ShapeDtypeStruct(probe_modes.shape, F32)),
        in_specs=[in_vmem, in_vmem],
        out_specs=(pl.BlockSpec(memory_space=pl.ANY), pl.BlockSpec(memory_space=pl.ANY)),
        scratch_shapes=[pltpu.SemaphoreType.DMA((2,))],
    )(*results)


def solution(mesh):
    placed = (P(None, "sy", "sx"), P(), P("sy", "sx", None, None), P("sy", "sx", None, None, None))
    return jax.shard_map(
        functools.partial(per_device, mesh.shape["sy"], mesh.shape["sx"]),
        mesh=mesh,
        in_specs=placed,
        out_specs=(P(None, "sy", "sx"), P()),
        check_vma=False,
    )
```

```python
import functools

import numpy as np
import jax
import jax.numpy as jnp
from jax import lax
from jax.experimental import pallas as pl
from jax.experimental.pallas import tpu as pltpu
from jax.sharding import PartitionSpec as P

ITERS = 2
OBJECT_STEP = 0.5
PROBE_STEP = 2.0
REGULAR = 1.0
N = 128
HALF = 64
Y_LO = 2
MESH = pl.DeviceIdType.MESH
F32 = jnp.float32
BF16 = jnp.bfloat16

SIDES = [(-1, -1), (1, -1), (-1, 1), (1, 1), (-1, 0), (1, 0), (0, -1), (0, 1)]


def dft_tables():
    index = np.arange(N)
    angle = (index[:, None] * index[None, :] % N) * (2.0 * np.pi / N)
    scale = 1.0 / np.sqrt(float(N))
    cosine, sine = np.cos(angle) * scale, np.sin(angle) * scale
    forward = np.block([[cosine, -sine], [sine, cosine]])
    parts = []
    for matrix in (forward, forward.T):
        high = matrix.astype(np.float32).astype(BF16)
        low = (matrix - high.astype(np.float64)).astype(np.float32).astype(BF16)
        parts += [high, low]
    return np.stack(parts)


def split(value):
    high = value.astype(BF16)
    low = (value - high.astype(F32)).astype(BF16)
    return high, low


def dot(left, right):
    return jnp.dot(left, right, preferred_element_type=F32)


def swap_blocks(value):
    top = jnp.concatenate([value[:N, :N], value[N:, :N]], axis=1)
    bottom = jnp.concatenate([value[:N, N:], value[N:, N:]], axis=1)
    return jnp.concatenate([top, bottom], axis=0)


def far_first(count):
    return sorted(range(count), key=lambda d: -min(d, count - d))


def kernel(n_sy, n_sx, positions, modes, offs_hbm, tile_hbm, probe_hbm, inten_hbm, tables_hbm,
           obj_out, prb_out,
           tile_in, probe_in, inten, tables, offs, near_offs,
           tile1, can_t, can_h, pack_l, pack_r, strip_l, strip_r,
           obj, back, pads, bright_pad, g_t, g_h, gp_l, gp_r, g_up, g_dn, f_l, f_r, l_sum,
           n_buf, n_pre, n_chip, n_rcv, n_part, nz_rcv,
           m_buf, m_pre, m_chip, m_rcv, m_part, mz_rcv, p_buf,
           side_send, side_recv, pair_send, pair_recv, all_send, all_recv, probe_recv, load_sem):
    sy = lax.axis_index("sy")
    sx = lax.axis_index("sx")
    depth = n_sx // Y_LO
    cores = 2
    n_yh = min(2, n_sy // cores)
    n_x, n_y = n_sy // (cores * n_yh), n_yh * Y_LO
    core = lax.rem(sy, cores)
    x = lax.div(sy, cores * n_yh)
    y_lo = lax.div(sx, depth)
    y = lax.rem(lax.div(sy, cores), n_yh) * Y_LO + y_lo
    z = lax.rem(sx, depth)
    x_at = [lax.rem(x + d, n_x) for d in range(n_x)]
    y_at = [lax.rem(y + d, n_y) for d in range(n_y)]
    y_row = [lax.div(v, Y_LO) * cores + core for v in y_at]
    y_col = [lax.rem(v, Y_LO) * depth + z for v in y_at]
    blocks = n_x * n_y
    rows = N // blocks
    me = x * n_y + y
    peers = [(dx, dy) for dx in far_first(n_x) for dy in far_first(n_y) if dx or dy]
    peers.sort(key=lambda p: -(min(p[0], n_x - p[0]) + min(p[1], n_y - p[1])))
    peer_index = [x_at[dx] * n_y + y_at[dy] for dx, dy in peers]
    peer_dev = [(x_at[dx] * (cores * n_yh) + y_row[dy], y_col[dy]) for dx, dy in peers]
    from_index = [x_at[-dx] * n_y + y_at[-dy] for dx, dy in peers]
    z_devs = [(sy, y_lo * depth + lax.rem(z + d, depth)) for d in far_first(depth) if d]
    partner = (sy + 1 - 2 * core, sx)

    def side_dev(step):
        dy, dx = step
        return (lax.rem(sy + (n_sy + dy), n_sy), lax.rem(sx + (n_sx + dx), n_sx))

    lane = lax.broadcasted_iota(jnp.int32, (HALF, N), 1)
    lane_n = lax.broadcasted_iota(jnp.int32, (N, N), 1)
    has_u = jnp.where(sy > 0, 1, 0)
    has_d = jnp.where(sy < n_sy - 1, 1, 0)
    has_l = jnp.where(sx > 0, 1, 0)
    has_r = jnp.where(sx < n_sx - 1, 1, 0)

    def remote(src, dst, send, recv, dev):
        return pltpu.make_async_remote_copy(
            src_ref=src, dst_ref=dst, send_sem=send, recv_sem=recv,
            device_id=dev, device_id_type=MESH)

    def await_bytes(ref, sem):
        pltpu.make_async_copy(ref, ref, sem).wait()

    def fetch_copies(it, tile):
        top, bottom, both = pl.ds(0, HALF), pl.ds(HALF, HALF), pl.ds(0, N)
        c_top, c_mid, c_low = pl.ds(0, HALF), pl.ds(HALF, N), pl.ds(N + HALF, HALF)
        plan = [
            (pack_l.at[it, top], strip_r.at[it, c_low]),
            (pack_l.at[it, bottom], strip_r.at[it, c_top]),
            (pack_r.at[it, top], strip_l.at[it, c_low]),
            (pack_r.at[it, bottom], strip_l.at[it, c_top]),
            (tile.at[:, top, :], can_t.at[it, :, c_low, :]),
            (tile.at[:, bottom, :], can_t.at[it, :, c_top, :]),
            (pack_l.at[it, both], strip_r.at[it, c_mid]),
            (pack_r.at[it, both], strip_l.at[it, c_mid]),
        ]
        return [remote(src, dst, side_send.at[0, it, i], side_recv.at[0, it, i], side_dev(SIDES[i]))
                for i, (src, dst) in enumerate(plan)]

    def strip_copies(kind, it, unit, vertical, src_l, src_r, left, right):
        top, mid, low = pl.ds(0, unit), pl.ds(unit, 2 * unit), pl.ds(3 * unit, unit)
        plan = [
            (src_l.at[top], right.at[top]),
            (src_l.at[low], right.at[low]),
            (src_r.at[top], left.at[top]),
            (src_r.at[low], left.at[low]),
        ] + vertical + [
            (src_l.at[mid], right.at[mid]),
            (src_r.at[mid], left.at[mid]),
        ]
        return [remote(src, dst, side_send.at[kind, it, i], side_recv.at[kind, it, i],
                       side_dev(SIDES[i])) for i, (src, dst) in enumerate(plan)]

    def grad_copies(it):
        vertical = [(g_t.at[it, :, pl.ds(0, HALF), :], g_up.at[it]),
                    (g_t.at[it, :, pl.ds(N + HALF, HALF), :], g_dn.at[it])]
        return strip_copies(1, it, HALF, vertical, gp_l.at[it], gp_r.at[it], f_l.at[it], f_r.at[it])

    def offset_copies():
        return [remote(offs, near_offs.at[i], side_send.at[2, 0, i], side_recv.at[2, 0, i],
                       side_dev(step)) for i, step in enumerate(SIDES)]

    def pack(it, tile):
        real, rolled = tile[0], pltpu.roll(tile[1], HALF, 1)
        pack_l[it] = jnp.where(lane_n < HALF, real, rolled)
        pack_r[it] = jnp.where(lane_n >= HALF, real, rolled)

    def column_mask(column):
        return (lane_n >= column - HALF) & (lane_n < column + HALF)

    def assemble(it, tile):
        keep_re = (lane >= HALF * (1 - has_r)) & (lane < HALF + HALF * has_l)
        keep_im = (lane >= HALF * (1 - has_l)) & (lane < HALF + HALF * has_r)
        keep_u = lane < N * has_u
        keep_d = lane < N * has_d
        for c in range(2):
            can_t[it, c, pl.ds(HALF, N), :] = tile[c]
            top = can_t[it, c, pl.ds(0, HALF), :]
            can_t[it, c, pl.ds(0, HALF), :] = jnp.where(keep_u, top, 0.0)
            low = can_t[it, c, pl.ds(N + HALF, HALF), :]
            can_t[it, c, pl.ds(N + HALF, HALF), :] = jnp.where(keep_d, low, 0.0)
        for part in range(4):
            at = pl.ds(part * HALF, HALF)
            left, right = strip_l[it, at], strip_r[it, at]
            real = jnp.where(keep_re, jnp.where(lane < HALF, right, left), 0.0)
            imag = jnp.where(keep_im, jnp.where(lane < HALF, left, right), 0.0)
            if part == 0:
                real, imag = jnp.where(keep_u, real, 0.0), jnp.where(keep_u, imag, 0.0)
            if part == 3:
                real, imag = jnp.where(keep_d, real, 0.0), jnp.where(keep_d, imag, 0.0)
            can_h[it, 0, at, :] = real
            can_h[it, 1, at, :] = pltpu.roll(imag, HALF, 1)

    def extract(it):
        total = None
        for j in range(positions):
            row, column = offs[0, 0, 0, j], offs[0, 0, 1, j]
            mask = column_mask(column)
            shift = lax.rem(HALF + N - column, N)
            for c in range(2):
                inner = can_t[it, c, pl.ds(row, N), :]
                outer = can_h[it, c, pl.ds(row, N), :]
                patch = pltpu.roll(jnp.where(mask, inner, outer), shift, 1)
                obj[j, c] = patch
                total = patch * patch if total is None else total + patch * patch
        m_buf[it] = total.reshape(blocks, rows, N)
        pair(0, it, m_buf.at[it], m_pre.at[it]).start()

    def place(channel, j, term):
        column = offs[0, 0, 1, j]
        mask = column_mask(column)
        turned = pltpu.roll(term, lax.rem(column + HALF, N), 1)
        pads[channel, 0, j, pl.ds(N, N), :] = jnp.where(mask, turned, 0.0)
        pads[channel, 1, j, pl.ds(N, N), :] = jnp.where(mask, 0.0, turned)

    def placed(channel, half):
        total = None
        for j in range(positions):
            window = pads[channel, half, j, pl.ds(N - offs[0, 0, 0, j], 2 * N), :]
            total = window if total is None else total + window
        return total

    def probe_part(it, k, c):
        if it == 0:
            return probe_in[k, c]
        return p_buf[it - 1, c, :, k].reshape(N, N)

    def light(it):
        bright = None
        for k in range(modes):
            for c in range(2):
                part = probe_part(it, k, c)
                bright = part * part if bright is None else bright + part * part
        bright_pad[pl.ds(N + HALF, N), :] = bright
        total = jnp.zeros((N, N), F32)
        for dy in (-1, 0, 1):
            for dx in (-1, 0, 1):
                inside = jnp.where((sy + dy >= 0) & (sy + dy < n_sy)
                                   & (sx + dx >= 0) & (sx + dx < n_sx), 0, 4 * N)
                table = near_offs.at[SIDES.index((-dy, -dx))] if dx or dy else offs

                def position(j, running, dy=dy, dx=dx, inside=inside, table=table):
                    column = table[0, 0, 1, j]
                    window = bright_pad[pl.ds(2 * N - N * dy - table[0, 0, 0, j], N), :]
                    turned = pltpu.roll(window, lax.rem(column + HALF, N), 1)
                    first = column + (N * dx - HALF) + inside
                    mask = (lane_n >= first) & (lane_n < first + N)
                    return running + jnp.where(mask, turned, 0.0)

                total = lax.fori_loop(0, positions, position, total)
        l_sum[it] = total

    def pair(what, it, src, dst):
        return remote(src, dst, pair_send.at[what, it], pair_recv.at[what, it], partner)

    def n_pair(it):
        return pair(1, it, n_buf.at[it, 1 - core], n_pre.at[it])

    def forward(it, at):
        pair(2, it, p_buf.at[it, core, at], p_buf.at[it, core, at]).start()

    def wait_p(it):
        await_bytes(p_buf.at[it, 0], pair_recv.at[2, it])

    def spread(what, it, source, target):
        for slot, (other, dev) in enumerate(zip(peer_index, peer_dev)):
            remote(source(other), target(slot), all_send.at[what, it], all_recv.at[what, it],
                   dev).start()

    def spread_z(what, it, source, target):
        for slot, dev in enumerate(z_devs):
            remote(source, target(slot), all_send.at[what, it], all_recv.at[what, it], dev).start()

    def send_m(it):
        pair(0, it, m_buf.at[it], m_pre.at[it]).wait_recv()
        m_chip[it] = m_buf[it] + m_pre[it]
        spread(0, it, lambda other: m_chip.at[it, other], lambda s: m_rcv.at[it, s])

    def send_mz(it):
        await_bytes(m_rcv.at[it], all_recv.at[0, it])
        m_part[it] = m_chip[it, me] + jnp.sum(m_rcv[it], axis=0)
        spread_z(1, it, m_part.at[it], lambda s: mz_rcv.at[it, s])

    def send_n(it):
        n_pair(it).wait_recv()
        n_chip[it] = n_buf[it, core] + n_pre[it]
        spread(2, it, lambda other: n_chip.at[it, other], lambda s: n_rcv.at[it, s])

    def send_nz(it):
        await_bytes(n_rcv.at[it], all_recv.at[2, it])
        n_part[it] = n_chip[it, me] + jnp.sum(n_rcv[it], axis=0)
        spread_z(3, it, n_part.at[it], lambda s: nz_rcv.at[it, s])

    def send_p(it):
        await_bytes(mz_rcv.at[it], all_recv.at[1, it])
        weight = m_part[it] + jnp.sum(mz_rcv[it], axis=0) + REGULAR
        await_bytes(nz_rcv.at[it], all_recv.at[3, it])
        numerator = n_part[it] + jnp.sum(nz_rcv[it], axis=0)
        for k in range(modes):
            if it == 0:
                old = probe_in[k, core, pl.ds(pl.multiple_of(me * rows, rows), rows), :]
            else:
                old = p_buf[it - 1, core, me, k]
            p_buf[it, core, me, k] = old - PROBE_STEP * numerator[k] / weight
        mine = p_buf.at[it, core, me]
        for slot, dev in enumerate(peer_dev):
            remote(mine, mine, all_send.at[4, it], probe_recv.at[it, slot], dev).start()
        forward(it, me)

    def forward_p(it):
        for slot in reversed(range(blocks - 1)):
            await_bytes(p_buf.at[it, core, from_index[slot]], probe_recv.at[it, slot])
            forward(it, from_index[slot])

    def waves(it):
        def right(v, t):
            h, l = split(v)
            count = v.shape[0]
            both = dot(jnp.concatenate([h, l], axis=0), tables[t])
            return both[:count] + both[count:] + dot(h, tables[t + 1])

        def right_all(vs, t):
            outs = []
            for i in range(0, len(vs), 2):
                out = right(jnp.concatenate(vs[i:i + 2], axis=0), t)
                outs += [out[:2 * N], out[2 * N:]]
            return outs

        def left(t, v):
            h, l = split(v)
            both = dot(tables[t:t + 2].reshape(4 * N, 2 * N), h)
            return both[:2 * N] + both[2 * N:] + dot(tables[t], l)

        def exits(j):
            o_re, o_im = obj[j, 0], obj[j, 1]
            wave = []
            for k in range(modes):
                p_re, p_im = probe_part(it, k, 0), probe_part(it, k, 1)
                wave.append(jnp.concatenate(
                    [p_re * o_re - p_im * o_im, p_re * o_im + p_im * o_re], axis=1))
            return jnp.concatenate(wave, axis=0)

        def misfits(j, spec):
            power = spec[:N] * spec[:N] + spec[N:] * spec[N:]
            misfit = power[:, :N] + power[:, N:] - inten[j]
            wide = jnp.concatenate([misfit, misfit], axis=1)
            return jnp.concatenate([spec[:N] * wide, spec[N:] * wide], axis=0)

        members = range(positions)
        waves_in = [exits(j) for j in members]
        half = [swap_blocks(v) for v in right_all(waves_in, 0)]
        spec = [left(2, v) for v in half]
        dev = [misfits(j, v) for j, v in zip(members, spec)]
        half = [swap_blocks(left(0, v)) for v in dev]
        chis = right_all(half, 2)
        for k in range(modes):
            n_re, n_im = None, None
            for j, chi in zip(members, chis):
                o_re, o_im = obj[j, 0], obj[j, 1]
                c_re, c_im = chi[k * N:(k + 1) * N, :N], chi[k * N:(k + 1) * N, N:]
                back[j, k, 0] = c_re
                back[j, k, 1] = c_im
                a_re = o_re * c_re + o_im * c_im
                a_im = o_re * c_im - o_im * c_re
                n_re = a_re if n_re is None else n_re + a_re
                n_im = a_im if n_im is None else n_im + a_im
            n_buf[it, 0, :, k] = n_re.reshape(blocks, rows, N)
            n_buf[it, 1, :, k] = n_im.reshape(blocks, rows, N)
        n_pair(it).start()

    def gradient(it):
        for j in range(positions):
            g_re, g_im = None, None
            for k in range(modes):
                c_re, c_im = back[j, k, 0], back[j, k, 1]
                p_re, p_im = probe_part(it, k, 0), probe_part(it, k, 1)
                a_re = p_re * c_re + p_im * c_im
                a_im = p_re * c_im - p_im * c_re
                g_re = a_re if g_re is None else g_re + a_re
                g_im = a_im if g_im is None else g_im + a_im
            place(0, j, g_re)
            place(1, j, g_im)
        for c in range(2):
            g_t[it, c] = placed(c, 0)
            g_h[c] = placed(c, 1)
        wide = lax.broadcasted_iota(jnp.int32, (2 * N, N), 1)
        real, rolled = g_h[0], pltpu.roll(g_h[1], HALF, 1)
        gp_l[it] = jnp.where(wide >= HALF, real, rolled)
        gp_r[it] = jnp.where(wide < HALF, real, rolled)

    def strip_sum(strip):
        top, low = strip[pl.ds(0, HALF)], strip[pl.ds(N + HALF, HALF)]
        upper = strip[pl.ds(HALF, HALF)] + jnp.where(lane < N * has_u, low, 0.0)
        lower = strip[pl.ds(N, HALF)] + jnp.where(lane < N * has_d, top, 0.0)
        return jnp.concatenate([upper, lower], axis=0)

    def update(it, old, new):
        from_l, from_r = strip_sum(f_l.at[it]), strip_sum(f_r.at[it])
        weight = l_sum[it] + REGULAR
        for c in range(2):
            from_up = jnp.where(lane < N * has_u, g_dn[it, c], 0.0)
            from_down = jnp.where(lane < N * has_d, g_up[it, c], 0.0)
            total = g_t[it, c, pl.ds(HALF, N), :] + jnp.concatenate([from_up, from_down], axis=0)
            left = from_l if c == 0 else pltpu.roll(from_l, HALF, 1)
            right = from_r if c == 0 else pltpu.roll(from_r, HALF, 1)
            total += jnp.where(lane_n < HALF * has_l, left, 0.0)
            total += jnp.where(lane_n >= N - HALF * has_r, right, 0.0)
            new[c] = old[c] - OBJECT_STEP * total / weight

    def drain():
        for copy in offset_copies():
            copy.wait_send()
        for it in range(ITERS):
            for copy in fetch_copies(it, tiles[it]) + grad_copies(it):
                copy.wait_send()
            pair(0, it, m_buf.at[it], m_pre.at[it]).wait_send()
            n_pair(it).wait_send()
            await_bytes(m_rcv.at[it], all_send.at[0, it])
            await_bytes(mz_rcv.at[it], all_send.at[1, it])
            await_bytes(n_rcv.at[it], all_send.at[2, it])
            await_bytes(nz_rcv.at[it], all_send.at[3, it])
            if it + 1 < ITERS:
                await_bytes(p_buf.at[it, 0], pair_send.at[2, it])
                await_bytes(p_buf.at[it, 0, pl.ds(0, blocks - 1)], all_send.at[4, it])

    barrier = pltpu.get_barrier_semaphore()
    greeted = [side_dev(step) for step in SIDES[:4]] + peer_dev + z_devs
    greeted += [side_dev(step) for step in SIDES[4:]] + [partner]
    for dev in greeted:
        pl.semaphore_signal(barrier, inc=1, device_id=dev, device_id_type=MESH)
    loads = [pltpu.make_async_copy(src, dst, load_sem.at[i]) for i, (src, dst) in enumerate(
        [(tile_hbm, tile_in), (offs_hbm, offs), (probe_hbm, probe_in), (tables_hbm, tables),
         (inten_hbm, inten)])]
    for load in loads:
        load.start()
    loads[0].wait()
    pack(0, tile_in)
    loads[1].wait()
    pl.semaphore_wait(barrier, len(greeted))

    for copy in fetch_copies(0, tile_in) + offset_copies():
        copy.start()
    for channel in range(2):
        for half in range(2):
            for j in range(positions):
                pads[channel, half, j, pl.ds(0, N), :] = jnp.zeros((N, N), F32)
                pads[channel, half, j, pl.ds(2 * N, N), :] = jnp.zeros((N, N), F32)
    bright_pad[...] = jnp.zeros_like(bright_pad)
    for load in loads[2:]:
        load.wait()

    tiles = [tile_in, tile1, obj_out]
    for it in range(ITERS):
        for copy in fetch_copies(it, tiles[it]):
            copy.wait_recv()
        assemble(it, tiles[it])
        extract(it)
        if it > 0:
            wait_p(it - 1)
        waves(it)
        send_m(it)
        gradient(it)
        if it + 1 < ITERS:
            for copy in grad_copies(it):
                copy.start()
        send_n(it)
        if it == 0:
            for copy in offset_copies():
                copy.wait_recv()
        light(it)
        send_mz(it)
        send_nz(it)
        if it + 1 == ITERS:
            for copy in grad_copies(it):
                copy.start()
        if it + 1 == ITERS:
            send_p(it)
        for copy in grad_copies(it):
            copy.wait_recv()
        update(it, tiles[it], tiles[it + 1])
        if it + 1 < ITERS:
            pack(it + 1, tiles[it + 1])
            for copy in fetch_copies(it + 1, tiles[it + 1]):
                copy.start()
            send_p(it)
        if it + 1 == ITERS:
            drain()
        forward_p(it)
    wait_p(ITERS - 1)
    for k in range(modes):
        for c in range(2):
            prb_out[k, c] = probe_part(ITERS, k, c)

    await_bytes(p_buf.at[ITERS - 1, 0], pair_send.at[2, ITERS - 1])
    await_bytes(p_buf.at[ITERS - 1, 0, pl.ds(0, blocks - 1)], all_send.at[4, ITERS - 1])


def deliver(obj_in, prb_in, obj_out, prb_out, sem):
    copies = [pltpu.make_async_copy(obj_in, obj_out, sem.at[0]),
              pltpu.make_async_copy(prb_in, prb_out, sem.at[1])]
    for copy in copies:
        copy.start()
    for copy in copies:
        copy.wait()


def per_device(n_sy, n_sx, object_tile, probe_modes, scan_offsets, intensities):
    positions = scan_offsets.shape[2]
    modes = probe_modes.shape[0]
    depth = n_sx // Y_LO
    blocks = n_sy // 2 * Y_LO
    rows = N // blocks
    offsets = scan_offsets.transpose(0, 1, 3, 2)
    measured = intensities[0, 0]
    tables = jnp.asarray(dft_tables())
    vmem = functools.partial(pltpu.VMEM, dtype=F32)
    it = ITERS
    scratch = [
        vmem(object_tile.shape), vmem(probe_modes.shape), vmem(measured.shape),
        pltpu.VMEM(tables.shape, BF16), pltpu.SMEM(offsets.shape, jnp.int32),
        pltpu.SMEM((len(SIDES),) + offsets.shape, jnp.int32),
        vmem((2, N, N)), vmem((it, 2, 2 * N, N)), vmem((it, 2, 2 * N, N)),
        vmem((it, N, N)), vmem((it, N, N)), vmem((it, 2 * N, N)), vmem((it, 2 * N, N)),
        vmem((positions, 2, N, N)), vmem((positions, modes, 2, N, N)),
        vmem((2, 2, positions, 3 * N, N)), vmem((4 * N, N)),
        vmem((it, 2, 2 * N, N)), vmem((2, 2 * N, N)),
        vmem((it, 2 * N, N)), vmem((it, 2 * N, N)), vmem((it, 2, HALF, N)), vmem((it, 2, HALF, N)),
        vmem((it, 2 * N, N)), vmem((it, 2 * N, N)), vmem((it, N, N)),
        vmem((it, 2, blocks, modes, rows, N)), vmem((it, blocks, modes, rows, N)),
        vmem((it, blocks, modes, rows, N)), vmem((it, blocks - 1, modes, rows, N)),
        vmem((it, modes, rows, N)), vmem((it, depth - 1, modes, rows, N)),
        vmem((it, blocks, rows, N)), vmem((it, blocks, rows, N)), vmem((it, blocks, rows, N)),
        vmem((it, blocks - 1, rows, N)), vmem((it, rows, N)), vmem((it, depth - 1, rows, N)),
        vmem((it, 2, blocks, modes, rows, N)),
        pltpu.SemaphoreType.DMA((3, it, len(SIDES))), pltpu.SemaphoreType.DMA((3, it, len(SIDES))),
        pltpu.SemaphoreType.DMA((3, it)), pltpu.SemaphoreType.DMA((3, it)),
        pltpu.SemaphoreType.DMA((5, it)), pltpu.SemaphoreType.DMA((4, it)),
        pltpu.SemaphoreType.DMA((it, blocks - 1)),
        pltpu.SemaphoreType.DMA((5,)),
    ]
    in_vmem = pl.BlockSpec(memory_space=pltpu.VMEM)
    results = pl.pallas_call(
        functools.partial(kernel, n_sy, n_sx, positions, modes),
        out_shape=(pltpu.VMEM(object_tile.shape, F32), pltpu.VMEM(probe_modes.shape, F32)),
        in_specs=[pl.BlockSpec(memory_space=pl.ANY)] * 5,
        out_specs=(in_vmem, in_vmem),
        scratch_shapes=scratch,
        compiler_params=pltpu.CompilerParams(collective_id=0, has_side_effects=True),
    )(offsets, object_tile, probe_modes, measured, tables)
    results = [pltpu.with_memory_space_constraint(r, pltpu.VMEM) for r in results]
    return pl.pallas_call(
        deliver,
        out_shape=(jax.ShapeDtypeStruct(object_tile.shape, F32),
                   jax.ShapeDtypeStruct(probe_modes.shape, F32)),
        in_specs=[in_vmem, in_vmem],
        out_specs=(pl.BlockSpec(memory_space=pl.ANY), pl.BlockSpec(memory_space=pl.ANY)),
        scratch_shapes=[pltpu.SemaphoreType.DMA((2,))],
    )(*results)


def solution(mesh):
    placed = (P(None, "sy", "sx"), P(), P("sy", "sx", None, None), P("sy", "sx", None, None, None))
    return jax.shard_map(
        functools.partial(per_device, mesh.shape["sy"], mesh.shape["sx"]),
        mesh=mesh,
        in_specs=placed,
        out_specs=(P(None, "sy", "sx"), P()),
        check_vma=False,
    )
```

```python
import functools

import numpy as np
import jax
import jax.numpy as jnp
from jax import lax
from jax.experimental import pallas as pl
from jax.experimental.pallas import tpu as pltpu
from jax.sharding import PartitionSpec as P

ITERS = 2
OBJECT_STEP = 0.5
PROBE_STEP = 2.0
REGULAR = 1.0
N = 128
HALF = 64
Y_LO = 2
MESH = pl.DeviceIdType.MESH
F32 = jnp.float32
BF16 = jnp.bfloat16

SIDES = [(-1, -1), (1, -1), (-1, 1), (1, 1), (-1, 0), (1, 0), (0, -1), (0, 1)]


def dft_tables():
    index = np.arange(N)
    angle = (index[:, None] * index[None, :] % N) * (2.0 * np.pi / N)
    scale = 1.0 / np.sqrt(float(N))
    cosine, sine = np.cos(angle) * scale, np.sin(angle) * scale
    forward = np.block([[cosine, -sine], [sine, cosine]])
    parts = []
    for matrix in (forward, forward.T):
        high = matrix.astype(np.float32).astype(BF16)
        low = (matrix - high.astype(np.float64)).astype(np.float32).astype(BF16)
        parts += [high, low]
    return np.stack(parts)


def split(value):
    high = value.astype(BF16)
    low = (value - high.astype(F32)).astype(BF16)
    return high, low


def dot(left, right):
    return jnp.dot(left, right, preferred_element_type=F32)


def swap_blocks(value):
    top = jnp.concatenate([value[:N, :N], value[N:, :N]], axis=1)
    bottom = jnp.concatenate([value[:N, N:], value[N:, N:]], axis=1)
    return jnp.concatenate([top, bottom], axis=0)


def far_first(count):
    return sorted(range(count), key=lambda d: -min(d, count - d))


def kernel(n_sy, n_sx, positions, modes, offs_hbm, tile_hbm, probe_hbm, inten_hbm, tables_hbm,
           obj_out, prb_out,
           tile_in, probe_in, inten, tables, offs, near_offs,
           tile1, can_t, can_h, pack_l, pack_r, strip_l, strip_r,
           obj, back, pads, bright_pad, g_t, g_h, gp_l, gp_r, g_up, g_dn, f_l, f_r, l_sum,
           n_buf, n_pre, n_chip, n_rcv, n_part, nz_rcv,
           m_buf, m_pre, m_chip, m_rcv, m_part, mz_rcv, p_buf,
           side_send, side_recv, pair_send, pair_recv, all_send, all_recv, probe_recv, load_sem):
    sy = lax.axis_index("sy")
    sx = lax.axis_index("sx")
    depth = n_sx // Y_LO
    cores = 2
    n_yh = min(2, n_sy // cores)
    n_x, n_y = n_sy // (cores * n_yh), n_yh * Y_LO
    core = lax.rem(sy, cores)
    x = lax.div(sy, cores * n_yh)
    y_lo = lax.div(sx, depth)
    y = lax.rem(lax.div(sy, cores), n_yh) * Y_LO + y_lo
    z = lax.rem(sx, depth)
    x_at = [lax.rem(x + d, n_x) for d in range(n_x)]
    y_at = [lax.rem(y + d, n_y) for d in range(n_y)]
    y_row = [lax.div(v, Y_LO) * cores + core for v in y_at]
    y_col = [lax.rem(v, Y_LO) * depth + z for v in y_at]
    blocks = n_x * n_y
    rows = N // blocks
    me = x * n_y + y
    peers = [(dx, dy) for dx in far_first(n_x) for dy in far_first(n_y) if dx or dy]
    peers.sort(key=lambda p: -(min(p[0], n_x - p[0]) + min(p[1], n_y - p[1])))
    peer_index = [x_at[dx] * n_y + y_at[dy] for dx, dy in peers]
    peer_dev = [(x_at[dx] * (cores * n_yh) + y_row[dy], y_col[dy]) for dx, dy in peers]
    from_index = [x_at[-dx] * n_y + y_at[-dy] for dx, dy in peers]
    z_devs = [(sy, y_lo * depth + lax.rem(z + d, depth)) for d in far_first(depth) if d]
    partner = (sy + 1 - 2 * core, sx)

    def side_dev(step):
        dy, dx = step
        return (lax.rem(sy + (n_sy + dy), n_sy), lax.rem(sx + (n_sx + dx), n_sx))

    lane = lax.broadcasted_iota(jnp.int32, (HALF, N), 1)
    lane_n = lax.broadcasted_iota(jnp.int32, (N, N), 1)
    has_u = jnp.where(sy > 0, 1, 0)
    has_d = jnp.where(sy < n_sy - 1, 1, 0)
    has_l = jnp.where(sx > 0, 1, 0)
    has_r = jnp.where(sx < n_sx - 1, 1, 0)

    def remote(src, dst, send, recv, dev):
        return pltpu.make_async_remote_copy(
            src_ref=src, dst_ref=dst, send_sem=send, recv_sem=recv,
            device_id=dev, device_id_type=MESH)

    def await_bytes(ref, sem):
        pltpu.make_async_copy(ref, ref, sem).wait()

    def fetch_copies(it, tile):
        top, bottom, both = pl.ds(0, HALF), pl.ds(HALF, HALF), pl.ds(0, N)
        c_top, c_mid, c_low = pl.ds(0, HALF), pl.ds(HALF, N), pl.ds(N + HALF, HALF)
        plan = [
            (pack_l.at[it, top], strip_r.at[it, c_low]),
            (pack_l.at[it, bottom], strip_r.at[it, c_top]),
            (pack_r.at[it, top], strip_l.at[it, c_low]),
            (pack_r.at[it, bottom], strip_l.at[it, c_top]),
            (tile.at[:, top, :], can_t.at[it, :, c_low, :]),
            (tile.at[:, bottom, :], can_t.at[it, :, c_top, :]),
            (pack_l.at[it, both], strip_r.at[it, c_mid]),
            (pack_r.at[it, both], strip_l.at[it, c_mid]),
        ]
        return [remote(src, dst, side_send.at[0, it, i], side_recv.at[0, it, i], side_dev(SIDES[i]))
                for i, (src, dst) in enumerate(plan)]

    def strip_copies(kind, it, unit, vertical, src_l, src_r, left, right):
        top, mid, low = pl.ds(0, unit), pl.ds(unit, 2 * unit), pl.ds(3 * unit, unit)
        plan = [
            (src_l.at[top], right.at[top]),
            (src_l.at[low], right.at[low]),
            (src_r.at[top], left.at[top]),
            (src_r.at[low], left.at[low]),
        ] + vertical + [
            (src_l.at[mid], right.at[mid]),
            (src_r.at[mid], left.at[mid]),
        ]
        return [remote(src, dst, side_send.at[kind, it, i], side_recv.at[kind, it, i],
                       side_dev(SIDES[i])) for i, (src, dst) in enumerate(plan)]

    def grad_copies(it):
        vertical = [(g_t.at[it, :, pl.ds(0, HALF), :], g_up.at[it]),
                    (g_t.at[it, :, pl.ds(N + HALF, HALF), :], g_dn.at[it])]
        return strip_copies(1, it, HALF, vertical, gp_l.at[it], gp_r.at[it], f_l.at[it], f_r.at[it])

    def offset_copies():
        return [remote(offs, near_offs.at[i], side_send.at[2, 0, i], side_recv.at[2, 0, i],
                       side_dev(step)) for i, step in enumerate(SIDES)]

    def pack(it, tile):
        real, rolled = tile[0], pltpu.roll(tile[1], HALF, 1)
        pack_l[it] = jnp.where(lane_n < HALF, real, rolled)
        pack_r[it] = jnp.where(lane_n >= HALF, real, rolled)

    def column_mask(column):
        return (lane_n >= column - HALF) & (lane_n < column + HALF)

    def assemble(it, tile):
        keep_re = (lane >= HALF * (1 - has_r)) & (lane < HALF + HALF * has_l)
        keep_im = (lane >= HALF * (1 - has_l)) & (lane < HALF + HALF * has_r)
        keep_u = lane < N * has_u
        keep_d = lane < N * has_d
        for c in range(2):
            can_t[it, c, pl.ds(HALF, N), :] = tile[c]
            top = can_t[it, c, pl.ds(0, HALF), :]
            can_t[it, c, pl.ds(0, HALF), :] = jnp.where(keep_u, top, 0.0)
            low = can_t[it, c, pl.ds(N + HALF, HALF), :]
            can_t[it, c, pl.ds(N + HALF, HALF), :] = jnp.where(keep_d, low, 0.0)
        for part in range(4):
            at = pl.ds(part * HALF, HALF)
            left, right = strip_l[it, at], strip_r[it, at]
            real = jnp.where(keep_re, jnp.where(lane < HALF, right, left), 0.0)
            imag = jnp.where(keep_im, jnp.where(lane < HALF, left, right), 0.0)
            if part == 0:
                real, imag = jnp.where(keep_u, real, 0.0), jnp.where(keep_u, imag, 0.0)
            if part == 3:
                real, imag = jnp.where(keep_d, real, 0.0), jnp.where(keep_d, imag, 0.0)
            can_h[it, 0, at, :] = real
            can_h[it, 1, at, :] = pltpu.roll(imag, HALF, 1)

    def extract(it):
        total = None
        for j in range(positions):
            row, column = offs[0, 0, 0, j], offs[0, 0, 1, j]
            mask = column_mask(column)
            shift = lax.rem(HALF + N - column, N)
            for c in range(2):
                inner = can_t[it, c, pl.ds(row, N), :]
                outer = can_h[it, c, pl.ds(row, N), :]
                patch = pltpu.roll(jnp.where(mask, inner, outer), shift, 1)
                obj[j, c] = patch
                total = patch * patch if total is None else total + patch * patch
        m_buf[it] = total.reshape(blocks, rows, N)
        pair(0, it, m_buf.at[it], m_pre.at[it]).start()

    def place(channel, j, term):
        column = offs[0, 0, 1, j]
        mask = column_mask(column)
        turned = pltpu.roll(term, lax.rem(column + HALF, N), 1)
        pads[channel, 0, j, pl.ds(N, N), :] = jnp.where(mask, turned, 0.0)
        pads[channel, 1, j, pl.ds(N, N), :] = jnp.where(mask, 0.0, turned)

    def placed(channel, half):
        total = None
        for j in range(positions):
            window = pads[channel, half, j, pl.ds(N - offs[0, 0, 0, j], 2 * N), :]
            total = window if total is None else total + window
        return total

    def probe_part(it, k, c):
        if it == 0:
            return probe_in[k, c]
        return p_buf[it - 1, c, :, k].reshape(N, N)

    def light(it):
        bright = None
        for k in range(modes):
            for c in range(2):
                part = probe_part(it, k, c)
                bright = part * part if bright is None else bright + part * part
        bright_pad[pl.ds(N + HALF, N), :] = bright
        total = jnp.zeros((N, N), F32)
        for dy in (-1, 0, 1):
            for dx in (-1, 0, 1):
                inside = jnp.where((sy + dy >= 0) & (sy + dy < n_sy)
                                   & (sx + dx >= 0) & (sx + dx < n_sx), 0, 4 * N)
                table = near_offs.at[SIDES.index((-dy, -dx))] if dx or dy else offs

                def position(j, running, dy=dy, dx=dx, inside=inside, table=table):
                    column = table[0, 0, 1, j]
                    window = bright_pad[pl.ds(2 * N - N * dy - table[0, 0, 0, j], N), :]
                    turned = pltpu.roll(window, lax.rem(column + HALF, N), 1)
                    first = column + (N * dx - HALF) + inside
                    mask = (lane_n >= first) & (lane_n < first + N)
                    return running + jnp.where(mask, turned, 0.0)

                total = lax.fori_loop(0, positions, position, total)
        l_sum[it] = total

    def pair(what, it, src, dst):
        return remote(src, dst, pair_send.at[what, it], pair_recv.at[what, it], partner)

    def n_pair(it):
        return pair(1, it, n_buf.at[it, 1 - core], n_pre.at[it])

    def forward(it, at):
        pair(2, it, p_buf.at[it, core, at], p_buf.at[it, core, at]).start()

    def wait_p(it):
        await_bytes(p_buf.at[it, 0], pair_recv.at[2, it])

    def spread(what, it, source, target):
        for slot, (other, dev) in enumerate(zip(peer_index, peer_dev)):
            remote(source(other), target(slot), all_send.at[what, it], all_recv.at[what, it],
                   dev).start()

    def spread_z(what, it, source, target):
        for slot, dev in enumerate(z_devs):
            remote(source, target(slot), all_send.at[what, it], all_recv.at[what, it], dev).start()

    def send_m(it):
        pair(0, it, m_buf.at[it], m_pre.at[it]).wait_recv()
        m_chip[it] = m_buf[it] + m_pre[it]
        spread(0, it, lambda other: m_chip.at[it, other], lambda s: m_rcv.at[it, s])

    def send_mz(it):
        await_bytes(m_rcv.at[it], all_recv.at[0, it])
        m_part[it] = m_chip[it, me] + jnp.sum(m_rcv[it], axis=0)
        spread_z(1, it, m_part.at[it], lambda s: mz_rcv.at[it, s])

    def send_n(it):
        n_pair(it).wait_recv()
        n_chip[it] = n_buf[it, core] + n_pre[it]
        spread(2, it, lambda other: n_chip.at[it, other], lambda s: n_rcv.at[it, s])

    def send_nz(it):
        await_bytes(n_rcv.at[it], all_recv.at[2, it])
        n_part[it] = n_chip[it, me] + jnp.sum(n_rcv[it], axis=0)
        spread_z(3, it, n_part.at[it], lambda s: nz_rcv.at[it, s])

    def send_p(it):
        await_bytes(mz_rcv.at[it], all_recv.at[1, it])
        weight = m_part[it] + jnp.sum(mz_rcv[it], axis=0) + REGULAR
        await_bytes(nz_rcv.at[it], all_recv.at[3, it])
        numerator = n_part[it] + jnp.sum(nz_rcv[it], axis=0)
        for k in range(modes):
            if it == 0:
                old = probe_in[k, core, pl.ds(pl.multiple_of(me * rows, rows), rows), :]
            else:
                old = p_buf[it - 1, core, me, k]
            p_buf[it, core, me, k] = old - PROBE_STEP * numerator[k] / weight
        mine = p_buf.at[it, core, me]
        for slot, dev in enumerate(peer_dev):
            remote(mine, mine, all_send.at[4, it], probe_recv.at[it, slot], dev).start()
        forward(it, me)

    def forward_p(it):
        for slot in reversed(range(blocks - 1)):
            await_bytes(p_buf.at[it, core, from_index[slot]], probe_recv.at[it, slot])
            forward(it, from_index[slot])

    def waves(it):
        def right(v, t):
            h, l = split(v)
            count = v.shape[0]
            both = dot(jnp.concatenate([h, l], axis=0), tables[t])
            return both[:count] + both[count:] + dot(h, tables[t + 1])

        def right_all(vs, t):
            return [right(v, t) for v in vs]

        def left(t, v):
            h, l = split(v)
            both = dot(tables[t:t + 2].reshape(4 * N, 2 * N), h)
            return both[:2 * N] + both[2 * N:] + dot(tables[t], l)

        def exits(j):
            o_re, o_im = obj[j, 0], obj[j, 1]
            wave = []
            for k in range(modes):
                p_re, p_im = probe_part(it, k, 0), probe_part(it, k, 1)
                wave.append(jnp.concatenate(
                    [p_re * o_re - p_im * o_im, p_re * o_im + p_im * o_re], axis=1))
            return jnp.concatenate(wave, axis=0)

        def misfits(j, spec):
            power = spec[:N] * spec[:N] + spec[N:] * spec[N:]
            misfit = power[:, :N] + power[:, N:] - inten[j]
            wide = jnp.concatenate([misfit, misfit], axis=1)
            return jnp.concatenate([spec[:N] * wide, spec[N:] * wide], axis=0)

        members = range(positions)
        waves_in = [exits(j) for j in members]
        half = [swap_blocks(v) for v in right_all(waves_in, 0)]
        spec = [left(2, v) for v in half]
        dev = [misfits(j, v) for j, v in zip(members, spec)]
        half = [swap_blocks(left(0, v)) for v in dev]
        chis = right_all(half, 2)
        for k in range(modes):
            n_re, n_im = None, None
            for j, chi in zip(members, chis):
                o_re, o_im = obj[j, 0], obj[j, 1]
                c_re, c_im = chi[k * N:(k + 1) * N, :N], chi[k * N:(k + 1) * N, N:]
                back[j, k, 0] = c_re
                back[j, k, 1] = c_im
                a_re = o_re * c_re + o_im * c_im
                a_im = o_re * c_im - o_im * c_re
                n_re = a_re if n_re is None else n_re + a_re
                n_im = a_im if n_im is None else n_im + a_im
            n_buf[it, 0, :, k] = n_re.reshape(blocks, rows, N)
            n_buf[it, 1, :, k] = n_im.reshape(blocks, rows, N)
        n_pair(it).start()

    def gradient(it):
        for j in range(positions):
            g_re, g_im = None, None
            for k in range(modes):
                c_re, c_im = back[j, k, 0], back[j, k, 1]
                p_re, p_im = probe_part(it, k, 0), probe_part(it, k, 1)
                a_re = p_re * c_re + p_im * c_im
                a_im = p_re * c_im - p_im * c_re
                g_re = a_re if g_re is None else g_re + a_re
                g_im = a_im if g_im is None else g_im + a_im
            place(0, j, g_re)
            place(1, j, g_im)
        for c in range(2):
            g_t[it, c] = placed(c, 0)
            g_h[c] = placed(c, 1)
        wide = lax.broadcasted_iota(jnp.int32, (2 * N, N), 1)
        real, rolled = g_h[0], pltpu.roll(g_h[1], HALF, 1)
        gp_l[it] = jnp.where(wide >= HALF, real, rolled)
        gp_r[it] = jnp.where(wide < HALF, real, rolled)

    def strip_sum(strip):
        top, low = strip[pl.ds(0, HALF)], strip[pl.ds(N + HALF, HALF)]
        upper = strip[pl.ds(HALF, HALF)] + jnp.where(lane < N * has_u, low, 0.0)
        lower = strip[pl.ds(N, HALF)] + jnp.where(lane < N * has_d, top, 0.0)
        return jnp.concatenate([upper, lower], axis=0)

    def update(it, old, new):
        from_l, from_r = strip_sum(f_l.at[it]), strip_sum(f_r.at[it])
        weight = l_sum[it] + REGULAR
        for c in range(2):
            from_up = jnp.where(lane < N * has_u, g_dn[it, c], 0.0)
            from_down = jnp.where(lane < N * has_d, g_up[it, c], 0.0)
            total = g_t[it, c, pl.ds(HALF, N), :] + jnp.concatenate([from_up, from_down], axis=0)
            left = from_l if c == 0 else pltpu.roll(from_l, HALF, 1)
            right = from_r if c == 0 else pltpu.roll(from_r, HALF, 1)
            total += jnp.where(lane_n < HALF * has_l, left, 0.0)
            total += jnp.where(lane_n >= N - HALF * has_r, right, 0.0)
            new[c] = old[c] - OBJECT_STEP * total / weight

    def drain():
        for copy in offset_copies():
            copy.wait_send()
        for it in range(ITERS):
            for copy in fetch_copies(it, tiles[it]) + grad_copies(it):
                copy.wait_send()
            pair(0, it, m_buf.at[it], m_pre.at[it]).wait_send()
            n_pair(it).wait_send()
            await_bytes(m_rcv.at[it], all_send.at[0, it])
            await_bytes(mz_rcv.at[it], all_send.at[1, it])
            await_bytes(n_rcv.at[it], all_send.at[2, it])
            await_bytes(nz_rcv.at[it], all_send.at[3, it])
            if it + 1 < ITERS:
                await_bytes(p_buf.at[it, 0], pair_send.at[2, it])
                await_bytes(p_buf.at[it, 0, pl.ds(0, blocks - 1)], all_send.at[4, it])

    barrier = pltpu.get_barrier_semaphore()
    greeted = [side_dev(step) for step in SIDES[:4]] + peer_dev + z_devs
    greeted += [side_dev(step) for step in SIDES[4:]] + [partner]
    for dev in greeted:
        pl.semaphore_signal(barrier, inc=1, device_id=dev, device_id_type=MESH)
    loads = [pltpu.make_async_copy(src, dst, load_sem.at[i]) for i, (src, dst) in enumerate(
        [(tile_hbm, tile_in), (offs_hbm, offs), (probe_hbm, probe_in), (tables_hbm, tables),
         (inten_hbm, inten)])]
    for load in loads:
        load.start()
    loads[0].wait()
    pack(0, tile_in)
    loads[1].wait()
    pl.semaphore_wait(barrier, len(greeted))

    for copy in fetch_copies(0, tile_in) + offset_copies():
        copy.start()
    for channel in range(2):
        for half in range(2):
            for j in range(positions):
                pads[channel, half, j, pl.ds(0, N), :] = jnp.zeros((N, N), F32)
                pads[channel, half, j, pl.ds(2 * N, N), :] = jnp.zeros((N, N), F32)
    bright_pad[...] = jnp.zeros_like(bright_pad)
    for load in loads[2:]:
        load.wait()

    tiles = [tile_in, tile1, obj_out]
    for it in range(ITERS):
        for copy in fetch_copies(it, tiles[it]):
            copy.wait_recv()
        assemble(it, tiles[it])
        extract(it)
        if it > 0:
            wait_p(it - 1)
        waves(it)
        send_m(it)
        gradient(it)
        if it + 1 < ITERS:
            for copy in grad_copies(it):
                copy.start()
        send_n(it)
        if it == 0:
            for copy in offset_copies():
                copy.wait_recv()
        light(it)
        send_mz(it)
        send_nz(it)
        if it + 1 == ITERS:
            for copy in grad_copies(it):
                copy.start()
        if it + 1 == ITERS:
            send_p(it)
        for copy in grad_copies(it):
            copy.wait_recv()
        update(it, tiles[it], tiles[it + 1])
        if it + 1 < ITERS:
            pack(it + 1, tiles[it + 1])
            for copy in fetch_copies(it + 1, tiles[it + 1]):
                copy.start()
            send_p(it)
        if it + 1 == ITERS:
            drain()
        forward_p(it)
    wait_p(ITERS - 1)
    for k in range(modes):
        for c in range(2):
            prb_out[k, c] = probe_part(ITERS, k, c)

    await_bytes(p_buf.at[ITERS - 1, 0], pair_send.at[2, ITERS - 1])
    await_bytes(p_buf.at[ITERS - 1, 0, pl.ds(0, blocks - 1)], all_send.at[4, ITERS - 1])


def deliver(obj_in, prb_in, obj_out, prb_out, sem):
    copies = [pltpu.make_async_copy(obj_in, obj_out, sem.at[0]),
              pltpu.make_async_copy(prb_in, prb_out, sem.at[1])]
    for copy in copies:
        copy.start()
    for copy in copies:
        copy.wait()


def per_device(n_sy, n_sx, object_tile, probe_modes, scan_offsets, intensities):
    positions = scan_offsets.shape[2]
    modes = probe_modes.shape[0]
    depth = n_sx // Y_LO
    blocks = n_sy // 2 * Y_LO
    rows = N // blocks
    offsets = scan_offsets.transpose(0, 1, 3, 2)
    measured = intensities[0, 0]
    tables = jnp.asarray(dft_tables())
    vmem = functools.partial(pltpu.VMEM, dtype=F32)
    it = ITERS
    scratch = [
        vmem(object_tile.shape), vmem(probe_modes.shape), vmem(measured.shape),
        pltpu.VMEM(tables.shape, BF16), pltpu.SMEM(offsets.shape, jnp.int32),
        pltpu.SMEM((len(SIDES),) + offsets.shape, jnp.int32),
        vmem((2, N, N)), vmem((it, 2, 2 * N, N)), vmem((it, 2, 2 * N, N)),
        vmem((it, N, N)), vmem((it, N, N)), vmem((it, 2 * N, N)), vmem((it, 2 * N, N)),
        vmem((positions, 2, N, N)), vmem((positions, modes, 2, N, N)),
        vmem((2, 2, positions, 3 * N, N)), vmem((4 * N, N)),
        vmem((it, 2, 2 * N, N)), vmem((2, 2 * N, N)),
        vmem((it, 2 * N, N)), vmem((it, 2 * N, N)), vmem((it, 2, HALF, N)), vmem((it, 2, HALF, N)),
        vmem((it, 2 * N, N)), vmem((it, 2 * N, N)), vmem((it, N, N)),
        vmem((it, 2, blocks, modes, rows, N)), vmem((it, blocks, modes, rows, N)),
        vmem((it, blocks, modes, rows, N)), vmem((it, blocks - 1, modes, rows, N)),
        vmem((it, modes, rows, N)), vmem((it, depth - 1, modes, rows, N)),
        vmem((it, blocks, rows, N)), vmem((it, blocks, rows, N)), vmem((it, blocks, rows, N)),
        vmem((it, blocks - 1, rows, N)), vmem((it, rows, N)), vmem((it, depth - 1, rows, N)),
        vmem((it, 2, blocks, modes, rows, N)),
        pltpu.SemaphoreType.DMA((3, it, len(SIDES))), pltpu.SemaphoreType.DMA((3, it, len(SIDES))),
        pltpu.SemaphoreType.DMA((3, it)), pltpu.SemaphoreType.DMA((3, it)),
        pltpu.SemaphoreType.DMA((5, it)), pltpu.SemaphoreType.DMA((4, it)),
        pltpu.SemaphoreType.DMA((it, blocks - 1)),
        pltpu.SemaphoreType.DMA((5,)),
    ]
    in_vmem = pl.BlockSpec(memory_space=pltpu.VMEM)
    results = pl.pallas_call(
        functools.partial(kernel, n_sy, n_sx, positions, modes),
        out_shape=(pltpu.VMEM(object_tile.shape, F32), pltpu.VMEM(probe_modes.shape, F32)),
        in_specs=[pl.BlockSpec(memory_space=pl.ANY)] * 5,
        out_specs=(in_vmem, in_vmem),
        scratch_shapes=scratch,
        compiler_params=pltpu.CompilerParams(collective_id=0, has_side_effects=True),
    )(offsets, object_tile, probe_modes, measured, tables)
    results = [pltpu.with_memory_space_constraint(r, pltpu.VMEM) for r in results]
    return pl.pallas_call(
        deliver,
        out_shape=(jax.ShapeDtypeStruct(object_tile.shape, F32),
                   jax.ShapeDtypeStruct(probe_modes.shape, F32)),
        in_specs=[in_vmem, in_vmem],
        out_specs=(pl.BlockSpec(memory_space=pl.ANY), pl.BlockSpec(memory_space=pl.ANY)),
        scratch_shapes=[pltpu.SemaphoreType.DMA((2,))],
    )(*results)


def solution(mesh):
    placed = (P(None, "sy", "sx"), P(), P("sy", "sx", None, None), P("sy", "sx", None, None, None))
    return jax.shard_map(
        functools.partial(per_device, mesh.shape["sy"], mesh.shape["sx"]),
        mesh=mesh,
        in_specs=placed,
        out_specs=(P(None, "sy", "sx"), P()),
        check_vma=False,
    )
```

```python
import functools

import numpy as np
import jax
import jax.numpy as jnp
from jax import lax
from jax.experimental import pallas as pl
from jax.experimental.pallas import tpu as pltpu
from jax.sharding import PartitionSpec as P

ITERS = 2
OBJECT_STEP = 0.5
PROBE_STEP = 2.0
REGULAR = 1.0
N = 128
HALF = 64
Y_LO = 2
MESH = pl.DeviceIdType.MESH
F32 = jnp.float32
BF16 = jnp.bfloat16

SIDES = [(-1, -1), (1, -1), (-1, 1), (1, 1), (-1, 0), (1, 0), (0, -1), (0, 1)]


def dft_tables():
    index = np.arange(N)
    angle = (index[:, None] * index[None, :] % N) * (2.0 * np.pi / N)
    scale = 1.0 / np.sqrt(float(N))
    cosine, sine = np.cos(angle) * scale, np.sin(angle) * scale
    forward = np.block([[cosine, -sine], [sine, cosine]])
    parts = []
    for matrix in (forward, forward.T):
        high = matrix.astype(np.float32).astype(BF16)
        low = (matrix - high.astype(np.float64)).astype(np.float32).astype(BF16)
        parts += [high, low]
    return np.stack(parts)


def split(value):
    high = value.astype(BF16)
    low = (value - high.astype(F32)).astype(BF16)
    return high, low


def dot(left, right):
    return jnp.dot(left, right, preferred_element_type=F32)


def swap_blocks(value):
    top = jnp.concatenate([value[:N, :N], value[N:, :N]], axis=1)
    bottom = jnp.concatenate([value[:N, N:], value[N:, N:]], axis=1)
    return jnp.concatenate([top, bottom], axis=0)


def far_first(count):
    return sorted(range(count), key=lambda d: -min(d, count - d))


def kernel(n_sy, n_sx, positions, modes, offs_hbm, tile_hbm, probe_hbm, inten_hbm, tables_hbm,
           obj_out, prb_out,
           tile_in, probe_in, inten, tables, offs, near_offs,
           tile1, can_t, can_h, pack_l, pack_r, strip_l, strip_r,
           obj, back, pads, bright_pad, g_t, g_h, gp_l, gp_r, g_up, g_dn, f_l, f_r, l_sum,
           n_buf, n_pre, n_chip, n_rcv, n_part, nz_rcv,
           m_buf, m_pre, m_chip, m_rcv, m_part, mz_rcv, p_buf,
           side_send, side_recv, pair_send, pair_recv, all_send, all_recv, probe_recv, load_sem):
    sy = lax.axis_index("sy")
    sx = lax.axis_index("sx")
    depth = n_sx // Y_LO
    cores = 2
    n_yh = min(2, n_sy // cores)
    n_x, n_y = n_sy // (cores * n_yh), n_yh * Y_LO
    core = lax.rem(sy, cores)
    x = lax.div(sy, cores * n_yh)
    y_lo = lax.div(sx, depth)
    y = lax.rem(lax.div(sy, cores), n_yh) * Y_LO + y_lo
    z = lax.rem(sx, depth)
    def up(value, count):
        return jnp.where(value >= count, value - count, value)

    def wrap(value, count, step):
        return up(value + step, count) if step >= 0 else jnp.where(
            value + step < 0, value + step + count, value + step)

    x_at = [wrap(x, n_x, d) for d in range(n_x)]
    y_at = [wrap(y, n_y, d) for d in range(n_y)]
    y_row = [lax.div(v, Y_LO) * cores + core for v in y_at]
    y_col = [lax.rem(v, Y_LO) * depth + z for v in y_at]
    blocks = n_x * n_y
    rows = N // blocks
    me = x * n_y + y
    peers = [(dx, dy) for dx in far_first(n_x) for dy in far_first(n_y) if dx or dy]
    peers.sort(key=lambda p: -(min(p[0], n_x - p[0]) + min(p[1], n_y - p[1])))
    peer_index = [x_at[dx] * n_y + y_at[dy] for dx, dy in peers]
    peer_dev = [(x_at[dx] * (cores * n_yh) + y_row[dy], y_col[dy]) for dx, dy in peers]
    from_index = [x_at[-dx] * n_y + y_at[-dy] for dx, dy in peers]
    z_devs = [(sy, y_lo * depth + wrap(z, depth, d)) for d in far_first(depth) if d]
    partner = (sy + 1 - 2 * core, sx)

    row_at = {d: wrap(sy, n_sy, d) for d in (-1, 0, 1)}
    col_at = {d: wrap(sx, n_sx, d) for d in (-1, 0, 1)}

    def side_dev(step):
        return (row_at[step[0]], col_at[step[1]])

    lane = lax.broadcasted_iota(jnp.int32, (HALF, N), 1)
    lane_n = lax.broadcasted_iota(jnp.int32, (N, N), 1)
    has_u = jnp.where(sy > 0, 1, 0)
    has_d = jnp.where(sy < n_sy - 1, 1, 0)
    has_l = jnp.where(sx > 0, 1, 0)
    has_r = jnp.where(sx < n_sx - 1, 1, 0)

    def remote(src, dst, send, recv, dev):
        return pltpu.make_async_remote_copy(
            src_ref=src, dst_ref=dst, send_sem=send, recv_sem=recv,
            device_id=dev, device_id_type=MESH)

    def await_bytes(ref, sem):
        pltpu.make_async_copy(ref, ref, sem).wait()

    def fetch_copies(it, tile):
        top, bottom, both = pl.ds(0, HALF), pl.ds(HALF, HALF), pl.ds(0, N)
        c_top, c_mid, c_low = pl.ds(0, HALF), pl.ds(HALF, N), pl.ds(N + HALF, HALF)
        plan = [
            (pack_l.at[it, top], strip_r.at[it, c_low]),
            (pack_l.at[it, bottom], strip_r.at[it, c_top]),
            (pack_r.at[it, top], strip_l.at[it, c_low]),
            (pack_r.at[it, bottom], strip_l.at[it, c_top]),
            (tile.at[:, top, :], can_t.at[it, :, c_low, :]),
            (tile.at[:, bottom, :], can_t.at[it, :, c_top, :]),
            (pack_l.at[it, both], strip_r.at[it, c_mid]),
            (pack_r.at[it, both], strip_l.at[it, c_mid]),
        ]
        return [remote(src, dst, side_send.at[0, it, i], side_recv.at[0, it, i], side_dev(SIDES[i]))
                for i, (src, dst) in enumerate(plan)]

    def strip_copies(kind, it, unit, vertical, src_l, src_r, left, right):
        top, mid, low = pl.ds(0, unit), pl.ds(unit, 2 * unit), pl.ds(3 * unit, unit)
        plan = [
            (src_l.at[top], right.at[top]),
            (src_l.at[low], right.at[low]),
            (src_r.at[top], left.at[top]),
            (src_r.at[low], left.at[low]),
        ] + vertical + [
            (src_l.at[mid], right.at[mid]),
            (src_r.at[mid], left.at[mid]),
        ]
        return [remote(src, dst, side_send.at[kind, it, i], side_recv.at[kind, it, i],
                       side_dev(SIDES[i])) for i, (src, dst) in enumerate(plan)]

    def grad_copies(it):
        vertical = [(g_t.at[it, :, pl.ds(0, HALF), :], g_up.at[it]),
                    (g_t.at[it, :, pl.ds(N + HALF, HALF), :], g_dn.at[it])]
        return strip_copies(1, it, HALF, vertical, gp_l.at[it], gp_r.at[it], f_l.at[it], f_r.at[it])

    def offset_copies():
        return [remote(offs, near_offs.at[i], side_send.at[2, 0, i], side_recv.at[2, 0, i],
                       side_dev(step)) for i, step in enumerate(SIDES)]

    def pack(it, tile):
        real, rolled = tile[0], pltpu.roll(tile[1], HALF, 1)
        pack_l[it] = jnp.where(lane_n < HALF, real, rolled)
        pack_r[it] = jnp.where(lane_n >= HALF, real, rolled)

    def column_mask(column):
        return (lane_n >= column - HALF) & (lane_n < column + HALF)

    def assemble(it, tile):
        keep_re = (lane >= HALF * (1 - has_r)) & (lane < HALF + HALF * has_l)
        keep_im = (lane >= HALF * (1 - has_l)) & (lane < HALF + HALF * has_r)
        keep_u = lane < N * has_u
        keep_d = lane < N * has_d
        for c in range(2):
            can_t[it, c, pl.ds(HALF, N), :] = tile[c]
            top = can_t[it, c, pl.ds(0, HALF), :]
            can_t[it, c, pl.ds(0, HALF), :] = jnp.where(keep_u, top, 0.0)
            low = can_t[it, c, pl.ds(N + HALF, HALF), :]
            can_t[it, c, pl.ds(N + HALF, HALF), :] = jnp.where(keep_d, low, 0.0)
        for part in range(4):
            at = pl.ds(part * HALF, HALF)
            left, right = strip_l[it, at], strip_r[it, at]
            real = jnp.where(keep_re, jnp.where(lane < HALF, right, left), 0.0)
            imag = jnp.where(keep_im, jnp.where(lane < HALF, left, right), 0.0)
            if part == 0:
                real, imag = jnp.where(keep_u, real, 0.0), jnp.where(keep_u, imag, 0.0)
            if part == 3:
                real, imag = jnp.where(keep_d, real, 0.0), jnp.where(keep_d, imag, 0.0)
            can_h[it, 0, at, :] = real
            can_h[it, 1, at, :] = pltpu.roll(imag, HALF, 1)

    def extract(it):
        total = None
        for j in range(positions):
            row, column = offs[0, 0, 0, j], offs[0, 0, 1, j]
            mask = column_mask(column)
            shift = lax.rem(HALF + N - column, N)
            for c in range(2):
                inner = can_t[it, c, pl.ds(row, N), :]
                outer = can_h[it, c, pl.ds(row, N), :]
                patch = pltpu.roll(jnp.where(mask, inner, outer), shift, 1)
                obj[j, c] = patch
                total = patch * patch if total is None else total + patch * patch
        m_buf[it] = total.reshape(blocks, rows, N)
        pair(0, it, m_buf.at[it], m_pre.at[it]).start()

    def place(channel, j, term):
        column = offs[0, 0, 1, j]
        mask = column_mask(column)
        turned = pltpu.roll(term, lax.rem(column + HALF, N), 1)
        pads[channel, 0, j, pl.ds(N, N), :] = jnp.where(mask, turned, 0.0)
        pads[channel, 1, j, pl.ds(N, N), :] = jnp.where(mask, 0.0, turned)

    def placed(channel, half):
        total = None
        for j in range(positions):
            window = pads[channel, half, j, pl.ds(N - offs[0, 0, 0, j], 2 * N), :]
            total = window if total is None else total + window
        return total

    def probe_part(it, k, c):
        if it == 0:
            return probe_in[k, c]
        return p_buf[it - 1, c, :, k].reshape(N, N)

    def light(it):
        bright = None
        for k in range(modes):
            for c in range(2):
                part = probe_part(it, k, c)
                bright = part * part if bright is None else bright + part * part
        bright_pad[pl.ds(N + HALF, N), :] = bright
        total = jnp.zeros((N, N), F32)
        for dy in (-1, 0, 1):
            for dx in (-1, 0, 1):
                inside = jnp.where((sy + dy >= 0) & (sy + dy < n_sy)
                                   & (sx + dx >= 0) & (sx + dx < n_sx), 0, 4 * N)
                table = near_offs.at[SIDES.index((-dy, -dx))] if dx or dy else offs

                def position(j, running, dy=dy, dx=dx, inside=inside, table=table):
                    column = table[0, 0, 1, j]
                    window = bright_pad[pl.ds(2 * N - N * dy - table[0, 0, 0, j], N), :]
                    turned = pltpu.roll(window, lax.rem(column + HALF, N), 1)
                    first = column + (N * dx - HALF) + inside
                    mask = (lane_n >= first) & (lane_n < first + N)
                    return running + jnp.where(mask, turned, 0.0)

                total = lax.fori_loop(0, positions, position, total)
        l_sum[it] = total

    def pair(what, it, src, dst):
        return remote(src, dst, pair_send.at[what, it], pair_recv.at[what, it], partner)

    def n_pair(it):
        return pair(1, it, n_buf.at[it, 1 - core], n_pre.at[it])

    def forward(it, at):
        pair(2, it, p_buf.at[it, core, at], p_buf.at[it, core, at]).start()

    def wait_p(it):
        await_bytes(p_buf.at[it, 0], pair_recv.at[2, it])

    def spread(what, it, source, target):
        for slot, (other, dev) in enumerate(zip(peer_index, peer_dev)):
            remote(source(other), target(slot), all_send.at[what, it], all_recv.at[what, it],
                   dev).start()

    def spread_z(what, it, source, target):
        for slot, dev in enumerate(z_devs):
            remote(source, target(slot), all_send.at[what, it], all_recv.at[what, it], dev).start()

    def send_m(it):
        pair(0, it, m_buf.at[it], m_pre.at[it]).wait_recv()
        m_chip[it] = m_buf[it] + m_pre[it]
        spread(0, it, lambda other: m_chip.at[it, other], lambda s: m_rcv.at[it, s])

    def send_mz(it):
        await_bytes(m_rcv.at[it], all_recv.at[0, it])
        m_part[it] = m_chip[it, me] + jnp.sum(m_rcv[it], axis=0)
        spread_z(1, it, m_part.at[it], lambda s: mz_rcv.at[it, s])

    def send_n(it):
        n_pair(it).wait_recv()
        n_chip[it] = n_buf[it, core] + n_pre[it]
        spread(2, it, lambda other: n_chip.at[it, other], lambda s: n_rcv.at[it, s])

    def send_nz(it):
        await_bytes(n_rcv.at[it], all_recv.at[2, it])
        n_part[it] = n_chip[it, me] + jnp.sum(n_rcv[it], axis=0)
        spread_z(3, it, n_part.at[it], lambda s: nz_rcv.at[it, s])

    def send_p(it):
        await_bytes(mz_rcv.at[it], all_recv.at[1, it])
        weight = m_part[it] + jnp.sum(mz_rcv[it], axis=0) + REGULAR
        await_bytes(nz_rcv.at[it], all_recv.at[3, it])
        numerator = n_part[it] + jnp.sum(nz_rcv[it], axis=0)
        for k in range(modes):
            if it == 0:
                old = probe_in[k, core, pl.ds(pl.multiple_of(me * rows, rows), rows), :]
            else:
                old = p_buf[it - 1, core, me, k]
            p_buf[it, core, me, k] = old - PROBE_STEP * numerator[k] / weight
        mine = p_buf.at[it, core, me]
        for slot, dev in enumerate(peer_dev):
            remote(mine, mine, all_send.at[4, it], probe_recv.at[it, slot], dev).start()
        forward(it, me)

    def forward_p(it):
        for slot in reversed(range(blocks - 1)):
            await_bytes(p_buf.at[it, core, from_index[slot]], probe_recv.at[it, slot])
            forward(it, from_index[slot])

    def waves(it):
        def right(v, t):
            h, l = split(v)
            count = v.shape[0]
            both = dot(jnp.concatenate([h, l], axis=0), tables[t])
            return both[:count] + both[count:] + dot(h, tables[t + 1])

        def right_all(vs, t):
            outs = []
            for i in range(0, len(vs), 2):
                out = right(jnp.concatenate(vs[i:i + 2], axis=0), t)
                outs += [out[:2 * N], out[2 * N:]]
            return outs

        def left(t, v):
            h, l = split(v)
            both = dot(tables[t:t + 2].reshape(4 * N, 2 * N), h)
            return both[:2 * N] + both[2 * N:] + dot(tables[t], l)

        def exits(j):
            o_re, o_im = obj[j, 0], obj[j, 1]
            wave = []
            for k in range(modes):
                p_re, p_im = probe_part(it, k, 0), probe_part(it, k, 1)
                wave.append(jnp.concatenate(
                    [p_re * o_re - p_im * o_im, p_re * o_im + p_im * o_re], axis=1))
            return jnp.concatenate(wave, axis=0)

        def misfits(j, spec):
            power = spec[:N] * spec[:N] + spec[N:] * spec[N:]
            misfit = power[:, :N] + power[:, N:] - inten[j]
            wide = jnp.concatenate([misfit, misfit], axis=1)
            return jnp.concatenate([spec[:N] * wide, spec[N:] * wide], axis=0)

        members = range(positions)
        waves_in = [exits(j) for j in members]
        half = [swap_blocks(v) for v in right_all(waves_in, 0)]
        spec = [left(2, v) for v in half]
        dev = [misfits(j, v) for j, v in zip(members, spec)]
        half = [swap_blocks(left(0, v)) for v in dev]
        chis = right_all(half, 2)
        for k in range(modes):
            n_re, n_im = None, None
            for j, chi in zip(members, chis):
                o_re, o_im = obj[j, 0], obj[j, 1]
                c_re, c_im = chi[k * N:(k + 1) * N, :N], chi[k * N:(k + 1) * N, N:]
                back[j, k, 0] = c_re
                back[j, k, 1] = c_im
                a_re = o_re * c_re + o_im * c_im
                a_im = o_re * c_im - o_im * c_re
                n_re = a_re if n_re is None else n_re + a_re
                n_im = a_im if n_im is None else n_im + a_im
            n_buf[it, 0, :, k] = n_re.reshape(blocks, rows, N)
            n_buf[it, 1, :, k] = n_im.reshape(blocks, rows, N)
        n_pair(it).start()

    def gradient(it):
        for j in range(positions):
            g_re, g_im = None, None
            for k in range(modes):
                c_re, c_im = back[j, k, 0], back[j, k, 1]
                p_re, p_im = probe_part(it, k, 0), probe_part(it, k, 1)
                a_re = p_re * c_re + p_im * c_im
                a_im = p_re * c_im - p_im * c_re
                g_re = a_re if g_re is None else g_re + a_re
                g_im = a_im if g_im is None else g_im + a_im
            place(0, j, g_re)
            place(1, j, g_im)
        for c in range(2):
            g_t[it, c] = placed(c, 0)
            g_h[c] = placed(c, 1)
        wide = lax.broadcasted_iota(jnp.int32, (2 * N, N), 1)
        real, rolled = g_h[0], pltpu.roll(g_h[1], HALF, 1)
        gp_l[it] = jnp.where(wide >= HALF, real, rolled)
        gp_r[it] = jnp.where(wide < HALF, real, rolled)

    def strip_sum(strip):
        top, low = strip[pl.ds(0, HALF)], strip[pl.ds(N + HALF, HALF)]
        upper = strip[pl.ds(HALF, HALF)] + jnp.where(lane < N * has_u, low, 0.0)
        lower = strip[pl.ds(N, HALF)] + jnp.where(lane < N * has_d, top, 0.0)
        return jnp.concatenate([upper, lower], axis=0)

    def update(it, old, new):
        from_l, from_r = strip_sum(f_l.at[it]), strip_sum(f_r.at[it])
        weight = l_sum[it] + REGULAR
        for c in range(2):
            from_up = jnp.where(lane < N * has_u, g_dn[it, c], 0.0)
            from_down = jnp.where(lane < N * has_d, g_up[it, c], 0.0)
            total = g_t[it, c, pl.ds(HALF, N), :] + jnp.concatenate([from_up, from_down], axis=0)
            left = from_l if c == 0 else pltpu.roll(from_l, HALF, 1)
            right = from_r if c == 0 else pltpu.roll(from_r, HALF, 1)
            total += jnp.where(lane_n < HALF * has_l, left, 0.0)
            total += jnp.where(lane_n >= N - HALF * has_r, right, 0.0)
            new[c] = old[c] - OBJECT_STEP * total / weight

    def drain():
        for copy in offset_copies():
            copy.wait_send()
        for it in range(ITERS):
            for copy in fetch_copies(it, tiles[it]) + grad_copies(it):
                copy.wait_send()
            pair(0, it, m_buf.at[it], m_pre.at[it]).wait_send()
            n_pair(it).wait_send()
            await_bytes(m_rcv.at[it], all_send.at[0, it])
            await_bytes(mz_rcv.at[it], all_send.at[1, it])
            await_bytes(n_rcv.at[it], all_send.at[2, it])
            await_bytes(nz_rcv.at[it], all_send.at[3, it])
            if it + 1 < ITERS:
                await_bytes(p_buf.at[it, 0], pair_send.at[2, it])
                await_bytes(p_buf.at[it, 0, pl.ds(0, blocks - 1)], all_send.at[4, it])

    barrier = pltpu.get_barrier_semaphore()
    greeted = [side_dev(step) for step in SIDES[:4]] + peer_dev + z_devs
    greeted += [side_dev(step) for step in SIDES[4:]]
    for dev in greeted:
        pl.semaphore_signal(barrier, inc=1, device_id=dev, device_id_type=MESH)
    loads = [pltpu.make_async_copy(src, dst, load_sem.at[i]) for i, (src, dst) in enumerate(
        [(tile_hbm, tile_in), (offs_hbm, offs), (probe_hbm, probe_in), (tables_hbm, tables),
         (inten_hbm, inten)])]
    for load in loads:
        load.start()
    loads[0].wait()
    pack(0, tile_in)
    loads[1].wait()
    pl.semaphore_wait(barrier, len(greeted))

    for copy in fetch_copies(0, tile_in) + offset_copies():
        copy.start()
    for channel in range(2):
        for half in range(2):
            for j in range(positions):
                pads[channel, half, j, pl.ds(0, N), :] = jnp.zeros((N, N), F32)
                pads[channel, half, j, pl.ds(2 * N, N), :] = jnp.zeros((N, N), F32)
    bright_pad[...] = jnp.zeros_like(bright_pad)
    for load in loads[2:]:
        load.wait()

    tiles = [tile_in, tile1, obj_out]
    for it in range(ITERS):
        for copy in fetch_copies(it, tiles[it]):
            copy.wait_recv()
        assemble(it, tiles[it])
        extract(it)
        if it > 0:
            wait_p(it - 1)
        waves(it)
        send_m(it)
        gradient(it)
        if it + 1 < ITERS:
            for copy in grad_copies(it):
                copy.start()
        send_n(it)
        if it == 0:
            for copy in offset_copies():
                copy.wait_recv()
        light(it)
        send_mz(it)
        send_nz(it)
        if it + 1 == ITERS:
            for copy in grad_copies(it):
                copy.start()
        if it + 1 == ITERS:
            send_p(it)
        for copy in grad_copies(it):
            copy.wait_recv()
        update(it, tiles[it], tiles[it + 1])
        if it + 1 < ITERS:
            pack(it + 1, tiles[it + 1])
            for copy in fetch_copies(it + 1, tiles[it + 1]):
                copy.start()
            send_p(it)
        if it + 1 == ITERS:
            drain()
        forward_p(it)
    wait_p(ITERS - 1)
    for k in range(modes):
        for c in range(2):
            prb_out[k, c] = probe_part(ITERS, k, c)

    await_bytes(p_buf.at[ITERS - 1, 0], pair_send.at[2, ITERS - 1])
    await_bytes(p_buf.at[ITERS - 1, 0, pl.ds(0, blocks - 1)], all_send.at[4, ITERS - 1])


def deliver(obj_in, prb_in, obj_out, prb_out, sem):
    copies = [pltpu.make_async_copy(obj_in, obj_out, sem.at[0]),
              pltpu.make_async_copy(prb_in, prb_out, sem.at[1])]
    for copy in copies:
        copy.start()
    for copy in copies:
        copy.wait()


def per_device(n_sy, n_sx, object_tile, probe_modes, scan_offsets, intensities):
    positions = scan_offsets.shape[2]
    modes = probe_modes.shape[0]
    depth = n_sx // Y_LO
    blocks = n_sy // 2 * Y_LO
    rows = N // blocks
    offsets = scan_offsets.transpose(0, 1, 3, 2)
    measured = intensities[0, 0]
    tables = jnp.asarray(dft_tables())
    vmem = functools.partial(pltpu.VMEM, dtype=F32)
    it = ITERS
    scratch = [
        vmem(object_tile.shape), vmem(probe_modes.shape), vmem(measured.shape),
        pltpu.VMEM(tables.shape, BF16), pltpu.SMEM(offsets.shape, jnp.int32),
        pltpu.SMEM((len(SIDES),) + offsets.shape, jnp.int32),
        vmem((2, N, N)), vmem((it, 2, 2 * N, N)), vmem((it, 2, 2 * N, N)),
        vmem((it, N, N)), vmem((it, N, N)), vmem((it, 2 * N, N)), vmem((it, 2 * N, N)),
        vmem((positions, 2, N, N)), vmem((positions, modes, 2, N, N)),
        vmem((2, 2, positions, 3 * N, N)), vmem((4 * N, N)),
        vmem((it, 2, 2 * N, N)), vmem((2, 2 * N, N)),
        vmem((it, 2 * N, N)), vmem((it, 2 * N, N)), vmem((it, 2, HALF, N)), vmem((it, 2, HALF, N)),
        vmem((it, 2 * N, N)), vmem((it, 2 * N, N)), vmem((it, N, N)),
        vmem((it, 2, blocks, modes, rows, N)), vmem((it, blocks, modes, rows, N)),
        vmem((it, blocks, modes, rows, N)), vmem((it, blocks - 1, modes, rows, N)),
        vmem((it, modes, rows, N)), vmem((it, depth - 1, modes, rows, N)),
        vmem((it, blocks, rows, N)), vmem((it, blocks, rows, N)), vmem((it, blocks, rows, N)),
        vmem((it, blocks - 1, rows, N)), vmem((it, rows, N)), vmem((it, depth - 1, rows, N)),
        vmem((it, 2, blocks, modes, rows, N)),
        pltpu.SemaphoreType.DMA((3, it, len(SIDES))), pltpu.SemaphoreType.DMA((3, it, len(SIDES))),
        pltpu.SemaphoreType.DMA((3, it)), pltpu.SemaphoreType.DMA((3, it)),
        pltpu.SemaphoreType.DMA((5, it)), pltpu.SemaphoreType.DMA((4, it)),
        pltpu.SemaphoreType.DMA((it, blocks - 1)),
        pltpu.SemaphoreType.DMA((5,)),
    ]
    in_vmem = pl.BlockSpec(memory_space=pltpu.VMEM)
    results = pl.pallas_call(
        functools.partial(kernel, n_sy, n_sx, positions, modes),
        out_shape=(pltpu.VMEM(object_tile.shape, F32), pltpu.VMEM(probe_modes.shape, F32)),
        in_specs=[pl.BlockSpec(memory_space=pl.ANY)] * 5,
        out_specs=(in_vmem, in_vmem),
        scratch_shapes=scratch,
        compiler_params=pltpu.CompilerParams(collective_id=0, has_side_effects=True),
    )(offsets, object_tile, probe_modes, measured, tables)
    results = [pltpu.with_memory_space_constraint(r, pltpu.VMEM) for r in results]
    return pl.pallas_call(
        deliver,
        out_shape=(jax.ShapeDtypeStruct(object_tile.shape, F32),
                   jax.ShapeDtypeStruct(probe_modes.shape, F32)),
        in_specs=[in_vmem, in_vmem],
        out_specs=(pl.BlockSpec(memory_space=pl.ANY), pl.BlockSpec(memory_space=pl.ANY)),
        scratch_shapes=[pltpu.SemaphoreType.DMA((2,))],
    )(*results)


def solution(mesh):
    placed = (P(None, "sy", "sx"), P(), P("sy", "sx", None, None), P("sy", "sx", None, None, None))
    return jax.shard_map(
        functools.partial(per_device, mesh.shape["sy"], mesh.shape["sx"]),
        mesh=mesh,
        in_specs=placed,
        out_specs=(P(None, "sy", "sx"), P()),
        check_vma=False,
    )
```

```python
import functools

import numpy as np
import jax
import jax.numpy as jnp
from jax import lax
from jax.experimental import pallas as pl
from jax.experimental.pallas import tpu as pltpu
from jax.sharding import PartitionSpec as P

ITERS = 2
OBJECT_STEP = 0.5
PROBE_STEP = 2.0
REGULAR = 1.0
N = 128
HALF = 64
Y_LO = 2
MESH = pl.DeviceIdType.MESH
F32 = jnp.float32
BF16 = jnp.bfloat16

SIDES = [(-1, -1), (1, -1), (-1, 1), (1, 1), (-1, 0), (1, 0), (0, -1), (0, 1)]


def dft_tables():
    index = np.arange(N)
    angle = (index[:, None] * index[None, :] % N) * (2.0 * np.pi / N)
    scale = 1.0 / np.sqrt(float(N))
    cosine, sine = np.cos(angle) * scale, np.sin(angle) * scale
    forward = np.block([[cosine, -sine], [sine, cosine]])
    parts = []
    for matrix in (forward, forward.T):
        high = matrix.astype(np.float32).astype(BF16)
        low = (matrix - high.astype(np.float64)).astype(np.float32).astype(BF16)
        parts += [high, low]
    return np.stack(parts)


def split(value):
    high = value.astype(BF16)
    low = (value - high.astype(F32)).astype(BF16)
    return high, low


def dot(left, right):
    return jnp.dot(left, right, preferred_element_type=F32)


def swap_blocks(value):
    top = jnp.concatenate([value[:N, :N], value[N:, :N]], axis=1)
    bottom = jnp.concatenate([value[:N, N:], value[N:, N:]], axis=1)
    return jnp.concatenate([top, bottom], axis=0)


def far_first(count):
    return sorted(range(count), key=lambda d: -min(d, count - d))


def kernel(n_sy, n_sx, positions, modes, offs_hbm, tile_hbm, probe_hbm, inten_hbm, tables_hbm,
           obj_out, prb_out,
           tile_in, probe_in, inten, tables, offs, near_offs,
           tile1, can_t, can_h, pack_l, pack_r, strip_l, strip_r,
           obj, back, pads, bright_pad, g_t, g_h, gp_l, gp_r, g_up, g_dn, f_l, f_r, l_sum,
           n_buf, n_pre, n_chip, n_rcv, n_part, nz_rcv,
           m_buf, m_pre, m_chip, m_rcv, m_part, mz_rcv, p_buf,
           side_send, side_recv, pair_send, pair_recv, all_send, all_recv, probe_recv, load_sem):
    sy = lax.axis_index("sy")
    sx = lax.axis_index("sx")
    depth = n_sx // Y_LO
    cores = 2
    n_yh = min(2, n_sy // cores)
    n_x, n_y = n_sy // (cores * n_yh), n_yh * Y_LO
    core = lax.rem(sy, cores)
    x = lax.div(sy, cores * n_yh)
    y_lo = lax.div(sx, depth)
    y = lax.rem(lax.div(sy, cores), n_yh) * Y_LO + y_lo
    z = lax.rem(sx, depth)
    def up(value, count):
        return jnp.where(value >= count, value - count, value)

    def wrap(value, count, step):
        return up(value + step, count) if step >= 0 else jnp.where(
            value + step < 0, value + step + count, value + step)

    x_at = [wrap(x, n_x, d) for d in range(n_x)]
    y_at = [wrap(y, n_y, d) for d in range(n_y)]
    y_row = [lax.div(v, Y_LO) * cores + core for v in y_at]
    y_col = [lax.rem(v, Y_LO) * depth + z for v in y_at]
    blocks = n_x * n_y
    rows = N // blocks
    me = x * n_y + y
    peers = [(dx, dy) for dx in far_first(n_x) for dy in far_first(n_y) if dx or dy]
    peers.sort(key=lambda p: -(min(p[0], n_x - p[0]) + min(p[1], n_y - p[1])))
    peer_index = [x_at[dx] * n_y + y_at[dy] for dx, dy in peers]
    peer_dev = [(x_at[dx] * (cores * n_yh) + y_row[dy], y_col[dy]) for dx, dy in peers]
    from_index = [x_at[-dx] * n_y + y_at[-dy] for dx, dy in peers]
    z_devs = [(sy, y_lo * depth + wrap(z, depth, d)) for d in far_first(depth) if d]
    partner = (sy + 1 - 2 * core, sx)

    row_at = {d: wrap(sy, n_sy, d) for d in (-1, 0, 1)}
    col_at = {d: wrap(sx, n_sx, d) for d in (-1, 0, 1)}

    def side_dev(step):
        return (row_at[step[0]], col_at[step[1]])

    lane = lax.broadcasted_iota(jnp.int32, (HALF, N), 1)
    lane_n = lax.broadcasted_iota(jnp.int32, (N, N), 1)
    has_u = jnp.where(sy > 0, 1, 0)
    has_d = jnp.where(sy < n_sy - 1, 1, 0)
    has_l = jnp.where(sx > 0, 1, 0)
    has_r = jnp.where(sx < n_sx - 1, 1, 0)

    def remote(src, dst, send, recv, dev):
        return pltpu.make_async_remote_copy(
            src_ref=src, dst_ref=dst, send_sem=send, recv_sem=recv,
            device_id=dev, device_id_type=MESH)

    def await_bytes(ref, sem):
        pltpu.make_async_copy(ref, ref, sem).wait()

    def fetch_copies(it, tile):
        top, bottom, both = pl.ds(0, HALF), pl.ds(HALF, HALF), pl.ds(0, N)
        c_top, c_mid, c_low = pl.ds(0, HALF), pl.ds(HALF, N), pl.ds(N + HALF, HALF)
        plan = [
            (pack_l.at[it, top], strip_r.at[it, c_low]),
            (pack_l.at[it, bottom], strip_r.at[it, c_top]),
            (pack_r.at[it, top], strip_l.at[it, c_low]),
            (pack_r.at[it, bottom], strip_l.at[it, c_top]),
            (tile.at[:, top, :], can_t.at[it, :, c_low, :]),
            (tile.at[:, bottom, :], can_t.at[it, :, c_top, :]),
            (pack_l.at[it, both], strip_r.at[it, c_mid]),
            (pack_r.at[it, both], strip_l.at[it, c_mid]),
        ]
        return [remote(src, dst, side_send.at[0, it, i], side_recv.at[0, it, i], side_dev(SIDES[i]))
                for i, (src, dst) in enumerate(plan)]

    def strip_copies(kind, it, unit, vertical, src_l, src_r, left, right):
        top, mid, low = pl.ds(0, unit), pl.ds(unit, 2 * unit), pl.ds(3 * unit, unit)
        plan = [
            (src_l.at[top], right.at[top]),
            (src_l.at[low], right.at[low]),
            (src_r.at[top], left.at[top]),
            (src_r.at[low], left.at[low]),
        ] + vertical + [
            (src_l.at[mid], right.at[mid]),
            (src_r.at[mid], left.at[mid]),
        ]
        return [remote(src, dst, side_send.at[kind, it, i], side_recv.at[kind, it, i],
                       side_dev(SIDES[i])) for i, (src, dst) in enumerate(plan)]

    def grad_copies(it):
        vertical = [(g_t.at[it, :, pl.ds(0, HALF), :], g_up.at[it]),
                    (g_t.at[it, :, pl.ds(N + HALF, HALF), :], g_dn.at[it])]
        return strip_copies(1, it, HALF, vertical, gp_l.at[it], gp_r.at[it], f_l.at[it], f_r.at[it])

    def offset_copies():
        return [remote(offs, near_offs.at[i], side_send.at[2, 0, i], side_recv.at[2, 0, i],
                       side_dev(step)) for i, step in enumerate(SIDES)]

    def pack(it, tile):
        real, rolled = tile[0], pltpu.roll(tile[1], HALF, 1)
        pack_l[it] = jnp.where(lane_n < HALF, real, rolled)
        pack_r[it] = jnp.where(lane_n >= HALF, real, rolled)

    def column_mask(column):
        return (lane_n >= column - HALF) & (lane_n < column + HALF)

    def assemble(it, tile):
        keep_re = (lane >= HALF * (1 - has_r)) & (lane < HALF + HALF * has_l)
        keep_im = (lane >= HALF * (1 - has_l)) & (lane < HALF + HALF * has_r)
        keep_u = lane < N * has_u
        keep_d = lane < N * has_d
        for c in range(2):
            can_t[it, c, pl.ds(HALF, N), :] = tile[c]
            top = can_t[it, c, pl.ds(0, HALF), :]
            can_t[it, c, pl.ds(0, HALF), :] = jnp.where(keep_u, top, 0.0)
            low = can_t[it, c, pl.ds(N + HALF, HALF), :]
            can_t[it, c, pl.ds(N + HALF, HALF), :] = jnp.where(keep_d, low, 0.0)
        for part in range(4):
            at = pl.ds(part * HALF, HALF)
            left, right = strip_l[it, at], strip_r[it, at]
            real = jnp.where(keep_re, jnp.where(lane < HALF, right, left), 0.0)
            imag = jnp.where(keep_im, jnp.where(lane < HALF, left, right), 0.0)
            if part == 0:
                real, imag = jnp.where(keep_u, real, 0.0), jnp.where(keep_u, imag, 0.0)
            if part == 3:
                real, imag = jnp.where(keep_d, real, 0.0), jnp.where(keep_d, imag, 0.0)
            can_h[it, 0, at, :] = real
            can_h[it, 1, at, :] = pltpu.roll(imag, HALF, 1)

    def extract(it):
        total = None
        for j in range(positions):
            row, column = offs[0, 0, 0, j], offs[0, 0, 1, j]
            mask = column_mask(column)
            shift = lax.rem(HALF + N - column, N)
            for c in range(2):
                inner = can_t[it, c, pl.ds(row, N), :]
                outer = can_h[it, c, pl.ds(row, N), :]
                patch = pltpu.roll(jnp.where(mask, inner, outer), shift, 1)
                obj[j, c] = patch
                total = patch * patch if total is None else total + patch * patch
        m_buf[it] = total.reshape(blocks, rows, N)
        pair(0, it, m_buf.at[it], m_pre.at[it]).start()

    def place(channel, j, term):
        column = offs[0, 0, 1, j]
        mask = column_mask(column)
        turned = pltpu.roll(term, lax.rem(column + HALF, N), 1)
        pads[channel, 0, j, pl.ds(N, N), :] = jnp.where(mask, turned, 0.0)
        pads[channel, 1, j, pl.ds(N, N), :] = jnp.where(mask, 0.0, turned)

    def placed(channel, half):
        total = None
        for j in range(positions):
            window = pads[channel, half, j, pl.ds(N - offs[0, 0, 0, j], 2 * N), :]
            total = window if total is None else total + window
        return total

    def probe_part(it, k, c):
        if it == 0:
            return probe_in[k, c]
        return p_buf[it - 1, c, :, k].reshape(N, N)

    def light(it):
        bright = None
        for k in range(modes):
            for c in range(2):
                part = probe_part(it, k, c)
                bright = part * part if bright is None else bright + part * part
        bright_pad[pl.ds(N + HALF, N), :] = bright
        total = jnp.zeros((N, N), F32)
        for dy in (-1, 0, 1):
            for dx in (-1, 0, 1):
                inside = jnp.where((sy + dy >= 0) & (sy + dy < n_sy)
                                   & (sx + dx >= 0) & (sx + dx < n_sx), 0, 4 * N)
                table = near_offs.at[SIDES.index((-dy, -dx))] if dx or dy else offs

                def position(j, running, dy=dy, dx=dx, inside=inside, table=table):
                    column = table[0, 0, 1, j]
                    window = bright_pad[pl.ds(2 * N - N * dy - table[0, 0, 0, j], N), :]
                    turned = pltpu.roll(window, lax.rem(column + HALF, N), 1)
                    first = column + (N * dx - HALF) + inside
                    mask = (lane_n >= first) & (lane_n < first + N)
                    return running + jnp.where(mask, turned, 0.0)

                total = lax.fori_loop(0, positions, position, total)
        l_sum[it] = total

    def pair(what, it, src, dst):
        return remote(src, dst, pair_send.at[what, it], pair_recv.at[what, it], partner)

    def n_pair(it):
        return pair(1, it, n_buf.at[it, 1 - core], n_pre.at[it])

    def forward(it, at):
        pair(2, it, p_buf.at[it, core, at], p_buf.at[it, core, at]).start()

    def wait_p(it):
        await_bytes(p_buf.at[it, 0], pair_recv.at[2, it])

    def spread(what, it, source, target):
        for slot, (other, dev) in enumerate(zip(peer_index, peer_dev)):
            remote(source(other), target(slot), all_send.at[what, it], all_recv.at[what, it],
                   dev).start()

    def spread_z(what, it, source, target):
        for slot, dev in enumerate(z_devs):
            remote(source, target(slot), all_send.at[what, it], all_recv.at[what, it], dev).start()

    def send_m(it):
        pair(0, it, m_buf.at[it], m_pre.at[it]).wait_recv()
        m_chip[it] = m_buf[it] + m_pre[it]
        spread(0, it, lambda other: m_chip.at[it, other], lambda s: m_rcv.at[it, s])

    def send_mz(it):
        await_bytes(m_rcv.at[it], all_recv.at[0, it])
        m_part[it] = m_chip[it, me] + jnp.sum(m_rcv[it], axis=0)
        spread_z(1, it, m_part.at[it], lambda s: mz_rcv.at[it, s])

    def send_n(it):
        n_pair(it).wait_recv()
        n_chip[it] = n_buf[it, core] + n_pre[it]
        spread(2, it, lambda other: n_chip.at[it, other], lambda s: n_rcv.at[it, s])

    def send_nz(it):
        await_bytes(n_rcv.at[it], all_recv.at[2, it])
        n_part[it] = n_chip[it, me] + jnp.sum(n_rcv[it], axis=0)
        spread_z(3, it, n_part.at[it], lambda s: nz_rcv.at[it, s])

    def send_p(it):
        await_bytes(mz_rcv.at[it], all_recv.at[1, it])
        weight = m_part[it] + jnp.sum(mz_rcv[it], axis=0) + REGULAR
        await_bytes(nz_rcv.at[it], all_recv.at[3, it])
        numerator = n_part[it] + jnp.sum(nz_rcv[it], axis=0)
        for k in range(modes):
            if it == 0:
                old = probe_in[k, core, pl.ds(pl.multiple_of(me * rows, rows), rows), :]
            else:
                old = p_buf[it - 1, core, me, k]
            p_buf[it, core, me, k] = old - PROBE_STEP * numerator[k] / weight
        mine = p_buf.at[it, core, me]
        for slot, dev in enumerate(peer_dev):
            remote(mine, mine, all_send.at[4, it], probe_recv.at[it, slot], dev).start()
        forward(it, me)

    def forward_p(it):
        for slot in reversed(range(blocks - 1)):
            await_bytes(p_buf.at[it, core, from_index[slot]], probe_recv.at[it, slot])
            forward(it, from_index[slot])

    def waves(it):
        def right(v, t):
            h, l = split(v)
            count = v.shape[0]
            both = dot(jnp.concatenate([h, l], axis=0), tables[t])
            return both[:count] + both[count:] + dot(h, tables[t + 1])

        def right_all(vs, t):
            return [right(v, t) for v in vs]

        def left(t, v):
            h, l = split(v)
            both = dot(tables[t:t + 2].reshape(4 * N, 2 * N), h)
            return both[:2 * N] + both[2 * N:] + dot(tables[t], l)

        def exits(j):
            o_re, o_im = obj[j, 0], obj[j, 1]
            wave = []
            for k in range(modes):
                p_re, p_im = probe_part(it, k, 0), probe_part(it, k, 1)
                wave.append(jnp.concatenate(
                    [p_re * o_re - p_im * o_im, p_re * o_im + p_im * o_re], axis=1))
            return jnp.concatenate(wave, axis=0)

        def misfits(j, spec):
            power = spec[:N] * spec[:N] + spec[N:] * spec[N:]
            misfit = power[:, :N] + power[:, N:] - inten[j]
            wide = jnp.concatenate([misfit, misfit], axis=1)
            return jnp.concatenate([spec[:N] * wide, spec[N:] * wide], axis=0)

        members = range(positions)
        waves_in = [exits(j) for j in members]
        half = [swap_blocks(v) for v in right_all(waves_in, 0)]
        spec = [left(2, v) for v in half]
        dev = [misfits(j, v) for j, v in zip(members, spec)]
        half = [swap_blocks(left(0, v)) for v in dev]
        chis = right_all(half, 2)
        for k in range(modes):
            n_re, n_im = None, None
            for j, chi in zip(members, chis):
                o_re, o_im = obj[j, 0], obj[j, 1]
                c_re, c_im = chi[k * N:(k + 1) * N, :N], chi[k * N:(k + 1) * N, N:]
                back[j, k, 0] = c_re
                back[j, k, 1] = c_im
                a_re = o_re * c_re + o_im * c_im
                a_im = o_re * c_im - o_im * c_re
                n_re = a_re if n_re is None else n_re + a_re
                n_im = a_im if n_im is None else n_im + a_im
            n_buf[it, 0, :, k] = n_re.reshape(blocks, rows, N)
            n_buf[it, 1, :, k] = n_im.reshape(blocks, rows, N)
        n_pair(it).start()

    def gradient(it):
        for j in range(positions):
            g_re, g_im = None, None
            for k in range(modes):
                c_re, c_im = back[j, k, 0], back[j, k, 1]
                p_re, p_im = probe_part(it, k, 0), probe_part(it, k, 1)
                a_re = p_re * c_re + p_im * c_im
                a_im = p_re * c_im - p_im * c_re
                g_re = a_re if g_re is None else g_re + a_re
                g_im = a_im if g_im is None else g_im + a_im
            place(0, j, g_re)
            place(1, j, g_im)
        for c in range(2):
            g_t[it, c] = placed(c, 0)
            g_h[c] = placed(c, 1)
        wide = lax.broadcasted_iota(jnp.int32, (2 * N, N), 1)
        real, rolled = g_h[0], pltpu.roll(g_h[1], HALF, 1)
        gp_l[it] = jnp.where(wide >= HALF, real, rolled)
        gp_r[it] = jnp.where(wide < HALF, real, rolled)

    def strip_sum(strip):
        top, low = strip[pl.ds(0, HALF)], strip[pl.ds(N + HALF, HALF)]
        upper = strip[pl.ds(HALF, HALF)] + jnp.where(lane < N * has_u, low, 0.0)
        lower = strip[pl.ds(N, HALF)] + jnp.where(lane < N * has_d, top, 0.0)
        return jnp.concatenate([upper, lower], axis=0)

    def update(it, old, new):
        from_l, from_r = strip_sum(f_l.at[it]), strip_sum(f_r.at[it])
        weight = l_sum[it] + REGULAR
        for c in range(2):
            from_up = jnp.where(lane < N * has_u, g_dn[it, c], 0.0)
            from_down = jnp.where(lane < N * has_d, g_up[it, c], 0.0)
            total = g_t[it, c, pl.ds(HALF, N), :] + jnp.concatenate([from_up, from_down], axis=0)
            left = from_l if c == 0 else pltpu.roll(from_l, HALF, 1)
            right = from_r if c == 0 else pltpu.roll(from_r, HALF, 1)
            total += jnp.where(lane_n < HALF * has_l, left, 0.0)
            total += jnp.where(lane_n >= N - HALF * has_r, right, 0.0)
            new[c] = old[c] - OBJECT_STEP * total / weight

    def drain():
        for copy in offset_copies():
            copy.wait_send()
        for it in range(ITERS):
            for copy in fetch_copies(it, tiles[it]) + grad_copies(it):
                copy.wait_send()
            pair(0, it, m_buf.at[it], m_pre.at[it]).wait_send()
            n_pair(it).wait_send()
            await_bytes(m_rcv.at[it], all_send.at[0, it])
            await_bytes(mz_rcv.at[it], all_send.at[1, it])
            await_bytes(n_rcv.at[it], all_send.at[2, it])
            await_bytes(nz_rcv.at[it], all_send.at[3, it])
            if it + 1 < ITERS:
                await_bytes(p_buf.at[it, 0], pair_send.at[2, it])
                await_bytes(p_buf.at[it, 0, pl.ds(0, blocks - 1)], all_send.at[4, it])

    barrier = pltpu.get_barrier_semaphore()
    greeted = [side_dev(step) for step in SIDES[:4]] + peer_dev + z_devs
    greeted += [side_dev(step) for step in SIDES[4:]]
    for dev in greeted:
        pl.semaphore_signal(barrier, inc=1, device_id=dev, device_id_type=MESH)
    loads = [pltpu.make_async_copy(src, dst, load_sem.at[i]) for i, (src, dst) in enumerate(
        [(tile_hbm, tile_in), (offs_hbm, offs), (probe_hbm, probe_in), (tables_hbm, tables),
         (inten_hbm, inten)])]
    for load in loads:
        load.start()
    loads[0].wait()
    pack(0, tile_in)
    loads[1].wait()
    pl.semaphore_wait(barrier, len(greeted))

    for copy in fetch_copies(0, tile_in) + offset_copies():
        copy.start()
    for channel in range(2):
        for half in range(2):
            for j in range(positions):
                pads[channel, half, j, pl.ds(0, N), :] = jnp.zeros((N, N), F32)
                pads[channel, half, j, pl.ds(2 * N, N), :] = jnp.zeros((N, N), F32)
    bright_pad[...] = jnp.zeros_like(bright_pad)
    for load in loads[2:]:
        load.wait()

    tiles = [tile_in, tile1, obj_out]
    for it in range(ITERS):
        for copy in fetch_copies(it, tiles[it]):
            copy.wait_recv()
        assemble(it, tiles[it])
        extract(it)
        if it > 0:
            wait_p(it - 1)
        waves(it)
        send_m(it)
        gradient(it)
        if it + 1 < ITERS:
            for copy in grad_copies(it):
                copy.start()
        send_n(it)
        if it == 0:
            for copy in offset_copies():
                copy.wait_recv()
        light(it)
        send_mz(it)
        send_nz(it)
        if it + 1 == ITERS:
            for copy in grad_copies(it):
                copy.start()
        if it + 1 == ITERS:
            send_p(it)
        for copy in grad_copies(it):
            copy.wait_recv()
        update(it, tiles[it], tiles[it + 1])
        if it + 1 < ITERS:
            pack(it + 1, tiles[it + 1])
            for copy in fetch_copies(it + 1, tiles[it + 1]):
                copy.start()
            send_p(it)
        if it + 1 == ITERS:
            drain()
        forward_p(it)
    wait_p(ITERS - 1)
    for k in range(modes):
        for c in range(2):
            prb_out[k, c] = probe_part(ITERS, k, c)

    await_bytes(p_buf.at[ITERS - 1, 0], pair_send.at[2, ITERS - 1])
    await_bytes(p_buf.at[ITERS - 1, 0, pl.ds(0, blocks - 1)], all_send.at[4, ITERS - 1])


def deliver(obj_in, prb_in, obj_out, prb_out, sem):
    copies = [pltpu.make_async_copy(obj_in, obj_out, sem.at[0]),
              pltpu.make_async_copy(prb_in, prb_out, sem.at[1])]
    for copy in copies:
        copy.start()
    for copy in copies:
        copy.wait()


def per_device(n_sy, n_sx, object_tile, probe_modes, scan_offsets, intensities):
    positions = scan_offsets.shape[2]
    modes = probe_modes.shape[0]
    depth = n_sx // Y_LO
    blocks = n_sy // 2 * Y_LO
    rows = N // blocks
    offsets = scan_offsets.transpose(0, 1, 3, 2)
    measured = intensities[0, 0]
    tables = jnp.asarray(dft_tables())
    vmem = functools.partial(pltpu.VMEM, dtype=F32)
    it = ITERS
    scratch = [
        vmem(object_tile.shape), vmem(probe_modes.shape), vmem(measured.shape),
        pltpu.VMEM(tables.shape, BF16), pltpu.SMEM(offsets.shape, jnp.int32),
        pltpu.SMEM((len(SIDES),) + offsets.shape, jnp.int32),
        vmem((2, N, N)), vmem((it, 2, 2 * N, N)), vmem((it, 2, 2 * N, N)),
        vmem((it, N, N)), vmem((it, N, N)), vmem((it, 2 * N, N)), vmem((it, 2 * N, N)),
        vmem((positions, 2, N, N)), vmem((positions, modes, 2, N, N)),
        vmem((2, 2, positions, 3 * N, N)), vmem((4 * N, N)),
        vmem((it, 2, 2 * N, N)), vmem((2, 2 * N, N)),
        vmem((it, 2 * N, N)), vmem((it, 2 * N, N)), vmem((it, 2, HALF, N)), vmem((it, 2, HALF, N)),
        vmem((it, 2 * N, N)), vmem((it, 2 * N, N)), vmem((it, N, N)),
        vmem((it, 2, blocks, modes, rows, N)), vmem((it, blocks, modes, rows, N)),
        vmem((it, blocks, modes, rows, N)), vmem((it, blocks - 1, modes, rows, N)),
        vmem((it, modes, rows, N)), vmem((it, depth - 1, modes, rows, N)),
        vmem((it, blocks, rows, N)), vmem((it, blocks, rows, N)), vmem((it, blocks, rows, N)),
        vmem((it, blocks - 1, rows, N)), vmem((it, rows, N)), vmem((it, depth - 1, rows, N)),
        vmem((it, 2, blocks, modes, rows, N)),
        pltpu.SemaphoreType.DMA((3, it, len(SIDES))), pltpu.SemaphoreType.DMA((3, it, len(SIDES))),
        pltpu.SemaphoreType.DMA((3, it)), pltpu.SemaphoreType.DMA((3, it)),
        pltpu.SemaphoreType.DMA((5, it)), pltpu.SemaphoreType.DMA((4, it)),
        pltpu.SemaphoreType.DMA((it, blocks - 1)),
        pltpu.SemaphoreType.DMA((5,)),
    ]
    in_vmem = pl.BlockSpec(memory_space=pltpu.VMEM)
    results = pl.pallas_call(
        functools.partial(kernel, n_sy, n_sx, positions, modes),
        out_shape=(pltpu.VMEM(object_tile.shape, F32), pltpu.VMEM(probe_modes.shape, F32)),
        in_specs=[pl.BlockSpec(memory_space=pl.ANY)] * 5,
        out_specs=(in_vmem, in_vmem),
        scratch_shapes=scratch,
        compiler_params=pltpu.CompilerParams(collective_id=0, has_side_effects=True),
    )(offsets, object_tile, probe_modes, measured, tables)
    results = [pltpu.with_memory_space_constraint(r, pltpu.VMEM) for r in results]
    return pl.pallas_call(
        deliver,
        out_shape=(jax.ShapeDtypeStruct(object_tile.shape, F32),
                   jax.ShapeDtypeStruct(probe_modes.shape, F32)),
        in_specs=[in_vmem, in_vmem],
        out_specs=(pl.BlockSpec(memory_space=pl.ANY), pl.BlockSpec(memory_space=pl.ANY)),
        scratch_shapes=[pltpu.SemaphoreType.DMA((2,))],
    )(*results)


def solution(mesh):
    placed = (P(None, "sy", "sx"), P(), P("sy", "sx", None, None), P("sy", "sx", None, None, None))
    return jax.shard_map(
        functools.partial(per_device, mesh.shape["sy"], mesh.shape["sx"]),
        mesh=mesh,
        in_specs=placed,
        out_specs=(P(None, "sy", "sx"), P()),
        check_vma=False,
    )
```
